32 devices in a mesh: dp: 8 (over y, x, core), mp: 4 (over z).
Axes of the slice: x: 2, y: 2, z: 4, core: 2. Of those that a mesh axis runs over, the one named last changes fastest.
Arguments:
- patches: bfloat16 [8192, 768], P('dp'), may hold values from -6 to 6
- attention_gain: bfloat16 [768], replicated, may hold values from 0.5 to 1.5
- query_weight: bfloat16 [768, 768], P(None, 'mp'), may hold values from -0.0390625 to 0.0390625
- key_weight: bfloat16 [768, 768], P(None, 'mp'), may hold values from -0.3125 to 0.3125
- value_weight: bfloat16 [768, 768], P(None, 'mp'), may hold values from -0.21875 to 0.21875
- output_weight: bfloat16 [768, 768], P('mp'), may hold values from -0.875 to 0.875
- feedforward_gain: bfloat16 [768], replicated, may hold values from 0.5 to 1.5
- gate_weight: bfloat16 [768, 2048], P(None, 'mp'), may hold values from -0.21875 to 0.21875
- up_weight: bfloat16 [768, 2048], P(None, 'mp'), may hold values from -0.21875 to 0.21875
- down_weight: bfloat16 [2048, 768], P('mp'), may hold values from -0.25 to 0.25
- cotangent: bfloat16 [8192, 768], P('dp'), may hold values from -6 to 6
- grid_extent: int32 [8, 2], P('dp'), may hold values from 16 to 32, as said below
Outputs:
- layer_output: bfloat16 [8192, 768], P('dp')
- input_grad: float32 [8192, 768], P('dp')
- attention_grad: float32 [768], P('dp')
- query_grad: float32 [768, 768], P('dp', 'mp')
- key_grad: float32 [768, 768], P('dp', 'mp')
- value_grad: float32 [768, 768], P('dp', 'mp')
- output_grad: float32 [768, 768], P('mp', 'dp')
- feedforward_grad: float32 [768], P('dp')
- gate_grad: float32 [768, 2048], P('dp', 'mp')
- up_grad: float32 [768, 2048], P('dp', 'mp')
- down_grad: float32 [2048, 768], P('mp', 'dp')
The draws below stay inside these ranges and needn't reach their ends.
Inputs may be any that keep to these rules, and one draw needn't show every extreme that they name: `grid_extent`: chart 0 has all 32 rows and columns.
All inputs are finite; a program needn't handle non-finite values.
Results may differ from the reference program's by a relative error of at most 0.015.
Values may be sent and summed in bfloat16 or wider, within the bound.
A program may use at most 128 MiB of HBM per device.

```python
import jax
import jax.numpy as jnp
from jax import lax

D = 768
HEADS = 12
HEAD = 64
FF = 2048
GRID = 32
SEQ = 1024
HD = 768
CHARTS = 8
TOKENS = 8192


def draw_grid_extent(key, part):
    extent = jax.random.randint(key, (CHARTS, 2), max(GRID // 2, 1), GRID + 1)
    extent = extent.at[0].set(GRID)
    return extent.astype(jnp.int32)


def raised(array, stream_key, source, target, blocks, factor):
    owner, partner = [(jnp.arange(array.shape[dim]) // (array.shape[dim] // blocks)).reshape([-1 if axis == dim else 1 for axis in range(array.ndim)]) for dim in (source, target)]
    chosen = jax.random.permutation(stream_key, blocks)[partner]
    strong = (owner == chosen) | (owner == (partner + blocks // 2) % blocks)
    return jnp.where(strong, factor * array, array)


def block_levels(rng, shape, cuts, least, largest):
    def one(axis_at, parts):
        draws = jax.random.uniform(jax.random.fold_in(jax.random.fold_in(rng, 6), axis_at), (parts,), jnp.float32, least / len(cuts), largest / len(cuts))
        return jnp.repeat(jnp.exp(draws), shape[axis_at] // parts).reshape((-1,) + (1,) * (len(shape) - axis_at - 1))

    level = one(*cuts[0])
    for cut in cuts[1:]:
        level = level * one(*cut)
    return level


def noise(stream_key, shape, width, limit, shards=(), kind=jnp.bfloat16):
    values = jax.random.normal(stream_key, shape, jnp.float32) * width
    if len(shards) > 0:
        values = block_levels(stream_key, shape, shards, -0.22, 0.18) * values
    return jnp.clip(values, min=-limit, max=limit).astype(kind)


def heavy_noise(own_key, shape, scale, limit, shards, heavy, kind=jnp.bfloat16):
    values = scale * jax.random.normal(own_key, shape, jnp.float32)
    if shards:
        values = values * block_levels(own_key, shape, shards, -0.22, 0.18)
    return jnp.clip(raised(values, jax.random.fold_in(own_key, 3), *heavy), -limit, limit).astype(kind)


def setup_inputs(seed: int = 0) -> dict:
    splits = jax.random.split(jax.random.key(seed), 13)
    return {
        "patches": heavy_noise(splits[0], (TOKENS, D), 1.0, 6.0, ((0, 8),), (0, 1, 8, 2.0)),
        "attention_gain": jnp.clip(1.0 + 0.1 * jax.random.normal(splits[1], (D,), jnp.float32), 0.5, 1.5).astype(jnp.bfloat16),
        "query_weight": noise(splits[2], (D, HD), (D * 32) ** -0.5, 0.0390625, ((1, 4),)),
        "key_weight": noise(splits[3], (D, HD), (D // 2) ** -0.5, 0.3125, ((1, 4),)),
        "value_weight": noise(splits[4], (D, HD), D ** -0.5, 0.21875, ((1, 4),)),
        "output_weight": noise(splits[5], (HD, D), (HD // 16) ** -0.5, 0.875, ((0, 4),)),
        "feedforward_gain": jnp.clip(1.0 + 0.1 * jax.random.normal(splits[6], (D,), jnp.float32), 0.5, 1.5).astype(jnp.bfloat16),
        "gate_weight": noise(splits[7], (D, FF), D ** -0.5, 0.21875, ((1, 4),)),
        "up_weight": noise(splits[8], (D, FF), D ** -0.5, 0.21875, ((1, 4),)),
        "down_weight": noise(splits[9], (FF, D), (FF // 4) ** -0.5, 0.25, ((0, 4),)),
        "cotangent": heavy_noise(splits[10], (TOKENS, D), 1.0, 6.0, ((0, 8),), (0, 1, 8, 2.0)),
        "grid_extent": draw_grid_extent(jax.random.fold_in(splits[12], 71), 0),
    }


@jax.custom_vjp
def low(v):
    return lax.optimization_barrier(v.astype(jnp.bfloat16)).astype(jnp.float32)

@jax.custom_vjp
def low_back(v):
    return v

def low_keep(v):
    return (low(v), None)

def low_pass(kept, grad):
    return (grad,)

def back_keep(v):
    return (v, None)

def back_low(kept, grad):
    return (low(grad),)
low.defvjp(low_keep, low_pass)
low_back.defvjp(back_keep, back_low)
epsilon = 1e-06
masked_score = -1000000000.0
highest = lax.Precision.HIGHEST

def rms_scale(values, gain_vec):
    return values * lax.rsqrt(lax.optimization_barrier(jnp.mean(values * values, axis=-1, keepdims=True)) + epsilon) * gain_vec

def chart_valid(extent):
    position = jnp.arange(SEQ, dtype=jnp.int32)
    return position < extent[0] * extent[1]

def chart_forward(params, chart_rows, valid_mask):
    first_gain, query_weight, key_weight, value_weight, output_weight, second_gain, gate_weight, up_weight, down_weight = params
    normed_one = low(rms_scale(chart_rows, first_gain))

    def project(matrix):
        return low(low_back(jnp.dot(normed_one, matrix, precision=highest))).reshape(SEQ, HEADS, HEAD)
    queries = project(query_weight)
    keys_all = project(key_weight)
    values_all = project(value_weight)
    scores = low_back(jnp.einsum('qhd,khd->hqk', queries, keys_all, precision=highest))
    scores = jnp.where(valid_mask[None, None, :], scores, masked_score)
    probs = low(jax.nn.softmax(scores, axis=-1))
    context = jnp.einsum('hqk,khd->qhd', probs, values_all, precision=highest).reshape(SEQ, HEADS * HEAD)
    context = low(low_back(context))
    attention_out = low_back(jnp.dot(context, output_weight, precision=highest))
    hidden = chart_rows + attention_out
    normed_two = low(rms_scale(hidden, second_gain))
    gate_pre = low_back(jnp.dot(normed_two, gate_weight, precision=highest))
    up_pre = low_back(jnp.dot(normed_two, up_weight, precision=highest))
    mixed = low(jax.nn.gelu(gate_pre, approximate=True) * up_pre)
    feedforward_out = low_back(jnp.dot(mixed, down_weight, precision=highest))
    return jnp.where(valid_mask[:, None], hidden + feedforward_out, 0.0)

def reference(patches, attention_gain, query_weight, key_weight, value_weight, output_weight, feedforward_gain, gate_weight, up_weight, down_weight, cotangent, grid_extent):
    params = tuple((weight.astype(jnp.float32) for weight in (attention_gain, query_weight, key_weight, value_weight, output_weight, feedforward_gain, gate_weight, up_weight, down_weight)))
    inputs = patches.astype(jnp.float32).reshape(CHARTS, SEQ, D)
    upstream = cotangent.astype(jnp.float32).reshape(CHARTS, SEQ, D)

    def chart_step(totals, chart_item):
        chart_rows, chart_upstream, extent = chart_item
        valid_mask = chart_valid(extent)
        output, pullback = jax.vjp(lambda prm, rows: chart_forward(prm, rows, valid_mask), params, chart_rows)
        param_grads, rows_grad = pullback(chart_upstream)
        totals = jax.tree.map(lambda left, right: left + right, totals, param_grads)
        return (totals, (output.astype(jnp.bfloat16), rows_grad))
    zeros_tree = jax.tree.map(jnp.zeros_like, params)
    grads, (outputs, rows_grads) = lax.scan(chart_step, zeros_tree, (inputs, upstream, grid_extent))
    return (outputs.reshape(TOKENS, D), rows_grads.reshape(TOKENS, D), grads[0], grads[1], grads[2], grads[3], grads[4], grads[5], grads[6], grads[7], grads[8])
```

```python
import functools

import jax
import jax.numpy as jnp
from jax import lax
from jax.experimental import pallas as pl
from jax.experimental.pallas import tpu as pltpu
from jax.sharding import PartitionSpec as P

HEAD = 64
EPSILON = 1e-06
MASKED = -1000000000.0
MESH = pl.DeviceIdType.MESH
f32 = jnp.float32
bf16 = jnp.bfloat16
GROUP = 8
VMEM_LIMIT = 61 << 20


def dot(left, right, left_dim, right_dim):
    return lax.dot_general(
        left, right, (((left_dim,), (right_dim,)), ((), ())), preferred_element_type=f32
    )


def flip(value, bits):
    result = value
    for bit in (1, 2, 4):
        if bits & bit:
            result = result + bit - 2 * bit * ((value // bit) % 2)
    return result


def aligned(value, multiple):
    return pl.multiple_of(value, multiple)


class Gather:
    KINDS = 5

    def __init__(self, sources, places, send_z, recv_z, send_x, recv_x, send_c, recv_c):
        self.dp, self.mp = lax.axis_index("dp"), lax.axis_index("mp")
        self.core = self.dp % 2
        self.chip = (self.dp // 2) % 4
        self.sources, self.places = sources, places
        self.sems = (send_z, recv_z, send_x, recv_x, send_c, recv_c)
        self.sends = []

    def part(self, ref, lead, quarter, half):
        rows, columns = ref.shape[-2] // 4, ref.shape[-1] // 2
        window = (
            pl.ds(aligned(quarter * rows, 16), rows),
            pl.ds(aligned(half * columns, 128), columns),
        )
        middle = (slice(None),) * (len(ref.shape) - 2 - len(lead))
        return ref.at[(*lead, *middle, *window)]

    def place(self, kind, shard, quarter, half):
        return self.part(self.places[kind], (shard,), quarter, half)

    def copy(self, source, target, send, recv, dp, mp):
        return pltpu.make_async_remote_copy(
            src_ref=source,
            dst_ref=target,
            send_sem=send,
            recv_sem=recv,
            device_id=(dp, mp),
            device_id_type=MESH,
        )

    def start(self, *operands):
        copy = self.copy(*operands)
        copy.start()
        self.sends.append(copy)

    def arrived(self, target, send, recv):
        self.copy(target, target, send, recv, self.dp, self.mp).wait_recv()

    def along_mp(self, kind, k):
        send_z, recv_z = self.sems[:2]
        self.start(
            self.part(self.sources[kind], (), self.chip, self.core),
            self.place(kind, self.mp, self.chip, self.core),
            send_z.at[kind, k],
            recv_z.at[kind, k],
            self.dp,
            flip(self.mp, k),
        )

    def to_core(self, kind, k, j):
        piece = self.place(kind, flip(self.mp, k), flip(self.chip, j), self.core)
        send_c, recv_c = self.sems[4:]
        self.start(
            piece, piece, send_c.at[kind, k, j], recv_c.at[kind, k, j], flip(self.dp, 1), self.mp
        )

    def to_chips(self, kind, k):
        send_z, recv_z, send_x, recv_x = self.sems[:4]
        piece = self.place(kind, flip(self.mp, k), self.chip, self.core)
        self.arrived(piece, send_z.at[kind, k], recv_z.at[kind, k])
        for j in (1, 2):
            self.start(
                piece,
                piece,
                send_x.at[kind, k, j],
                recv_x.at[kind, k, j],
                flip(self.dp, 2 * j),
                self.mp,
            )
        self.to_core(kind, k, 0)

    def to_corner(self, kind, k):
        send_x, recv_x = self.sems[2:4]
        shard = flip(self.mp, k)
        for j in (1, 2):
            piece = self.place(kind, shard, flip(self.chip, j), self.core)
            self.arrived(piece, send_x.at[kind, k, j], recv_x.at[kind, k, j])
        from_y, from_x = flip(self.chip, 2), flip(self.chip, 1)
        to_x, to_y = flip(self.dp, 2), flip(self.dp, 4)
        piece = self.place(kind, shard, from_y + self.core * (from_x - from_y), self.core)
        self.start(
            piece,
            piece,
            send_x.at[kind, k, 3],
            recv_x.at[kind, k, 3],
            to_x + self.core * (to_y - to_x),
            self.mp,
        )
        self.to_core(kind, k, 1)
        self.to_core(kind, k, 2)

    def last_core(self, kind, k):
        send_x, recv_x = self.sems[2:4]
        piece = self.place(kind, flip(self.mp, k), flip(self.chip, 3), self.core)
        self.arrived(piece, send_x.at[kind, k, 3], recv_x.at[kind, k, 3])
        self.to_core(kind, k, 3)

    def settled(self, kind, k):
        send_c, recv_c = self.sems[4:]
        for j in range(4):
            piece = self.place(kind, flip(self.mp, k), flip(self.chip, j), 1 - self.core)
            self.arrived(piece, send_c.at[kind, k, j], recv_c.at[kind, k, j])

    def schedule(self, jobs):
        stages = (self.to_chips, self.to_corner, self.last_core, self.settled)
        steps = []
        for tick in range(len(jobs) + len(stages) - 1):
            for depth in reversed(range(len(stages))):
                if 0 <= tick - depth < len(jobs):
                    job = jobs[tick - depth]
                    steps.append((functools.partial(stages[depth], *job), job, depth == 3))
        return steps

    def finish(self):
        for copy in self.sends:
            copy.wait_send()


def barrier(devices):
    semaphore = pltpu.get_barrier_semaphore()
    for device in devices:
        pl.semaphore_signal(semaphore, inc=1, device_id=device, device_id_type=MESH)
    pl.semaphore_wait(semaphore, len(devices))


def row_keep(count, first, rows):
    return lax.broadcasted_iota(jnp.int32, (rows, 1), 0) + first < count


def project(weights_ref, normed_ref, out_ref, shard):
    parts, features, depth = weights_ref.shape[1:]
    rows = normed_ref.shape[0]
    block = 256

    def step(i, _):
        at = pl.ds(aligned(i * block, block), block)
        weights = weights_ref[shard].reshape(parts * features, depth)
        out_ref[shard, :, at] = dot(weights, normed_ref[at, :], 1, 1).astype(bf16)
        return 0

    lax.fori_loop(0, rows // block, step, 0)


def attend(qkv_ref, shard, head, count, probs_ref, context_ref, scale_ref, local_heads):
    rows = qkv_ref.shape[2]
    width = local_heads * HEAD
    block = 256
    at = aligned(head * HEAD, HEAD)
    keys = qkv_ref[shard, pl.ds(aligned(width + head * HEAD, HEAD), HEAD), :].T
    values = qkv_ref[shard, pl.ds(aligned(2 * width + head * HEAD, HEAD), HEAD), :]
    bias = jnp.where(row_keep(count, 0, rows), 0.0, MASKED).astype(f32)
    number = shard * local_heads + head
    for first in range(0, rows, block):
        queries = qkv_ref[shard, pl.ds(at, HEAD), first : first + block]
        scores = dot(keys, queries, 1, 0) + bias
        highest = jnp.max(scores, axis=0, keepdims=True)
        weights = jnp.exp(scores - highest)
        scale = 1.0 / jnp.sum(weights, axis=0, keepdims=True)
        low = weights.astype(bf16)
        probs_ref[:, first : first + block] = low
        context = dot(values, low, 1, 0) * scale
        context_ref[pl.ds(aligned(shard * width + head * HEAD, HEAD), HEAD), first : first + block] = (
            context.astype(bf16)
        )
        scale_ref[number, :, first : first + block] = scale


def gelu_parts(gate):
    root = 0.7978845608028654
    square = gate * gate
    bend = jnp.tanh(gate * (root + (root * 0.044715) * square))
    half = 0.5 + 0.5 * bend
    slope = half + (0.5 * gate) * (1.0 - bend * bend) * (root + (3 * root * 0.044715) * square)
    return gate * half, slope


def forward_kernel(
    extent,
    inputs,
    upstream,
    first_gain,
    second_gain,
    attention_source,
    output_source,
    gate_source,
    up_source,
    down_source,
    layer_output,
    qkv,
    probs_out,
    context_back,
    delta,
    hidden,
    weights_out,
    normed_one,
    wide_grad,
    gain_grad,
    attention_weights,
    output_weights,
    gate_weights,
    up_weights,
    down_weights,
    context,
    probs,
    scale,
    normed_two,
    out_low,
    forward_sum,
    back_sum,
    mixed_own,
    gate_own,
    up_own,
    local_sem,
    probs_sem,
    weights_sem,
    send_z,
    recv_z,
    send_x,
    recv_x,
    send_c,
    recv_c,
):
    dp, mp = lax.axis_index("dp"), lax.axis_index("mp")
    shards = attention_weights.shape[0]
    rows, depth = inputs.shape
    local_heads = attention_weights.shape[2] // HEAD
    count = extent[0, 0] * extent[0, 1]
    block = 256
    blocks = rows // block

    sources = (attention_source, output_source, gate_source, up_source, down_source)
    places = (attention_weights, output_weights, gate_weights, up_weights, down_weights)
    locals_ = [
        pltpu.make_async_copy(source, place.at[mp], local_sem.at[i])
        for i, (source, place) in enumerate(zip(sources, places))
    ]
    for copy in locals_:
        copy.start()
    barrier(
        [(flip(dp, j), mp) for j in (1, 2, 4)] + [(dp, flip(mp, k)) for k in range(1, shards)]
    )
    gather = Gather(sources, places, send_z, recv_z, send_x, recv_x, send_c, recv_c)
    jobs = [(kind, k) for kind in (0, 1) for k in range(1, shards)]
    jobs += [(kind, k) for k in range(1, shards) for kind in (2, 3, 4)]
    for job in jobs:
        gather.along_mp(*job)
    steps = gather.schedule(jobs)
    position = [0]

    def advance(amount):
        for step, _, _ in steps[position[0] : position[0] + amount]:
            step()
        position[0] = min(position[0] + amount, len(steps))

    def until(job):
        where = [i for i, (_, name, last) in enumerate(steps) if last and name == job][0]
        advance(max(0, where + 1 - position[0]))

    def normalise(i, _):
        at = pl.ds(aligned(i * block, block), block)
        values = inputs[at, :].astype(f32)
        root = lax.rsqrt(jnp.mean(values * values, axis=-1, keepdims=True) + EPSILON)
        normed_one[at, :] = (values * root * first_gain[...]).astype(bf16)
        low = jnp.where(row_keep(count, i * block, block), upstream[at, :].astype(f32), 0.0)
        out_low[at, :] = low.astype(bf16)
        return 0

    lax.fori_loop(0, blocks, normalise, 0)

    def probs_copy(slot, number):
        return pltpu.make_async_copy(probs.at[slot], probs_out.at[number], probs_sem.at[slot])

    done = 0
    for k in range(shards):
        shard = flip(mp, k)
        if k == 0:
            locals_[0].wait()
        else:
            until((0, k))
        project(attention_weights, normed_one, qkv, shard)
        for head in range(local_heads):
            slot = done % 2
            number = shard * local_heads + head
            if done >= 2:
                probs_copy(slot, number).wait()
            attend(qkv, shard, head, count, probs.at[slot], context, scale, local_heads)
            probs_copy(slot, number).start()
            done += 1
            advance(2)
    weights_copy = pltpu.make_async_copy(attention_weights, weights_out, weights_sem)
    weights_copy.start()

    locals_[1].wait()
    for k in range(1, shards):
        until((1, k))
    every_output = output_weights[...].reshape(depth, depth)

    def join(i, _):
        at = pl.ds(aligned(i * block, block), block)
        values = inputs[at, :].astype(f32) + dot(context[:, at], every_output, 0, 0)
        hidden[at, :] = values
        root = lax.rsqrt(jnp.mean(values * values, axis=-1, keepdims=True) + EPSILON)
        normed_two[at, :] = (values * root * second_gain[...]).astype(bf16)
        return 0

    lax.fori_loop(0, blocks, join, 0)

    def feed(shard, k):
        def step(i, _):
            at = pl.ds(aligned(i * block, block), block)
            normed, low = normed_two[at, :], out_low[at, :]
            gate = dot(normed, gate_weights[shard], 1, 0)
            up = dot(normed, up_weights[shard], 1, 0)
            mixed_back = dot(low, down_weights[shard], 1, 1)
            bent, slope = gelu_parts(gate)
            mixed = (bent * up).astype(bf16)
            gate_back = (mixed_back * up * slope).astype(bf16)
            up_back = (mixed_back * bent).astype(bf16)
            ahead = dot(mixed, down_weights[shard], 1, 0)
            back = dot(gate_back, gate_weights[shard], 1, 1) + dot(up_back, up_weights[shard], 1, 1)
            if k == 0:
                mixed_own[at, :] = mixed
                gate_own[at, :] = gate_back
                up_own[at, :] = up_back
                forward_sum[at, :] = ahead
                back_sum[at, :] = back
            else:
                forward_sum[at, :] += ahead
                back_sum[at, :] += back
            return 0

        lax.fori_loop(0, blocks, step, 0)

    slices = wide_grad.shape[:3]
    width = gate_weights.shape[2]
    for k in range(shards):
        if k == 0:
            for copy in locals_[2:]:
                copy.wait()
        else:
            for kind in (2, 3, 4):
                until((kind, k))
        feed(flip(mp, k), k)
        advance(4)
        if k == 0:
            pairs = ((normed_two, gate_own), (normed_two, up_own), (out_low, mixed_own))
            for i, (left, right) in enumerate(pairs):
                part = dot(left[...], right[...], 0, 0).astype(bf16)
                wide_grad[:, :, :, i * width : (i + 1) * width] = part.reshape(*slices, width)
                advance(2)
    advance(len(steps))

    gain_grad[...] = jnp.zeros_like(gain_grad)

    def close(i, _):
        at = pl.ds(aligned(i * block, block), block)
        keep = row_keep(count, i * block, block)
        values, back = hidden[at, :], back_sum[at, :]
        layer_output[at, :] = jnp.where(keep, values + forward_sum[at, :], 0.0).astype(bf16)
        root = lax.rsqrt(jnp.mean(values * values, axis=-1, keepdims=True) + EPSILON)
        scaled = back * values
        gain_grad[0:1, :] += jnp.sum(scaled * root, axis=0, keepdims=True)
        mean = jnp.mean(scaled * second_gain[...], axis=-1, keepdims=True)
        out_back = jnp.where(keep, upstream[at, :].astype(f32), 0.0)
        result = out_back + root * (second_gain[...] * back) - values * (root * root * root * mean)
        hidden[at, :] = result
        normed_two[at, :] = result.astype(bf16)
        return 0

    lax.fori_loop(0, blocks, close, 0)
    hidden_low = normed_two

    features = output_weights.shape[1]
    own = context[pl.ds(aligned(mp * features, 64), features), :]
    part = dot(own, hidden_low[...], 1, 0).T.astype(bf16)
    wide_grad[:, :, :, 3 * width : 3 * width + features] = part.reshape(*slices, features)

    def context_step(head, _):
        at = pl.ds(aligned(head * HEAD, HEAD), HEAD)
        shard, local = head // local_heads, head % local_heads
        weights = output_weights[shard, pl.ds(aligned(local * HEAD, HEAD), HEAD), :]
        back = dot(weights, hidden_low[...], 1, 1) * scale[head]
        low = back.astype(bf16)
        context_back[at, :] = low
        delta[head] = jnp.sum(low.astype(f32) * context[at, :].astype(f32), axis=0, keepdims=True)
        return 0

    lax.fori_loop(0, shards * local_heads, context_step, 0)

    for slot, number in ((done % 2, 0), ((done + 1) % 2, 0)):
        probs_copy(slot, number).wait()
    weights_copy.wait()
    gather.finish()


def attend_back(qkv_ref, grad_ref, shard, head, probs, context_back, delta, score_back, local_heads):
    rows = qkv_ref.shape[2]
    width = local_heads * HEAD
    block = 256
    head_at = pl.ds(aligned(head * HEAD, HEAD), HEAD)
    key_at = pl.ds(aligned(width + head * HEAD, HEAD), HEAD)
    value_at = pl.ds(aligned(2 * width + head * HEAD, HEAD), HEAD)
    number = shard * local_heads + head
    upstream_at = pl.ds(aligned(number * HEAD, HEAD), HEAD)
    values = qkv_ref[shard, value_at, :].T
    keys = qkv_ref[shard, key_at, :]
    for first in range(0, rows, block):
        columns = slice(first, first + block)
        probs_back = dot(values, context_back[upstream_at, columns], 1, 0)
        part = probs[:, columns].astype(f32) * (probs_back - delta[number, :, columns])
        low = part.astype(bf16)
        score_back[:, columns] = low
        grad_ref[shard, head_at, columns] = dot(keys, low, 1, 0).astype(bf16)
    grad_ref[shard, value_at, :] = dot(context_back[upstream_at, :], probs[...], 1, 1).astype(bf16)
    grad_ref[shard, key_at, :] = dot(qkv_ref[shard, head_at, :], score_back[...], 1, 1).astype(bf16)


class Reduce:
    def __init__(self, local, from_core, staged, from_chips, total, sems):
        self.local, self.from_core, self.staged = local, from_core, staged
        self.from_chips, self.total, self.sems = from_chips, total, sems
        self.dp, self.mp = lax.axis_index("dp"), lax.axis_index("mp")
        self.core, self.chip = self.dp % 2, (self.dp // 2) % 4
        self.copies = []

    def begin(self):
        copy = pltpu.make_async_remote_copy(
            src_ref=self.local.at[:, 1 - self.core],
            dst_ref=self.from_core,
            send_sem=self.sems.at[0, 0],
            recv_sem=self.sems.at[1, 0],
            device_id=(flip(self.dp, 1), self.mp),
            device_id_type=MESH,
        )
        copy.start()
        self.first = copy

    def middle(self):
        self.first.wait()
        for j in (1, 2, 3, 0):
            chip = flip(self.chip, j)
            part = self.local[chip, self.core].astype(f32) + self.from_core[chip].astype(f32)
            if j == 0:
                self.total[...] = part
                continue
            self.staged[j - 1] = part.astype(bf16)
            copy = pltpu.make_async_remote_copy(
                src_ref=self.staged.at[j - 1],
                dst_ref=self.from_chips.at[j - 1],
                send_sem=self.sems.at[0, j],
                recv_sem=self.sems.at[1, j],
                device_id=(flip(self.dp, 2 * j), self.mp),
                device_id_type=MESH,
            )
            copy.start()
            self.copies.append(copy)

    def end(self):
        for copy in self.copies:
            copy.wait()
        self.total[...] += (
            self.from_chips[0].astype(f32)
            + self.from_chips[1].astype(f32)
            + self.from_chips[2].astype(f32)
        )


def backward_kernel(
    inputs,
    first_gain,
    qkv,
    probs_in,
    context_back,
    delta,
    hidden_back,
    weights,
    normed_one,
    wide_grad,
    gain_grad,
    input_grad,
    wide_total,
    narrow_total,
    gains_total,
    grads,
    probs,
    score_back,
    narrow_grad,
    wide_core,
    wide_staged,
    wide_chips,
    narrow_core,
    narrow_staged,
    narrow_chips,
    gains_own,
    gains_in,
    probs_sem,
    wide_sem,
    narrow_sem,
    gains_send,
    gains_recv,
):
    dp, mp = lax.axis_index("dp"), lax.axis_index("mp")
    shards = qkv.shape[0]
    local_heads = qkv.shape[1] // (3 * HEAD)
    rows, depth = inputs.shape
    block = 256
    blocks = rows // block

    heads = [(k, head) for k in range(shards) for head in range(local_heads)]

    def fetch(i):
        k, head = heads[i]
        number = flip(mp, k) * local_heads + head
        return pltpu.make_async_copy(probs_in.at[number], probs.at[i % 2], probs_sem.at[i % 2])

    fetch(0).start()
    barrier([(flip(dp, j), mp) for j in range(1, GROUP)])
    wide = Reduce(wide_grad, wide_core, wide_staged, wide_chips, wide_total, wide_sem)
    narrow = Reduce(narrow_grad, narrow_core, narrow_staged, narrow_chips, narrow_total, narrow_sem)
    wide.begin()
    for i, (k, head) in enumerate(heads):
        fetch(i).wait()
        if i + 1 < len(heads):
            fetch(i + 1).start()
        shard = flip(mp, k)
        attend_back(
            qkv, grads, shard, head, probs.at[i % 2], context_back, delta, score_back, local_heads
        )
        if i == 0:
            wide.middle()
        if i == local_heads - 1:
            part = dot(grads[mp], normed_one[...], 1, 0).T.astype(bf16)
            narrow_grad[...] = part.reshape(narrow_grad.shape)
            narrow.begin()
        if i == local_heads:
            narrow.middle()
        if i == len(heads) - 1:
            wide.end()
            narrow.end()

    gains_own[0:1, :] = gain_grad[0:1, :]
    gains_own[1:, :] = jnp.zeros((gains_own.shape[0] - 1, depth), f32)
    every_weight = weights[...].reshape(-1, depth)

    def close(i, _):
        at = pl.ds(aligned(i * block, block), block)
        values = inputs[at, :].astype(f32)
        back = dot(grads[:, :, at].reshape(-1, block), every_weight, 0, 0)
        root = lax.rsqrt(jnp.mean(values * values, axis=-1, keepdims=True) + EPSILON)
        scaled = back * values
        gains_own[1:2, :] += jnp.sum(scaled * root, axis=0, keepdims=True)
        mean = jnp.mean(scaled * first_gain[...], axis=-1, keepdims=True)
        input_grad[at, :] = (
            hidden_back[at, :]
            + root * (first_gain[...] * back)
            - values * (root * root * root * mean)
        )
        return 0

    lax.fori_loop(0, blocks, close, 0)
    copies = []
    for j in range(1, GROUP):
        copy = pltpu.make_async_remote_copy(
            src_ref=gains_own,
            dst_ref=gains_in.at[j - 1],
            send_sem=gains_send.at[j - 1],
            recv_sem=gains_recv.at[j - 1],
            device_id=(flip(dp, j), mp),
            device_id_type=MESH,
        )
        copy.start()
        copies.append(copy)
    for copy in copies:
        copy.wait()
    total = gains_own[...]
    for j in range(GROUP - 1):
        total = total + gains_in[j]
    gains_total[...] = total


def vmem():
    return pl.BlockSpec(memory_space=pltpu.VMEM)


def anywhere():
    return pl.BlockSpec(memory_space=pl.ANY)


def body(groups, shards, *arguments):
    (
        patches,
        attention_gain,
        query_weight,
        key_weight,
        value_weight,
        output_weight,
        feedforward_gain,
        gate_weight,
        up_weight,
        down_weight,
        cotangent,
        grid_extent,
    ) = arguments
    rows, depth = patches.shape
    features, units = query_weight.shape[1], gate_weight.shape[1]
    heads = shards * features // HEAD
    piece = depth // GROUP
    wide, narrow = 3 * units + features, 3 * features
    first_gain = attention_gain.astype(f32).reshape(1, depth)
    second_gain = feedforward_gain.astype(f32).reshape(1, depth)
    attention_source = jnp.stack([query_weight.T, key_weight.T, value_weight.T])

    shape = jax.ShapeDtypeStruct
    kinds = Gather.KINDS
    dma = pltpu.SemaphoreType.DMA
    (
        layer_output,
        qkv,
        probs,
        context_back,
        delta,
        hidden_back,
        weights,
        normed_one,
        wide_grad,
        gain_grad,
    ) = pl.pallas_call(
        forward_kernel,
        name="gather_forward",
        out_shape=(
            shape((rows, depth), bf16),
            shape((shards, narrow, rows), bf16),
            shape((heads, rows, rows), bf16),
            shape((depth, rows), bf16),
            shape((heads, 1, rows), f32),
            shape((rows, depth), f32),
            shape((shards, 3, features, depth), bf16),
            shape((rows, depth), bf16),
            shape((4, 2, piece, wide), bf16),
            shape((8, depth), f32),
        ),
        in_specs=[pl.BlockSpec(memory_space=pltpu.SMEM)] + [vmem()] * 4 + [anywhere()] * 5,
        out_specs=(
            vmem(),
            vmem(),
            anywhere(),
            vmem(),
            vmem(),
            vmem(),
            anywhere(),
            vmem(),
            vmem(),
            vmem(),
        ),
        scratch_shapes=[
            pltpu.VMEM((shards, 3, features, depth), bf16),
            pltpu.VMEM((shards, features, depth), bf16),
            pltpu.VMEM((shards, depth, units), bf16),
            pltpu.VMEM((shards, depth, units), bf16),
            pltpu.VMEM((shards, units, depth), bf16),
            pltpu.VMEM((depth, rows), bf16),
            pltpu.VMEM((2, rows, rows), bf16),
            pltpu.VMEM((heads, 1, rows), f32),
            pltpu.VMEM((rows, depth), bf16),
            pltpu.VMEM((rows, depth), bf16),
            pltpu.VMEM((rows, depth), f32),
            pltpu.VMEM((rows, depth), f32),
            pltpu.VMEM((rows, units), bf16),
            pltpu.VMEM((rows, units), bf16),
            pltpu.VMEM((rows, units), bf16),
            dma((kinds,)),
            dma((2,)),
            dma,
            dma((kinds, shards)),
            dma((kinds, shards)),
            dma((kinds, shards, 4)),
            dma((kinds, shards, 4)),
            dma((kinds, shards, 4)),
            dma((kinds, shards, 4)),
        ],
        compiler_params=pltpu.CompilerParams(
            collective_id=0, has_side_effects=True, vmem_limit_bytes=VMEM_LIMIT
        ),
    )(
        grid_extent,
        patches,
        cotangent,
        first_gain,
        second_gain,
        attention_source,
        output_weight,
        gate_weight,
        up_weight,
        down_weight,
    )

    input_grad, wide_total, narrow_total, gains_total = pl.pallas_call(
        backward_kernel,
        name="attention_backward",
        out_shape=(
            shape((rows, depth), f32),
            shape((piece, wide), f32),
            shape((piece, narrow), f32),
            shape((8, depth), f32),
        ),
        in_specs=[vmem()] * 3 + [anywhere()] + [vmem()] * 7,
        out_specs=(vmem(),) * 4,
        scratch_shapes=[
            pltpu.VMEM((shards, narrow, rows), bf16),
            pltpu.VMEM((2, rows, rows), bf16),
            pltpu.VMEM((rows, rows), bf16),
            pltpu.VMEM((4, 2, piece, narrow), bf16),
            pltpu.VMEM((4, piece, wide), bf16),
            pltpu.VMEM((3, piece, wide), bf16),
            pltpu.VMEM((3, piece, wide), bf16),
            pltpu.VMEM((4, piece, narrow), bf16),
            pltpu.VMEM((3, piece, narrow), bf16),
            pltpu.VMEM((3, piece, narrow), bf16),
            pltpu.VMEM((8, depth), f32),
            pltpu.VMEM((GROUP - 1, 8, depth), f32),
            dma((2,)),
            dma((2, 4)),
            dma((2, 4)),
            dma((GROUP - 1,)),
            dma((GROUP - 1,)),
        ],
        compiler_params=pltpu.CompilerParams(
            collective_id=1, has_side_effects=True, vmem_limit_bytes=VMEM_LIMIT
        ),
    )(
        patches,
        first_gain,
        qkv,
        probs,
        context_back,
        delta,
        hidden_back,
        weights,
        normed_one,
        wide_grad,
        gain_grad,
    )

    index = lax.axis_index("dp")
    if groups > 1:

        def spread(block):
            whole = jnp.zeros((depth, block.shape[1]), f32)
            whole = lax.dynamic_update_slice(whole, block, ((index % GROUP) * piece, 0))
            return lax.psum_scatter(whole, "dp", scatter_dimension=0, tiled=True)

        wide_total, narrow_total = spread(wide_total), spread(narrow_total)
        gains_total = lax.psum(gains_total, "dp") / GROUP
    kept = depth // (groups * GROUP)
    gains = lax.dynamic_slice_in_dim(gains_total[:2], index * kept, kept, 1)
    return (
        layer_output,
        input_grad,
        gains[1],
        narrow_total[:, :features],
        narrow_total[:, features : 2 * features],
        narrow_total[:, 2 * features :],
        wide_total[:, 3 * units :].T,
        gains[0],
        wide_total[:, :units],
        wide_total[:, units : 2 * units],
        wide_total[:, 2 * units : 3 * units].T,
    )


def solution(mesh):
    placed = (
        P("dp", None),
        P(),
        P(None, "mp"),
        P(None, "mp"),
        P(None, "mp"),
        P("mp", None),
        P(),
        P(None, "mp"),
        P(None, "mp"),
        P("mp", None),
        P("dp", None),
        P("dp", None),
    )
    return jax.shard_map(
        functools.partial(body, mesh.shape["dp"] // GROUP, mesh.shape["mp"]),
        mesh=mesh,
        in_specs=placed,
        out_specs=(
            P("dp", None),
            P("dp", None),
            P("dp"),
            P("dp", "mp"),
            P("dp", "mp"),
            P("dp", "mp"),
            P("mp", "dp"),
            P("dp"),
            P("dp", "mp"),
            P("dp", "mp"),
            P("mp", "dp"),
        ),
        check_vma=False,
    )
```

```python
import functools

import jax
import jax.numpy as jnp
from jax import lax
from jax.experimental import pallas as pl
from jax.experimental.pallas import tpu as pltpu
from jax.sharding import PartitionSpec as P

HEAD = 64
EPSILON = 1e-06
MASKED = -1000000000.0
MESH = pl.DeviceIdType.MESH
f32 = jnp.float32
bf16 = jnp.bfloat16
GROUP = 8
VMEM_LIMIT = 61 << 20


def dot(left, right, left_dim, right_dim):
    return lax.dot_general(
        left, right, (((left_dim,), (right_dim,)), ((), ())), preferred_element_type=f32
    )


def flip(value, bits):
    result = value
    for bit in (1, 2, 4):
        if bits & bit:
            result = result + bit - 2 * bit * ((value // bit) % 2)
    return result


def aligned(value, multiple):
    return pl.multiple_of(value, multiple)


class Gather:
    KINDS = 5

    def __init__(self, sources, places, send_z, recv_z, send_x, recv_x, send_c, recv_c):
        self.dp, self.mp = lax.axis_index("dp"), lax.axis_index("mp")
        self.core = self.dp % 2
        self.chip = (self.dp // 2) % 4
        self.sources, self.places = sources, places
        self.sems = (send_z, recv_z, send_x, recv_x, send_c, recv_c)
        self.sends = []

    def part(self, ref, lead, quarter, half):
        rows, columns = ref.shape[-2] // 4, ref.shape[-1] // 2
        window = (
            pl.ds(aligned(quarter * rows, 16), rows),
            pl.ds(aligned(half * columns, 128), columns),
        )
        middle = (slice(None),) * (len(ref.shape) - 2 - len(lead))
        return ref.at[(*lead, *middle, *window)]

    def place(self, kind, shard, quarter, half):
        return self.part(self.places[kind], (shard,), quarter, half)

    def copy(self, source, target, send, recv, dp, mp):
        return pltpu.make_async_remote_copy(
            src_ref=source,
            dst_ref=target,
            send_sem=send,
            recv_sem=recv,
            device_id=(dp, mp),
            device_id_type=MESH,
        )

    def start(self, *operands):
        copy = self.copy(*operands)
        copy.start()
        self.sends.append(copy)

    def arrived(self, target, send, recv):
        self.copy(target, target, send, recv, self.dp, self.mp).wait_recv()

    def along_mp(self, kind, k):
        send_z, recv_z = self.sems[:2]
        self.start(
            self.part(self.sources[kind], (), self.chip, self.core),
            self.place(kind, self.mp, self.chip, self.core),
            send_z.at[kind, k],
            recv_z.at[kind, k],
            self.dp,
            flip(self.mp, k),
        )

    def to_core(self, kind, k, j):
        piece = self.place(kind, flip(self.mp, k), flip(self.chip, j), self.core)
        send_c, recv_c = self.sems[4:]
        self.start(
            piece, piece, send_c.at[kind, k, j], recv_c.at[kind, k, j], flip(self.dp, 1), self.mp
        )

    def to_chips(self, kind, k):
        send_z, recv_z, send_x, recv_x = self.sems[:4]
        piece = self.place(kind, flip(self.mp, k), self.chip, self.core)
        self.arrived(piece, send_z.at[kind, k], recv_z.at[kind, k])
        for j in (1, 2):
            self.start(
                piece,
                piece,
                send_x.at[kind, k, j],
                recv_x.at[kind, k, j],
                flip(self.dp, 2 * j),
                self.mp,
            )
        self.to_core(kind, k, 0)

    def to_corner(self, kind, k):
        send_x, recv_x = self.sems[2:4]
        shard = flip(self.mp, k)
        for j in (1, 2):
            piece = self.place(kind, shard, flip(self.chip, j), self.core)
            self.arrived(piece, send_x.at[kind, k, j], recv_x.at[kind, k, j])
        from_y, from_x = flip(self.chip, 2), flip(self.chip, 1)
        to_x, to_y = flip(self.dp, 2), flip(self.dp, 4)
        piece = self.place(kind, shard, from_y + self.core * (from_x - from_y), self.core)
        self.start(
            piece,
            piece,
            send_x.at[kind, k, 3],
            recv_x.at[kind, k, 3],
            to_x + self.core * (to_y - to_x),
            self.mp,
        )
        self.to_core(kind, k, 1)
        self.to_core(kind, k, 2)

    def last_core(self, kind, k):
        send_x, recv_x = self.sems[2:4]
        piece = self.place(kind, flip(self.mp, k), flip(self.chip, 3), self.core)
        self.arrived(piece, send_x.at[kind, k, 3], recv_x.at[kind, k, 3])
        self.to_core(kind, k, 3)

    def settled(self, kind, k):
        send_c, recv_c = self.sems[4:]
        for j in range(4):
            piece = self.place(kind, flip(self.mp, k), flip(self.chip, j), 1 - self.core)
            self.arrived(piece, send_c.at[kind, k, j], recv_c.at[kind, k, j])

    def schedule(self, jobs, window=8, start=3.0, pace=2.6, lags=(5.0, 10.0, 12.0)):
        for job in jobs[:window]:
            self.along_mp(*job)

        def first(i):
            self.to_chips(*jobs[i])
            if i + window < len(jobs):
                self.along_mp(*jobs[i + window])

        steps = []
        clock = start
        for i, job in enumerate(jobs):
            clock += 0.37 * pace if job[0] == 1 else pace
            steps.append((clock, functools.partial(first, i), job, False))
            later = (self.to_corner, self.last_core, self.settled)
            for lag, step in zip(lags, later):
                steps.append((clock + lag, functools.partial(step, *job), job, step == later[-1]))
        return sorted(steps, key=lambda step: step[0])

    def finish(self):
        for copy in self.sends:
            copy.wait_send()


def barrier(devices):
    semaphore = pltpu.get_barrier_semaphore()
    for device in devices:
        pl.semaphore_signal(semaphore, inc=1, device_id=device, device_id_type=MESH)
    pl.semaphore_wait(semaphore, len(devices))


def row_keep(count, first, rows):
    return lax.broadcasted_iota(jnp.int32, (rows, 1), 0) + first < count


def project(weights_ref, normed_ref, out_ref, shard):
    parts, features, depth = weights_ref.shape[1:]
    rows = normed_ref.shape[0]
    block = 256

    def step(i, _):
        at = pl.ds(aligned(i * block, block), block)
        weights = weights_ref[shard].reshape(parts * features, depth)
        out_ref[shard, :, at] = dot(weights, normed_ref[at, :], 1, 1).astype(bf16)
        return 0

    lax.fori_loop(0, rows // block, step, 0)


def attend(qkv_ref, shard, head, count, probs_ref, context_ref, scale_ref, scores, keys, local_heads, pause):
    rows = qkv_ref.shape[2]
    width = local_heads * HEAD
    block, chunk, group = 256, 128, 64
    at = pl.ds(aligned(head * HEAD, HEAD), HEAD)
    number = shard * local_heads + head
    context_at = pl.ds(aligned(number * HEAD, HEAD), HEAD)
    masked = jnp.where(row_keep(count, 0, rows), 0.0, MASKED)
    first_lane = lax.broadcasted_iota(jnp.int32, (rows, HEAD), 1) == 0
    keys[:, :HEAD] = qkv_ref[shard, pl.ds(aligned(width + head * HEAD, HEAD), HEAD), :].T
    keys[:, HEAD:] = jnp.where(first_lane, masked, 0.0).astype(bf16)
    queries = jnp.concatenate([qkv_ref[shard, at, :], jnp.ones((HEAD, rows), bf16)], axis=0)
    values = qkv_ref[shard, pl.ds(aligned(2 * width + head * HEAD, HEAD), HEAD), :]
    values = jnp.concatenate([values, jnp.ones((16, rows), bf16)], axis=0)
    blocks = rows // block
    highest = None
    for i in range(blocks + 1):
        ahead = None
        for first in range(0, rows, chunk):
            part = slice(first, first + chunk)
            if i < blocks:
                product = dot(keys[part, :], queries[:, i * block : (i + 1) * block], 1, 0)
                scores[i % 2, part, :] = product
                top = jnp.max(product.reshape(chunk // group, group, block), axis=0)
                ahead = top if ahead is None else jnp.maximum(ahead, top)
            if i > 0:
                weights = jnp.exp(scores[(i - 1) % 2, part, :] - highest)
                probs_ref[part, (i - 1) * block : i * block] = weights.astype(bf16)
        if i > 0:
            columns = slice((i - 1) * block, i * block)
            context = dot(values, probs_ref[:, columns], 1, 0)
            scale = 1.0 / context[HEAD : HEAD + 1]
            context_ref[context_at, columns] = (context[:HEAD] * scale).astype(bf16)
            scale_ref[number, :, columns] = scale
        if i < blocks:
            highest = jnp.max(ahead, axis=0, keepdims=True)
            pause(0.4)


def gelu_parts(gate):
    root = 0.7978845608028654
    square = gate * gate
    bend = jnp.tanh(gate * (root + (root * 0.044715) * square))
    half = 0.5 + 0.5 * bend
    slope = half + (0.5 * gate) * (1.0 - bend * bend) * (root + (3 * root * 0.044715) * square)
    return gate * half, slope


def forward_kernel(
    extent,
    inputs,
    upstream,
    first_gain,
    second_gain,
    attention_source,
    output_source,
    gate_source,
    up_source,
    down_source,
    layer_output,
    qkv,
    probs_out,
    context_back,
    delta,
    hidden,
    weights_out,
    normed_one,
    wide_grad,
    gain_grad,
    attention_weights,
    output_weights,
    gate_weights,
    up_weights,
    down_weights,
    context,
    probs,
    scale,
    normed_two,
    out_low,
    forward_sum,
    back_sum,
    mixed_own,
    gate_own,
    up_own,
    scores,
    keys,
    local_sem,
    probs_sem,
    weights_sem,
    send_z,
    recv_z,
    send_x,
    recv_x,
    send_c,
    recv_c,
):
    dp, mp = lax.axis_index("dp"), lax.axis_index("mp")
    shards = attention_weights.shape[0]
    rows, depth = inputs.shape
    local_heads = attention_weights.shape[2] // HEAD
    count = extent[0, 0] * extent[0, 1]
    block = 256
    blocks = rows // block

    sources = (attention_source, output_source, gate_source, up_source, down_source)
    places = (attention_weights, output_weights, gate_weights, up_weights, down_weights)
    locals_ = [
        pltpu.make_async_copy(source, place.at[mp], local_sem.at[i])
        for i, (source, place) in enumerate(zip(sources, places))
    ]
    for copy in locals_:
        copy.start()
    barrier(
        [(flip(dp, j), mp) for j in (1, 2, 4)] + [(dp, flip(mp, k)) for k in range(1, shards)]
    )
    gather = Gather(sources, places, send_z, recv_z, send_x, recv_x, send_c, recv_c)
    jobs = [(kind, k) for kind in (0, 1) for k in range(1, shards)]
    jobs += [(kind, k) for k in range(1, shards) for kind in (2, 3, 4)]
    steps = gather.schedule(jobs)
    position = [0]
    clock = [0.0]

    def advance(stop):
        for step in steps[position[0] : stop]:
            step[1]()
        position[0] = max(position[0], stop)

    def pause(spent):
        clock[0] += spent
        advance(sum(step[0] <= clock[0] for step in steps))

    def until(job):
        where = [i for i, step in enumerate(steps) if step[3] and step[2] == job][0]
        clock[0] = max(clock[0], steps[where][0])
        advance(where + 1)

    def normalise(i, _):
        at = pl.ds(aligned(i * block, block), block)
        values = inputs[at, :].astype(f32)
        root = lax.rsqrt(jnp.mean(values * values, axis=-1, keepdims=True) + EPSILON)
        normed_one[at, :] = (values * root * first_gain[...]).astype(bf16)
        low = jnp.where(row_keep(count, i * block, block), upstream[at, :].astype(f32), 0.0)
        out_low[at, :] = low.astype(bf16)
        return 0

    lax.fori_loop(0, blocks, normalise, 0)
    pause(1.5)

    def probs_copy(slot, number):
        return pltpu.make_async_copy(probs.at[slot], probs_out.at[number], probs_sem.at[slot])

    done = 0
    for k in range(shards):
        shard = flip(mp, k)
        if k == 0:
            locals_[0].wait()
        else:
            until((0, k))
        project(attention_weights, normed_one, qkv, shard)
        pause(1.8)
        for head in range(local_heads):
            slot = done % 2
            number = shard * local_heads + head
            if done >= 2:
                probs_copy(slot, number).wait()
            attend(
                qkv,
                shard,
                head,
                count,
                probs.at[slot],
                context,
                scale,
                scores,
                keys,
                local_heads,
                pause,
            )
            probs_copy(slot, number).start()
            done += 1
    weights_copy = pltpu.make_async_copy(attention_weights, weights_out, weights_sem)
    weights_copy.start()

    locals_[1].wait()
    for k in range(1, shards):
        until((1, k))
    every_output = output_weights[...].reshape(depth, depth)

    def join(i, _):
        at = pl.ds(aligned(i * block, block), block)
        values = inputs[at, :].astype(f32) + dot(context[:, at], every_output, 0, 0)
        hidden[at, :] = values
        root = lax.rsqrt(jnp.mean(values * values, axis=-1, keepdims=True) + EPSILON)
        normed_two[at, :] = (values * root * second_gain[...]).astype(bf16)
        return 0

    lax.fori_loop(0, blocks, join, 0)
    pause(2.4)

    def feed(shard, k):
        def step(i, _):
            at = pl.ds(aligned(i * block, block), block)
            normed, low = normed_two[at, :], out_low[at, :]
            gate = dot(normed, gate_weights[shard], 1, 0)
            up = dot(normed, up_weights[shard], 1, 0)
            mixed_back = dot(low, down_weights[shard], 1, 1)
            bent, slope = gelu_parts(gate)
            mixed = (bent * up).astype(bf16)
            gate_back = (mixed_back * up * slope).astype(bf16)
            up_back = (mixed_back * bent).astype(bf16)
            ahead = dot(mixed, down_weights[shard], 1, 0)
            back = dot(gate_back, gate_weights[shard], 1, 1) + dot(up_back, up_weights[shard], 1, 1)
            if k == 0:
                mixed_own[at, :] = mixed
                gate_own[at, :] = gate_back
                up_own[at, :] = up_back
                forward_sum[at, :] = ahead
                back_sum[at, :] = back
            else:
                forward_sum[at, :] += ahead
                back_sum[at, :] += back
            return 0

        lax.fori_loop(0, blocks, step, 0)

    slices = wide_grad.shape[:3]
    width = gate_weights.shape[2]
    for k in range(shards):
        if k == 0:
            for copy in locals_[2:]:
                copy.wait()
        else:
            for kind in (2, 3, 4):
                until((kind, k))
        feed(flip(mp, k), k)
        pause(6.0)
        if k == 0:
            pairs = ((normed_two, gate_own), (normed_two, up_own), (out_low, mixed_own))
            for i, (left, right) in enumerate(pairs):
                part = dot(left[...], right[...], 0, 0).astype(bf16)
                wide_grad[:, :, :, i * width : (i + 1) * width] = part.reshape(*slices, width)
                pause(0.9)
    advance(len(steps))

    gain_grad[...] = jnp.zeros_like(gain_grad)

    def close(i, _):
        at = pl.ds(aligned(i * block, block), block)
        keep = row_keep(count, i * block, block)
        values, back = hidden[at, :], back_sum[at, :]
        layer_output[at, :] = jnp.where(keep, values + forward_sum[at, :], 0.0).astype(bf16)
        root = lax.rsqrt(jnp.mean(values * values, axis=-1, keepdims=True) + EPSILON)
        scaled = back * values
        gain_grad[0:1, :] += jnp.sum(scaled * root, axis=0, keepdims=True)
        mean = jnp.mean(scaled * second_gain[...], axis=-1, keepdims=True)
        out_back = jnp.where(keep, upstream[at, :].astype(f32), 0.0)
        result = out_back + root * (second_gain[...] * back) - values * (root * root * root * mean)
        hidden[at, :] = result
        normed_two[at, :] = result.astype(bf16)
        return 0

    lax.fori_loop(0, blocks, close, 0)
    hidden_low = normed_two
    every_output = output_weights[...].reshape(depth, depth)

    features = output_weights.shape[1]
    own = context[pl.ds(aligned(mp * features, 64), features), :]
    part = dot(own, hidden_low[...], 1, 0).T.astype(bf16)
    wide_grad[:, :, :, 3 * width : 3 * width + features] = part.reshape(*slices, features)

    heads = shards * local_heads

    def context_step(i, _):
        at = pl.ds(aligned(i * block, block), block)
        back = dot(every_output, hidden_low[at, :], 1, 1).reshape(heads, HEAD, block)
        low = (back * scale[:, :, at]).astype(bf16)
        context_back[:, at] = low.reshape(depth, block)
        ahead = context[:, at].reshape(heads, HEAD, block).astype(f32)
        delta[:, :, at] = jnp.sum(low.astype(f32) * ahead, axis=1, keepdims=True)
        return 0

    lax.fori_loop(0, blocks, context_step, 0)

    for slot, number in ((done % 2, 0), ((done + 1) % 2, 0)):
        probs_copy(slot, number).wait()
    weights_copy.wait()
    gather.finish()


def attend_back(qkv_ref, grad_ref, shard, head, probs, context_back, delta, score_back, local_heads):
    rows = qkv_ref.shape[2]
    width = local_heads * HEAD
    block = 256
    head_at = pl.ds(aligned(head * HEAD, HEAD), HEAD)
    key_at = pl.ds(aligned(width + head * HEAD, HEAD), HEAD)
    value_at = pl.ds(aligned(2 * width + head * HEAD, HEAD), HEAD)
    number = shard * local_heads + head
    upstream = context_back[pl.ds(aligned(number * HEAD, HEAD), HEAD), :]
    queries, keys = qkv_ref[shard, head_at, :], qkv_ref[shard, key_at, :]
    high = delta[number].astype(bf16)
    low = (delta[number] - high.astype(f32)).astype(bf16)
    right = jnp.concatenate([upstream, high, low, jnp.zeros((14, rows), bf16)], axis=0)
    lane = lax.broadcasted_iota(jnp.int32, (rows, 16), 1)
    minus = jnp.where(lane < 2, -1.0, 0.0).astype(bf16)
    left = jnp.concatenate([qkv_ref[shard, value_at, :].T, minus], axis=1)
    for first in range(0, rows, block):
        part = slice(first, first + block)
        for i in range(0, rows, block):
            columns = slice(i, i + block)
            change = dot(left[part], right[:, columns], 1, 0)
            score_back[part, columns] = (probs[part, columns].astype(f32) * change).astype(bf16)
        grad_ref[shard, value_at, part] = dot(upstream, probs[part, :], 1, 1).astype(bf16)
        grad_ref[shard, key_at, part] = dot(queries, score_back[part, :], 1, 1).astype(bf16)
    grad_ref[shard, head_at, :] = dot(keys, score_back[...], 1, 0).astype(bf16)


class Reduce:
    def __init__(self, local, from_core, staged, from_chips, total, sems):
        self.local, self.from_core, self.staged = local, from_core, staged
        self.from_chips, self.total, self.sems = from_chips, total, sems
        self.dp, self.mp = lax.axis_index("dp"), lax.axis_index("mp")
        self.core, self.chip = self.dp % 2, (self.dp // 2) % 4
        self.copies = []

    def begin(self):
        copy = pltpu.make_async_remote_copy(
            src_ref=self.local.at[:, 1 - self.core],
            dst_ref=self.from_core,
            send_sem=self.sems.at[0, 0],
            recv_sem=self.sems.at[1, 0],
            device_id=(flip(self.dp, 1), self.mp),
            device_id_type=MESH,
        )
        copy.start()
        self.first = copy

    def middle(self):
        self.first.wait()
        for j in (1, 2, 3, 0):
            chip = flip(self.chip, j)
            part = self.local[chip, self.core].astype(f32) + self.from_core[chip].astype(f32)
            if j == 0:
                self.total[...] = part
                continue
            self.staged[j - 1] = part.astype(bf16)
            copy = pltpu.make_async_remote_copy(
                src_ref=self.staged.at[j - 1],
                dst_ref=self.from_chips.at[j - 1],
                send_sem=self.sems.at[0, j],
                recv_sem=self.sems.at[1, j],
                device_id=(flip(self.dp, 2 * j), self.mp),
                device_id_type=MESH,
            )
            copy.start()
            self.copies.append(copy)

    def end(self):
        for copy in self.copies:
            copy.wait()
        self.total[...] += (
            self.from_chips[0].astype(f32)
            + self.from_chips[1].astype(f32)
            + self.from_chips[2].astype(f32)
        )


def backward_kernel(
    inputs,
    first_gain,
    qkv,
    probs_in,
    context_back,
    delta,
    hidden_back,
    weights,
    normed_one,
    wide_grad,
    gain_grad,
    input_grad,
    wide_total,
    narrow_total,
    gains_total,
    grads,
    probs,
    score_back,
    narrow_grad,
    wide_core,
    wide_staged,
    wide_chips,
    narrow_core,
    narrow_staged,
    narrow_chips,
    gains_own,
    gains_in,
    probs_sem,
    wide_sem,
    narrow_sem,
    gains_send,
    gains_recv,
):
    dp, mp = lax.axis_index("dp"), lax.axis_index("mp")
    shards = qkv.shape[0]
    local_heads = qkv.shape[1] // (3 * HEAD)
    rows, depth = inputs.shape
    block = 256
    blocks = rows // block

    heads = [(k, head) for k in range(shards) for head in range(local_heads)]

    def fetch(i):
        k, head = heads[i]
        number = flip(mp, k) * local_heads + head
        return pltpu.make_async_copy(probs_in.at[number], probs.at[i % 2], probs_sem.at[i % 2])

    fetch(0).start()
    barrier([(flip(dp, j), mp) for j in range(1, GROUP)])
    wide = Reduce(wide_grad, wide_core, wide_staged, wide_chips, wide_total, wide_sem)
    narrow = Reduce(narrow_grad, narrow_core, narrow_staged, narrow_chips, narrow_total, narrow_sem)
    wide.begin()
    for i, (k, head) in enumerate(heads):
        fetch(i).wait()
        if i + 1 < len(heads):
            fetch(i + 1).start()
        shard = flip(mp, k)
        attend_back(
            qkv, grads, shard, head, probs.at[i % 2], context_back, delta, score_back, local_heads
        )
        if i == 0:
            wide.middle()
        if i == local_heads - 1:
            part = dot(grads[mp], normed_one[...], 1, 0).T.astype(bf16)
            narrow_grad[...] = part.reshape(narrow_grad.shape)
            narrow.begin()
        if i == local_heads:
            narrow.middle()
        if i == len(heads) - 1:
            wide.end()
            narrow.end()

    gains_own[0:1, :] = gain_grad[0:1, :]
    gains_own[1:, :] = jnp.zeros((gains_own.shape[0] - 1, depth), f32)
    every_weight = weights[...].reshape(-1, depth)

    def close(i, _):
        at = pl.ds(aligned(i * block, block), block)
        values = inputs[at, :].astype(f32)
        back = dot(grads[:, :, at].reshape(-1, block), every_weight, 0, 0)
        root = lax.rsqrt(jnp.mean(values * values, axis=-1, keepdims=True) + EPSILON)
        scaled = back * values
        gains_own[1:2, :] += jnp.sum(scaled * root, axis=0, keepdims=True)
        mean = jnp.mean(scaled * first_gain[...], axis=-1, keepdims=True)
        input_grad[at, :] = (
            hidden_back[at, :]
            + root * (first_gain[...] * back)
            - values * (root * root * root * mean)
        )
        return 0

    lax.fori_loop(0, blocks, close, 0)
    copies = []
    for j in range(1, GROUP):
        copy = pltpu.make_async_remote_copy(
            src_ref=gains_own,
            dst_ref=gains_in.at[j - 1],
            send_sem=gains_send.at[j - 1],
            recv_sem=gains_recv.at[j - 1],
            device_id=(flip(dp, j), mp),
            device_id_type=MESH,
        )
        copy.start()
        copies.append(copy)
    for copy in copies:
        copy.wait()
    total = gains_own[...]
    for j in range(GROUP - 1):
        total = total + gains_in[j]
    gains_total[...] = total


def vmem():
    return pl.BlockSpec(memory_space=pltpu.VMEM)


def anywhere():
    return pl.BlockSpec(memory_space=pl.ANY)


def body(groups, shards, *arguments):
    (
        patches,
        attention_gain,
        query_weight,
        key_weight,
        value_weight,
        output_weight,
        feedforward_gain,
        gate_weight,
        up_weight,
        down_weight,
        cotangent,
        grid_extent,
    ) = arguments
    rows, depth = patches.shape
    features, units = query_weight.shape[1], gate_weight.shape[1]
    heads = shards * features // HEAD
    piece = depth // GROUP
    wide, narrow = 3 * units + features, 3 * features
    first_gain = attention_gain.astype(f32).reshape(1, depth)
    second_gain = feedforward_gain.astype(f32).reshape(1, depth)
    attention_source = jnp.stack([query_weight.T, key_weight.T, value_weight.T])

    shape = jax.ShapeDtypeStruct
    kinds = Gather.KINDS
    dma = pltpu.SemaphoreType.DMA
    (
        layer_output,
        qkv,
        probs,
        context_back,
        delta,
        hidden_back,
        weights,
        normed_one,
        wide_grad,
        gain_grad,
    ) = pl.pallas_call(
        forward_kernel,
        name="gather_forward",
        out_shape=(
            shape((rows, depth), bf16),
            shape((shards, narrow, rows), bf16),
            shape((heads, rows, rows), bf16),
            shape((depth, rows), bf16),
            shape((heads, 1, rows), f32),
            shape((rows, depth), f32),
            shape((shards, 3, features, depth), bf16),
            shape((rows, depth), bf16),
            shape((4, 2, piece, wide), bf16),
            shape((8, depth), f32),
        ),
        in_specs=[pl.BlockSpec(memory_space=pltpu.SMEM)] + [vmem()] * 4 + [anywhere()] * 5,
        out_specs=(
            vmem(),
            vmem(),
            anywhere(),
            vmem(),
            vmem(),
            vmem(),
            anywhere(),
            vmem(),
            vmem(),
            vmem(),
        ),
        scratch_shapes=[
            pltpu.VMEM((shards, 3, features, depth), bf16),
            pltpu.VMEM((shards, features, depth), bf16),
            pltpu.VMEM((shards, depth, units), bf16),
            pltpu.VMEM((shards, depth, units), bf16),
            pltpu.VMEM((shards, units, depth), bf16),
            pltpu.VMEM((depth, rows), bf16),
            pltpu.VMEM((2, rows, rows), bf16),
            pltpu.VMEM((heads, 1, rows), f32),
            pltpu.VMEM((rows, depth), bf16),
            pltpu.VMEM((rows, depth), bf16),
            pltpu.VMEM((rows, depth), f32),
            pltpu.VMEM((rows, depth), f32),
            pltpu.VMEM((rows, units), bf16),
            pltpu.VMEM((rows, units), bf16),
            pltpu.VMEM((rows, units), bf16),
            pltpu.VMEM((2, rows, 256), f32),
            pltpu.VMEM((rows, 2 * HEAD), bf16),
            dma((kinds,)),
            dma((2,)),
            dma,
            dma((kinds, shards)),
            dma((kinds, shards)),
            dma((kinds, shards, 4)),
            dma((kinds, shards, 4)),
            dma((kinds, shards, 4)),
            dma((kinds, shards, 4)),
        ],
        compiler_params=pltpu.CompilerParams(
            collective_id=0, has_side_effects=True, vmem_limit_bytes=VMEM_LIMIT
        ),
    )(
        grid_extent,
        patches,
        cotangent,
        first_gain,
        second_gain,
        attention_source,
        output_weight,
        gate_weight,
        up_weight,
        down_weight,
    )

    input_grad, wide_total, narrow_total, gains_total = pl.pallas_call(
        backward_kernel,
        name="attention_backward",
        out_shape=(
            shape((rows, depth), f32),
            shape((piece, wide), f32),
            shape((piece, narrow), f32),
            shape((8, depth), f32),
        ),
        in_specs=[vmem()] * 3 + [anywhere()] + [vmem()] * 7,
        out_specs=(vmem(),) * 4,
        scratch_shapes=[
            pltpu.VMEM((shards, narrow, rows), bf16),
            pltpu.VMEM((2, rows, rows), bf16),
            pltpu.VMEM((rows, rows), bf16),
            pltpu.VMEM((4, 2, piece, narrow), bf16),
            pltpu.VMEM((4, piece, wide), bf16),
            pltpu.VMEM((3, piece, wide), bf16),
            pltpu.VMEM((3, piece, wide), bf16),
            pltpu.VMEM((4, piece, narrow), bf16),
            pltpu.VMEM((3, piece, narrow), bf16),
            pltpu.VMEM((3, piece, narrow), bf16),
            pltpu.VMEM((8, depth), f32),
            pltpu.VMEM((GROUP - 1, 8, depth), f32),
            dma((2,)),
            dma((2, 4)),
            dma((2, 4)),
            dma((GROUP - 1,)),
            dma((GROUP - 1,)),
        ],
        compiler_params=pltpu.CompilerParams(
            collective_id=1, has_side_effects=True, vmem_limit_bytes=VMEM_LIMIT
        ),
    )(
        patches,
        first_gain,
        qkv,
        probs,
        context_back,
        delta,
        hidden_back,
        weights,
        normed_one,
        wide_grad,
        gain_grad,
    )

    index = lax.axis_index("dp")
    if groups > 1:

        def spread(block):
            whole = jnp.zeros((depth, block.shape[1]), f32)
            whole = lax.dynamic_update_slice(whole, block, ((index % GROUP) * piece, 0))
            return lax.psum_scatter(whole, "dp", scatter_dimension=0, tiled=True)

        wide_total, narrow_total = spread(wide_total), spread(narrow_total)
        gains_total = lax.psum(gains_total, "dp") / GROUP
    kept = depth // (groups * GROUP)
    gains = lax.dynamic_slice_in_dim(gains_total[:2], index * kept, kept, 1)
    return (
        layer_output,
        input_grad,
        gains[1],
        narrow_total[:, :features],
        narrow_total[:, features : 2 * features],
        narrow_total[:, 2 * features :],
        wide_total[:, 3 * units :].T,
        gains[0],
        wide_total[:, :units],
        wide_total[:, units : 2 * units],
        wide_total[:, 2 * units : 3 * units].T,
    )


def solution(mesh):
    placed = (
        P("dp", None),
        P(),
        P(None, "mp"),
        P(None, "mp"),
        P(None, "mp"),
        P("mp", None),
        P(),
        P(None, "mp"),
        P(None, "mp"),
        P("mp", None),
        P("dp", None),
        P("dp", None),
    )
    return jax.shard_map(
        functools.partial(body, mesh.shape["dp"] // GROUP, mesh.shape["mp"]),
        mesh=mesh,
        in_specs=placed,
        out_specs=(
            P("dp", None),
            P("dp", None),
            P("dp"),
            P("dp", "mp"),
            P("dp", "mp"),
            P("dp", "mp"),
            P("mp", "dp"),
            P("dp"),
            P("dp", "mp"),
            P("dp", "mp"),
            P("mp", "dp"),
        ),
        check_vma=False,
    )
```

```python
import functools

import jax
import jax.numpy as jnp
from jax import lax
from jax.experimental import pallas as pl
from jax.experimental.pallas import tpu as pltpu
from jax.sharding import PartitionSpec as P

HEAD = 64
EPSILON = 1e-06
MASKED = -1000000000.0
MESH = pl.DeviceIdType.MESH
f32 = jnp.float32
bf16 = jnp.bfloat16
GROUP = 8
VMEM_LIMIT = 61 << 20


def dot(left, right, left_dim, right_dim):
    return lax.dot_general(
        left, right, (((left_dim,), (right_dim,)), ((), ())), preferred_element_type=f32
    )


def flip(value, bits):
    result = value
    for bit in (1, 2, 4):
        if bits & bit:
            result = result + bit - 2 * bit * ((value // bit) % 2)
    return result


def cross(value, mask):
    low = (value + mask) % 2
    return low + 2 * ((value // 2 + mask // 2) % 2)


def aligned(value, multiple):
    return pl.multiple_of(value, multiple)


class Gather:
    KINDS = 5

    def __init__(self, sources, places, send_z, recv_z, send_x, recv_x, send_c, recv_c):
        self.dp, self.mp = lax.axis_index("dp"), lax.axis_index("mp")
        self.core = self.dp % 2
        self.chip = (self.dp // 2) % 4
        self.sources, self.places = sources, places
        self.sems = (send_z, recv_z, send_x, recv_x, send_c, recv_c)
        self.sends = []

    def part(self, ref, lead, quarter, half):
        rows, columns = ref.shape[-2] // 4, ref.shape[-1] // 2
        window = (
            pl.ds(aligned(quarter * rows, 16), rows),
            pl.ds(aligned(half * columns, 128), columns),
        )
        middle = (slice(None),) * (len(ref.shape) - 2 - len(lead))
        return ref.at[(*lead, *middle, *window)]

    def place(self, kind, shard, quarter, half):
        return self.part(self.places[kind], (shard,), quarter, half)

    def copy(self, source, target, send, recv, dp, mp):
        return pltpu.make_async_remote_copy(
            src_ref=source,
            dst_ref=target,
            send_sem=send,
            recv_sem=recv,
            device_id=(dp, mp),
            device_id_type=MESH,
        )

    def start(self, make, *which):
        make(*which).start()
        self.sends.append((make, which))

    def arrived(self, target, send, recv):
        self.copy(target, target, send, recv, self.dp, self.mp).wait_recv()

    def along_mp(self, kind, k):
        send_z, recv_z = self.sems[:2]
        target = self.place(kind, self.mp, self.chip, self.core)
        source = target
        if self.sources[kind] is not None:
            source = self.part(self.sources[kind], (), self.chip, self.core)
        peer = flip(self.mp, k)
        return self.copy(source, target, send_z.at[kind, k], recv_z.at[kind, k], self.dp, peer)

    def to_core(self, kind, k, j):
        piece = self.place(kind, flip(self.mp, k), flip(self.chip, j), self.core)
        send_c, recv_c = self.sems[4:]
        peer = flip(self.dp, 1)
        return self.copy(piece, piece, send_c.at[kind, k, j], recv_c.at[kind, k, j], peer, self.mp)

    def to_chip(self, kind, k, j):
        send_x, recv_x = self.sems[2:4]
        quarter, peer = self.chip, flip(self.dp, 2 * j)
        if j == 3:
            from_y, from_x = flip(self.chip, 2), flip(self.chip, 1)
            to_x, to_y = flip(self.dp, 2), flip(self.dp, 4)
            quarter = from_y + self.core * (from_x - from_y)
            peer = to_x + self.core * (to_y - to_x)
        piece = self.place(kind, flip(self.mp, k), quarter, self.core)
        return self.copy(piece, piece, send_x.at[kind, k, j], recv_x.at[kind, k, j], peer, self.mp)

    def to_chips(self, kind, k):
        send_z, recv_z = self.sems[:2]
        piece = self.place(kind, flip(self.mp, k), self.chip, self.core)
        self.arrived(piece, send_z.at[kind, k], recv_z.at[kind, k])
        self.start(self.to_chip, kind, k, 1)
        self.start(self.to_chip, kind, k, 2)
        self.start(self.to_core, kind, k, 0)

    def to_corner(self, kind, k):
        send_x, recv_x = self.sems[2:4]
        for j in (1, 2):
            piece = self.place(kind, flip(self.mp, k), flip(self.chip, j), self.core)
            self.arrived(piece, send_x.at[kind, k, j], recv_x.at[kind, k, j])
        self.start(self.to_chip, kind, k, 3)
        self.start(self.to_core, kind, k, 1)
        self.start(self.to_core, kind, k, 2)

    def last_core(self, kind, k):
        send_x, recv_x = self.sems[2:4]
        piece = self.place(kind, flip(self.mp, k), flip(self.chip, 3), self.core)
        self.arrived(piece, send_x.at[kind, k, 3], recv_x.at[kind, k, 3])
        self.start(self.to_core, kind, k, 3)

    def settled(self, kind, k):
        send_c, recv_c = self.sems[4:]
        for j in range(4):
            piece = self.place(kind, flip(self.mp, k), flip(self.chip, j), 1 - self.core)
            self.arrived(piece, send_c.at[kind, k, j], recv_c.at[kind, k, j])

    def schedule(self, jobs, window=8, start=3.0, pace=2.6, lags=(5.0, 10.0, 12.0)):
        for job in jobs[:window]:
            self.start(self.along_mp, *job)

        def first(i):
            self.to_chips(*jobs[i])
            if i + window < len(jobs):
                self.start(self.along_mp, *jobs[i + window])

        steps = []
        clock = start
        for i, job in enumerate(jobs):
            clock += 0.37 * pace if job[0] == 1 else pace
            steps.append((clock, functools.partial(first, i), job, False))
            later = (self.to_corner, self.last_core, self.settled)
            for lag, step in zip(lags, later):
                steps.append((clock + lag, functools.partial(step, *job), job, step == later[-1]))
        return sorted(steps, key=lambda step: step[0])

    def finish(self):
        for make, which in self.sends:
            make(*which).wait_send()


def announce(devices):
    semaphore = pltpu.get_barrier_semaphore()
    for device in devices:
        pl.semaphore_signal(semaphore, inc=1, device_id=device, device_id_type=MESH)
    return semaphore


def row_keep(count, first, rows):
    return lax.broadcasted_iota(jnp.int32, (rows, 1), 0) + first < count


def project(weights_ref, normed_ref, out_ref, shard):
    parts, features, depth = weights_ref.shape[1:]
    rows = normed_ref.shape[0]
    block = 256

    def step(i, _):
        at = pl.ds(aligned(i * block, block), block)
        weights = weights_ref[shard].reshape(parts * features, depth)
        out_ref[shard, :, at] = dot(weights, normed_ref[at, :], 1, 1).astype(bf16)
        return 0

    lax.fori_loop(0, rows // block, step, 0)


def attend(qkv_ref, shard, head, count, probs_ref, context_ref, scale_ref, scores, keys, local_heads, pause):
    rows = qkv_ref.shape[2]
    width = local_heads * HEAD
    block, chunk, group = 256, 128, 64
    at = pl.ds(aligned(head * HEAD, HEAD), HEAD)
    number = shard * local_heads + head
    context_at = pl.ds(aligned(number * HEAD, HEAD), HEAD)
    masked = jnp.where(row_keep(count, 0, rows), 0.0, MASKED)
    first_lane = lax.broadcasted_iota(jnp.int32, (rows, HEAD), 1) == 0
    keys[:, :HEAD] = qkv_ref[shard, pl.ds(aligned(width + head * HEAD, HEAD), HEAD), :].T
    keys[:, HEAD:] = jnp.where(first_lane, masked, 0.0).astype(bf16)
    queries = jnp.concatenate([qkv_ref[shard, at, :], jnp.ones((HEAD, rows), bf16)], axis=0)
    values = qkv_ref[shard, pl.ds(aligned(2 * width + head * HEAD, HEAD), HEAD), :]
    values = jnp.concatenate([values, jnp.ones((16, rows), bf16)], axis=0)
    blocks = rows // block
    highest = None
    for i in range(blocks + 1):
        ahead = None
        for first in range(0, rows, chunk):
            part = slice(first, first + chunk)
            if i < blocks:
                product = dot(keys[part, :], queries[:, i * block : (i + 1) * block], 1, 0)
                scores[i % 2, part, :] = product
                top = jnp.max(product.reshape(chunk // group, group, block), axis=0)
                ahead = top if ahead is None else jnp.maximum(ahead, top)
            if i > 0:
                weights = jnp.exp(scores[(i - 1) % 2, part, :] - highest)
                probs_ref[part, (i - 1) * block : i * block] = weights.astype(bf16)
        if i > 0:
            columns = slice((i - 1) * block, i * block)
            context = dot(values, probs_ref[:, columns], 1, 0)
            scale = 1.0 / context[HEAD : HEAD + 1]
            context_ref[context_at, columns] = (context[:HEAD] * scale).astype(bf16)
            scale_ref[number, :, columns] = scale
        if i < blocks:
            highest = jnp.max(ahead, axis=0, keepdims=True)
            pause(0.4)


def gelu_parts(gate):
    root = 0.7978845608028654
    square = gate * gate
    bend = jnp.tanh(gate * (root + (root * 0.044715) * square))
    half = 0.5 + 0.5 * bend
    slope = half + (0.5 * gate) * (1.0 - bend * bend) * (root + (3 * root * 0.044715) * square)
    return gate * half, slope


def attend_back(qkv_ref, grad_ref, shard, head, probs, context_back, delta, score_back, local_heads):
    rows = qkv_ref.shape[2]
    width = local_heads * HEAD
    block = 256
    head_at = pl.ds(aligned(head * HEAD, HEAD), HEAD)
    key_at = pl.ds(aligned(width + head * HEAD, HEAD), HEAD)
    value_at = pl.ds(aligned(2 * width + head * HEAD, HEAD), HEAD)
    number = shard * local_heads + head
    upstream = context_back[pl.ds(aligned(number * HEAD, HEAD), HEAD), :]
    queries, keys = qkv_ref[shard, head_at, :], qkv_ref[shard, key_at, :]
    high = delta[number].astype(bf16)
    low = (delta[number] - high.astype(f32)).astype(bf16)
    right = jnp.concatenate([upstream, high, low, jnp.zeros((14, rows), bf16)], axis=0)
    lane = lax.broadcasted_iota(jnp.int32, (rows, 16), 1)
    minus = jnp.where(lane < 2, -1.0, 0.0).astype(bf16)
    left = jnp.concatenate([qkv_ref[shard, value_at, :].T, minus], axis=1)
    for first in range(0, rows, block):
        part = slice(first, first + block)
        for i in range(0, rows, block):
            columns = slice(i, i + block)
            change = dot(left[part], right[:, columns], 1, 0)
            score_back[part, columns] = (probs[part, columns].astype(f32) * change).astype(bf16)
        grad_ref[shard, value_at, part] = dot(upstream, probs[part, :], 1, 1).astype(bf16)
        grad_ref[shard, key_at, part] = dot(queries, score_back[part, :], 1, 1).astype(bf16)
    grad_ref[shard, head_at, :] = dot(keys, score_back[...], 1, 0).astype(bf16)


class Reduce:
    def __init__(self, local, from_core, from_chips, total, sems):
        self.local, self.from_core = local, from_core
        self.from_chips, self.total, self.sems = from_chips, total, sems
        self.dp, self.mp = lax.axis_index("dp"), lax.axis_index("mp")
        self.core, self.chip = self.dp % 2, (self.dp // 2) % 4

    def copy(self, j):
        if j == 0:
            source, target, peer = self.local.at[:, 1 - self.core], self.from_core, flip(self.dp, 1)
        else:
            source, target = self.local.at[flip(self.chip, j), self.core], self.from_chips.at[j - 1]
            peer = flip(self.dp, 2 * j)
        return pltpu.make_async_remote_copy(
            src_ref=source,
            dst_ref=target,
            send_sem=self.sems.at[0, j],
            recv_sem=self.sems.at[1, j],
            device_id=(peer, self.mp),
            device_id_type=MESH,
        )

    def begin(self):
        self.copy(0).start()

    def middle(self):
        self.copy(0).wait()
        for j in (1, 2, 3, 0):
            chip = flip(self.chip, j)
            part = self.local[chip, self.core].astype(f32) + self.from_core[chip].astype(f32)
            if j == 0:
                self.total[...] = part
            else:
                self.local[chip, self.core] = part.astype(bf16)
                self.copy(j).start()

    def end(self):
        for j in (1, 2, 3):
            self.copy(j).wait()
        first, second, third = (self.from_chips[i].astype(f32) for i in range(3))
        self.total[...] += first + second + third


def main_kernel(
    extent,
    inputs,
    first_gain,
    second_gain,
    upstream,
    query_source,
    key_source,
    value_source,
    output_source,
    gate_source,
    up_source,
    down_source,
    layer_output,
    probs_out,
    grads_out,
    weights_out,
    hidden_out,
    wide_total,
    narrow_total,
    gains_total,
    attention_weights,
    output_weights,
    gate_weights,
    up_weights,
    down_weights,
    qkv,
    context,
    normed_one,
    normed_two,
    out_low,
    hidden,
    scale,
    delta,
    context_back,
    wide_grad,
    narrow_grad,
    wide_core,
    wide_chips,
    narrow_core,
    narrow_chips,
    gains_own,
    gains_in,
    own_weights,
    local_sem,
    probs_sem,
    out_sem,
    grads_sem,
    wide_sem,
    narrow_sem,
    gains_sem,
    send_z,
    recv_z,
    send_x,
    recv_x,
    send_c,
    recv_c,
):
    dp, mp = lax.axis_index("dp"), lax.axis_index("mp")
    shards = attention_weights.shape[0]
    rows, depth = inputs.shape
    features = output_weights.shape[1]
    units = gate_weights.shape[2]
    local_heads = features // HEAD
    heads = shards * local_heads
    count = extent[0, 0] * extent[0, 1]
    block = 256
    blocks = rows // block

    def each_block(step):
        def run(i, _):
            step(i * block, pl.ds(aligned(i * block, block), block))
            return 0

        lax.fori_loop(0, blocks, run, 0)

    sources = (None, output_source, gate_source, up_source, down_source)
    places = (attention_weights, output_weights, gate_weights, up_weights, down_weights)
    owned = [
        pltpu.make_async_copy(source, place.at[mp], local_sem.at[i])
        for i, (source, place) in enumerate(zip(sources[1:], places[1:]))
    ]
    owned.append(pltpu.make_async_copy(upstream, out_low, local_sem.at[4]))
    turned = [
        pltpu.make_async_copy(source, attention_weights.at[mp, i], local_sem.at[5 + i])
        for i, source in enumerate((query_source, key_source, value_source))
    ]
    peers = [(flip(dp, j), mp) for j in range(1, GROUP)]
    peers += [(dp, flip(mp, k)) for k in range(1, shards)]
    semaphore = announce(peers)
    for copy in turned + owned:
        copy.start()
    for copy in turned:
        copy.wait()
    own_weights[...] = attention_weights[mp].reshape(3 * features, depth).T
    pl.semaphore_wait(semaphore, len(peers))
    gather = Gather(sources, places, send_z, recv_z, send_x, recv_x, send_c, recv_c)
    jobs = [(kind, k) for kind in (0, 1) for k in range(1, shards)]
    jobs += [(kind, k) for k in range(1, shards) for kind in (2, 3, 4)]
    steps = gather.schedule(jobs)
    position = [0]
    clock = [0.0]

    def advance(stop):
        for step in steps[position[0] : stop]:
            step[1]()
        position[0] = max(position[0], stop)

    def pause(spent):
        clock[0] += spent
        advance(sum(step[0] <= clock[0] for step in steps))

    def until(job):
        where = [i for i, step in enumerate(steps) if step[3] and step[2] == job][0]
        clock[0] = max(clock[0], steps[where][0])
        advance(where + 1)

    def gain_of(ref):
        return ref[...].astype(f32).reshape(1, depth)

    def normalise(first, at):
        values = inputs[at, :].astype(f32)
        root = lax.rsqrt(jnp.mean(values * values, axis=-1, keepdims=True) + EPSILON)
        normed_one[at, :] = (values * root * gain_of(first_gain)).astype(bf16)

    each_block(normalise)
    pause(1.5)

    def join(first, at):
        every_output = output_weights[...].reshape(depth, depth)
        values = inputs[at, :].astype(f32) + dot(context[:, at], every_output, 0, 0)
        hidden[at, :] = values
        root = lax.rsqrt(jnp.mean(values * values, axis=-1, keepdims=True) + EPSILON)
        normed_two[at, :] = (values * root * gain_of(second_gain)).astype(bf16)
        out_low[at, :] = jnp.where(row_keep(count, first, block), out_low[at, :], jnp.zeros((), bf16))

    def attention(probs, scores, keys):
        def probs_copy(slot, number):
            return pltpu.make_async_copy(probs.at[slot], probs_out.at[number], probs_sem.at[slot])

        done = 0
        for k in range(shards):
            shard = flip(mp, k)
            if k > 0:
                until((0, k))
            project(attention_weights, normed_one, qkv, shard)
            pause(1.8)
            for head in range(local_heads):
                slot = done % 2
                number = shard * local_heads + head
                if done >= 2:
                    probs_copy(slot, number).wait()
                attend(
                    qkv,
                    shard,
                    head,
                    count,
                    probs.at[slot],
                    context,
                    scale,
                    scores,
                    keys,
                    local_heads,
                    pause,
                )
                probs_copy(slot, number).start()
                done += 1
        pltpu.make_async_copy(attention_weights, weights_out, out_sem.at[0]).start()
        owned[0].wait()
        owned[4].wait()
        for k in range(1, shards):
            until((1, k))
        each_block(join)
        pause(2.4)
        for slot in (done % 2, (done + 1) % 2):
            probs_copy(slot, 0).wait()

    pl.run_scoped(
        attention,
        pltpu.VMEM((2, rows, rows), bf16),
        pltpu.VMEM((2, rows, block), f32),
        pltpu.VMEM((rows, 2 * HEAD), bf16),
    )

    slices = wide_grad.shape[:3]

    def feed_forward(forward_sum, back_sum, mixed_own, gate_own, up_own):
        def feed(shard, k):
            def step(first, at):
                normed, low = normed_two[at, :], out_low[at, :]
                gate = dot(normed, gate_weights[shard], 1, 0)
                up = dot(normed, up_weights[shard], 1, 0)
                mixed_back = dot(low, down_weights[shard], 1, 1)
                bent, slope = gelu_parts(gate)
                mixed = (bent * up).astype(bf16)
                gate_back = (mixed_back * up * slope).astype(bf16)
                up_back = (mixed_back * bent).astype(bf16)
                ahead = dot(mixed, down_weights[shard], 1, 0)
                back = dot(gate_back, gate_weights[shard], 1, 1)
                back = back + dot(up_back, up_weights[shard], 1, 1)
                if k == 0:
                    mixed_own[at, :] = mixed
                    gate_own[at, :] = gate_back
                    up_own[at, :] = up_back
                    forward_sum[at, :] = ahead
                    back_sum[at, :] = back
                else:
                    forward_sum[at, :] += ahead
                    back_sum[at, :] += back

            each_block(step)

        for k in range(shards):
            if k == 0:
                for copy in owned[1:4]:
                    copy.wait()
            else:
                for kind in (2, 3, 4):
                    until((kind, k))
            feed(flip(mp, k), k)
            pause(6.0)
            if k == 0:
                pairs = ((normed_two, gate_own), (normed_two, up_own), (out_low, mixed_own))
                for i, (left, right) in enumerate(pairs):
                    part = dot(left[...], right[...], 0, 0).astype(bf16)
                    wide_grad[:, :, :, i * units : (i + 1) * units] = part.reshape(*slices, units)
                    pause(0.9)
        advance(len(steps))

        def close(first, at):
            keep = row_keep(count, first, block)
            values, back = hidden[at, :], back_sum[at, :]
            out_back = out_low[at, :].astype(f32)
            out_low[at, :] = jnp.where(keep, values + forward_sum[at, :], 0.0).astype(bf16)
            root = lax.rsqrt(jnp.mean(values * values, axis=-1, keepdims=True) + EPSILON)
            scaled = gain_of(second_gain) * back
            mean = jnp.mean(scaled * values, axis=-1, keepdims=True)
            result = out_back + root * scaled - values * (root * root * root * mean)
            hidden[at, :] = result
            normed_two[at, :] = result.astype(bf16)

        each_block(close)

    pl.run_scoped(
        feed_forward,
        pltpu.VMEM((rows, depth), f32),
        pltpu.VMEM((rows, depth), f32),
        pltpu.VMEM((rows, units), bf16),
        pltpu.VMEM((rows, units), bf16),
        pltpu.VMEM((rows, units), bf16),
    )
    pltpu.make_async_copy(out_low, layer_output, out_sem.at[1]).start()
    pltpu.make_async_copy(hidden, hidden_out, out_sem.at[2]).start()
    hidden_low = normed_two
    own = context[pl.ds(aligned(mp * features, HEAD), features), :]
    part = dot(own, hidden_low[...], 1, 0).T.astype(bf16)
    wide_grad[:, :, :, 3 * units :] = part.reshape(*slices, features)
    wide = Reduce(wide_grad, wide_core, wide_chips, wide_total, wide_sem)
    narrow = Reduce(narrow_grad, narrow_core, narrow_chips, narrow_total, narrow_sem)
    wide.begin()

    def context_step(first, at):
        every_output = output_weights[...].reshape(depth, depth)
        back = dot(every_output, hidden_low[at, :], 1, 1).reshape(heads, HEAD, block)
        low = (back * scale[:, :, at]).astype(bf16)
        context_back[:, at] = low.reshape(depth, block)
        ahead = context[:, at].reshape(heads, HEAD, block).astype(f32)
        delta[:, :, at] = jnp.sum(low.astype(f32) * ahead, axis=1, keepdims=True)

    each_block(context_step)

    def gains_copy(k):
        return pltpu.make_async_remote_copy(
            src_ref=gains_own,
            dst_ref=gains_in.at[k - 1],
            send_sem=gains_sem.at[0, k],
            recv_sem=gains_sem.at[1, k],
            device_id=(dp, flip(mp, k)),
            device_id_type=MESH,
        )

    def gains():
        piece = gains_own.shape[0]
        at = pl.ds(aligned((dp % GROUP) * piece, 32), piece)
        second = gate_weights[mp, at, :].astype(f32) * wide_total[:, :units]
        second = second + up_weights[mp, at, :].astype(f32) * wide_total[:, units : 2 * units]
        first = own_weights[at, :].astype(f32) * narrow_total[...]
        lane = lax.broadcasted_iota(jnp.int32, gains_own.shape, 1)
        first = jnp.sum(first, axis=1, keepdims=True)
        second = jnp.sum(second, axis=1, keepdims=True)
        gains_own[...] = jnp.where(lane == 0, first, jnp.where(lane == 1, second, 0.0))
        for k in range(1, shards):
            gains_copy(k).start()

    def attention_back(probs, score_back, grads):
        def fetch(i):
            number = cross(mp, i // local_heads) * local_heads + i % local_heads
            return pltpu.make_async_copy(probs_out.at[number], probs.at[i % 2], probs_sem.at[i % 2])

        def keep_grads(shard, k):
            return pltpu.make_async_copy(grads.at[shard], grads_out.at[shard], grads_sem.at[k])

        def step(i, _):
            k, head = i // local_heads, i % local_heads
            shard = cross(mp, k)
            fetch(i).wait()

            @pl.when(i + 1 < heads)
            def _():
                fetch(i + 1).start()

            attend_back(
                qkv,
                grads,
                shard,
                head,
                probs.at[i % 2],
                context_back,
                delta,
                score_back,
                local_heads,
            )

            @pl.when(head == local_heads - 1)
            def _():
                keep_grads(shard, k).start()

            @pl.when(i == local_heads - 1)
            def _():
                wide.middle()
                part = dot(grads[mp], normed_one[...], 1, 0).T.astype(bf16)
                narrow_grad[...] = part.reshape(narrow_grad.shape)
                narrow.begin()

            @pl.when(i == local_heads)
            def _():
                narrow.middle()

            @pl.when(i == heads - 2)
            def _():
                wide.end()
                narrow.end()
                gains()

            return 0

        fetch(0).start()
        lax.fori_loop(0, heads, step, 0)
        for k in range(shards):
            keep_grads(flip(mp, k), k).wait()

    pl.run_scoped(
        attention_back,
        pltpu.VMEM((2, rows, rows), bf16),
        pltpu.VMEM((rows, rows), bf16),
        pltpu.VMEM((shards, 3 * features, rows), bf16),
    )
    for k in range(1, shards):
        gains_copy(k).wait()
    gains_total[...] = (gains_own[...] + gains_in[0]) + (gains_in[1] + gains_in[2])
    pltpu.make_async_copy(attention_weights, weights_out, out_sem.at[0]).wait()
    pltpu.make_async_copy(out_low, layer_output, out_sem.at[1]).wait()
    pltpu.make_async_copy(hidden, hidden_out, out_sem.at[2]).wait()
    gather.finish()


def close_kernel(
    grads,
    weights,
    hidden_back,
    inputs,
    first_gain,
    layer_in,
    wide_total,
    narrow_total,
    input_grad,
    layer_output,
    query_grad,
    key_grad,
    value_grad,
    output_grad,
    gate_grad,
    up_grad,
    down_grad,
):
    shards, narrow, block = grads.shape
    depth = inputs.shape[1]
    values = inputs[...].astype(f32)
    every_weight = weights[...].reshape(shards * narrow, depth)
    back = dot(grads[...].reshape(shards * narrow, block), every_weight, 0, 0)
    root = lax.rsqrt(jnp.mean(values * values, axis=-1, keepdims=True) + EPSILON)
    scaled = first_gain[...].astype(f32).reshape(1, depth) * back
    mean = jnp.mean(scaled * values, axis=-1, keepdims=True)
    result = hidden_back[...] + root * scaled
    input_grad[...] = result - values * (root * root * root * mean)
    layer_output[...] = layer_in[...]

    @pl.when(pl.program_id(0) == 0)
    def _():
        features, units = query_grad.shape[1], gate_grad.shape[1]
        query_grad[...] = narrow_total[:, :features]
        key_grad[...] = narrow_total[:, features : 2 * features]
        value_grad[...] = narrow_total[:, 2 * features :]
        gate_grad[...] = wide_total[:, :units]
        up_grad[...] = wide_total[:, units : 2 * units]
        down_grad[...] = wide_total[:, 2 * units : 3 * units].T
        output_grad[...] = wide_total[:, 3 * units :].T


def vmem():
    return pl.BlockSpec(memory_space=pltpu.VMEM)


def anywhere():
    return pl.BlockSpec(memory_space=pl.ANY)


def body(groups, shards, *arguments):
    (
        patches,
        attention_gain,
        query_weight,
        key_weight,
        value_weight,
        output_weight,
        feedforward_gain,
        gate_weight,
        up_weight,
        down_weight,
        cotangent,
        grid_extent,
    ) = arguments
    rows, depth = patches.shape
    features, units = query_weight.shape[1], gate_weight.shape[1]
    heads = shards * features // HEAD
    piece = depth // GROUP
    wide, narrow = 3 * units + features, 3 * features

    shape = jax.ShapeDtypeStruct
    kinds = Gather.KINDS
    dma = pltpu.SemaphoreType.DMA
    (
        layer_output,
        _,
        grads,
        weights,
        hidden_back,
        wide_total,
        narrow_total,
        gains_total,
    ) = pl.pallas_call(
        main_kernel,
        name="layer",
        out_shape=(
            shape((rows, depth), bf16),
            shape((heads, rows, rows), bf16),
            shape((shards, narrow, rows), bf16),
            shape((shards, 3, features, depth), bf16),
            shape((rows, depth), f32),
            shape((piece, wide), f32),
            shape((piece, narrow), f32),
            shape((piece, 128), f32),
        ),
        in_specs=[pl.BlockSpec(memory_space=pltpu.SMEM)] + [vmem()] * 3 + [anywhere()] * 8,
        out_specs=(anywhere(),) * 5 + (vmem(),) * 3,
        scratch_shapes=[
            pltpu.VMEM((shards, 3, features, depth), bf16),
            pltpu.VMEM((shards, features, depth), bf16),
            pltpu.VMEM((shards, depth, units), bf16),
            pltpu.VMEM((shards, depth, units), bf16),
            pltpu.VMEM((shards, units, depth), bf16),
            pltpu.VMEM((shards, narrow, rows), bf16),
            pltpu.VMEM((depth, rows), bf16),
            pltpu.VMEM((rows, depth), bf16),
            pltpu.VMEM((rows, depth), bf16),
            pltpu.VMEM((rows, depth), bf16),
            pltpu.VMEM((rows, depth), f32),
            pltpu.VMEM((heads, 1, rows), f32),
            pltpu.VMEM((heads, 1, rows), f32),
            pltpu.VMEM((depth, rows), bf16),
            pltpu.VMEM((4, 2, piece, wide), bf16),
            pltpu.VMEM((4, 2, piece, narrow), bf16),
            pltpu.VMEM((4, piece, wide), bf16),
            pltpu.VMEM((3, piece, wide), bf16),
            pltpu.VMEM((4, piece, narrow), bf16),
            pltpu.VMEM((3, piece, narrow), bf16),
            pltpu.VMEM((piece, 128), f32),
            pltpu.VMEM((3, piece, 128), f32),
            pltpu.VMEM((depth, narrow), bf16),
            dma((8,)),
            dma((2,)),
            dma((3,)),
            dma((shards,)),
            dma((2, 4)),
            dma((2, 4)),
            dma((2, shards)),
            dma((kinds, shards)),
            dma((kinds, shards)),
            dma((kinds, shards, 4)),
            dma((kinds, shards, 4)),
            dma((kinds, shards, 4)),
            dma((kinds, shards, 4)),
        ],
        compiler_params=pltpu.CompilerParams(
            collective_id=0, has_side_effects=True, vmem_limit_bytes=VMEM_LIMIT
        ),
    )(
        grid_extent,
        patches,
        attention_gain,
        feedforward_gain,
        cotangent,
        query_weight.T,
        key_weight.T,
        value_weight.T,
        output_weight,
        gate_weight,
        up_weight,
        down_weight,
    )

    block = 256

    def whole(*dims):
        return pl.BlockSpec(dims, lambda i: (0,) * len(dims))

    by_rows = pl.BlockSpec((block, depth), lambda i: (i, 0))
    small = [(piece, features)] * 3 + [(features, piece)] + [(piece, units)] * 2 + [(units, piece)]
    input_grad, layer_output, *small_grads = pl.pallas_call(
        close_kernel,
        name="close",
        grid=(rows // block,),
        out_shape=[shape((rows, depth), f32), shape((rows, depth), bf16)]
        + [shape(dims, f32) for dims in small],
        in_specs=[
            pl.BlockSpec((shards, narrow, block), lambda i: (0, 0, i)),
            whole(shards, 3, features, depth),
            by_rows,
            by_rows,
            whole(depth),
            by_rows,
            whole(piece, wide),
            whole(piece, narrow),
        ],
        out_specs=[by_rows, by_rows] + [whole(*dims) for dims in small],
        compiler_params=pltpu.CompilerParams(vmem_limit_bytes=VMEM_LIMIT),
    )(grads, weights, hidden_back, patches, attention_gain, layer_output, wide_total, narrow_total)

    index = lax.axis_index("dp")
    gains_total = gains_total[:, :2]
    if groups > 1:

        def spread(block, turned=False):
            block = block.T if turned else block
            whole = jnp.zeros((depth, block.shape[1]), f32)
            whole = lax.dynamic_update_slice(whole, block, ((index % GROUP) * piece, 0))
            own = lax.psum_scatter(whole, "dp", scatter_dimension=0, tiled=True)
            return own.T if turned else own

        small_grads = [spread(grad, i in (3, 6)) for i, grad in enumerate(small_grads)]
        gains_total = spread(gains_total)
    kept = depth // (groups * GROUP)

    def gain_grad(column, gain):
        own = lax.dynamic_slice_in_dim(gain.astype(f32), index * kept, kept)
        return gains_total[:, column] / own

    query_grad, key_grad, value_grad, output_grad, gate_grad, up_grad, down_grad = small_grads
    return (
        layer_output,
        input_grad,
        gain_grad(0, attention_gain),
        query_grad,
        key_grad,
        value_grad,
        output_grad,
        gain_grad(1, feedforward_gain),
        gate_grad,
        up_grad,
        down_grad,
    )


def solution(mesh):
    placed = (
        P("dp", None),
        P(),
        P(None, "mp"),
        P(None, "mp"),
        P(None, "mp"),
        P("mp", None),
        P(),
        P(None, "mp"),
        P(None, "mp"),
        P("mp", None),
        P("dp", None),
        P("dp", None),
    )
    return jax.shard_map(
        functools.partial(body, mesh.shape["dp"] // GROUP, mesh.shape["mp"]),
        mesh=mesh,
        in_specs=placed,
        out_specs=(
            P("dp", None),
            P("dp", None),
            P("dp"),
            P("dp", "mp"),
            P("dp", "mp"),
            P("dp", "mp"),
            P("mp", "dp"),
            P("dp"),
            P("dp", "mp"),
            P("dp", "mp"),
            P("mp", "dp"),
        ),
        check_vma=False,
    )
```

```python
import functools

import jax
import jax.numpy as jnp
from jax import lax
from jax.experimental import pallas as pl
from jax.experimental.pallas import tpu as pltpu
from jax.sharding import PartitionSpec as P

HEAD = 64
EPSILON = 1e-06
MASKED = -1000000000.0
MESH = pl.DeviceIdType.MESH
f32 = jnp.float32
bf16 = jnp.bfloat16
GROUP = 8
VMEM_LIMIT = 61 << 20


def dot(left, right, left_dim, right_dim):
    return lax.dot_general(
        left, right, (((left_dim,), (right_dim,)), ((), ())), preferred_element_type=f32
    )


def flip(value, bits):
    result = value
    for bit in (1, 2, 4):
        if bits & bit:
            result = result + bit - 2 * bit * ((value // bit) % 2)
    return result


def cross(value, mask):
    low = (value + mask) % 2
    return low + 2 * ((value // 2 + mask // 2) % 2)


def aligned(value, multiple):
    return pl.multiple_of(value, multiple)


class Gather:
    KINDS = 5

    def __init__(self, sources, places, send_z, recv_z, send_x, recv_x, send_c, recv_c):
        self.dp, self.mp = lax.axis_index("dp"), lax.axis_index("mp")
        self.core = self.dp % 2
        self.chip = (self.dp // 2) % 4
        self.sources, self.places = sources, places
        self.sems = (send_z, recv_z, send_x, recv_x, send_c, recv_c)
        self.sends = []

    def part(self, ref, lead, quarter, half):
        rows, columns = ref.shape[-2] // 4, ref.shape[-1] // 2
        window = (
            pl.ds(aligned(quarter * rows, 16), rows),
            pl.ds(aligned(half * columns, 128), columns),
        )
        middle = (slice(None),) * (len(ref.shape) - 2 - len(lead))
        return ref.at[(*lead, *middle, *window)]

    def place(self, kind, shard, quarter, half):
        return self.part(self.places[kind], (shard,), quarter, half)

    def copy(self, source, target, send, recv, dp, mp):
        return pltpu.make_async_remote_copy(
            src_ref=source,
            dst_ref=target,
            send_sem=send,
            recv_sem=recv,
            device_id=(dp, mp),
            device_id_type=MESH,
        )

    def start(self, make, *which):
        make(*which).start()
        self.sends.append((make, which))

    def arrived(self, target, send, recv):
        self.copy(target, target, send, recv, self.dp, self.mp).wait_recv()

    def along_mp(self, kind, k):
        send_z, recv_z = self.sems[:2]
        target = self.place(kind, self.mp, self.chip, self.core)
        source = target
        if self.sources[kind] is not None:
            source = self.part(self.sources[kind], (), self.chip, self.core)
        peer = flip(self.mp, k)
        return self.copy(source, target, send_z.at[kind, k], recv_z.at[kind, k], self.dp, peer)

    def to_core(self, kind, k, j):
        piece = self.place(kind, flip(self.mp, k), flip(self.chip, j), self.core)
        send_c, recv_c = self.sems[4:]
        peer = flip(self.dp, 1)
        return self.copy(piece, piece, send_c.at[kind, k, j], recv_c.at[kind, k, j], peer, self.mp)

    def to_chip(self, kind, k, j):
        send_x, recv_x = self.sems[2:4]
        quarter, peer = self.chip, flip(self.dp, 2 * j)
        if j == 3:
            from_y, from_x = flip(self.chip, 2), flip(self.chip, 1)
            to_x, to_y = flip(self.dp, 2), flip(self.dp, 4)
            quarter = from_y + self.core * (from_x - from_y)
            peer = to_x + self.core * (to_y - to_x)
        piece = self.place(kind, flip(self.mp, k), quarter, self.core)
        return self.copy(piece, piece, send_x.at[kind, k, j], recv_x.at[kind, k, j], peer, self.mp)

    def to_chips(self, kind, k):
        send_z, recv_z = self.sems[:2]
        piece = self.place(kind, flip(self.mp, k), self.chip, self.core)
        self.arrived(piece, send_z.at[kind, k], recv_z.at[kind, k])
        self.start(self.to_chip, kind, k, 1)
        self.start(self.to_chip, kind, k, 2)
        self.start(self.to_core, kind, k, 0)

    def to_corner(self, kind, k):
        send_x, recv_x = self.sems[2:4]
        for j in (1, 2):
            piece = self.place(kind, flip(self.mp, k), flip(self.chip, j), self.core)
            self.arrived(piece, send_x.at[kind, k, j], recv_x.at[kind, k, j])
        self.start(self.to_chip, kind, k, 3)
        self.start(self.to_core, kind, k, 1)
        self.start(self.to_core, kind, k, 2)

    def last_core(self, kind, k):
        send_x, recv_x = self.sems[2:4]
        piece = self.place(kind, flip(self.mp, k), flip(self.chip, 3), self.core)
        self.arrived(piece, send_x.at[kind, k, 3], recv_x.at[kind, k, 3])
        self.start(self.to_core, kind, k, 3)

    def settled(self, kind, k):
        send_c, recv_c = self.sems[4:]
        for j in range(4):
            piece = self.place(kind, flip(self.mp, k), flip(self.chip, j), 1 - self.core)
            self.arrived(piece, send_c.at[kind, k, j], recv_c.at[kind, k, j])

    def schedule(self, jobs, window=8, start=3.0, pace=3.2, lags=(6.0, 12.0, 14.0)):
        for job in jobs[:window]:
            self.start(self.along_mp, *job)

        def first(i):
            self.to_chips(*jobs[i])
            if i + window < len(jobs):
                self.start(self.along_mp, *jobs[i + window])

        steps = []
        clock = start
        for i, job in enumerate(jobs):
            clock += 0.37 * pace if job[0] == 1 else pace
            steps.append((clock, functools.partial(first, i), job, False))
            later = (self.to_corner, self.last_core, self.settled)
            for lag, step in zip(lags, later):
                steps.append((clock + lag, functools.partial(step, *job), job, step == later[-1]))
        return sorted(steps, key=lambda step: step[0])

    def finish(self):
        for make, which in self.sends:
            make(*which).wait_send()


def announce(devices):
    semaphore = pltpu.get_barrier_semaphore()
    for device in devices:
        pl.semaphore_signal(semaphore, inc=1, device_id=device, device_id_type=MESH)
    return semaphore


def row_keep(count, first, rows):
    return lax.broadcasted_iota(jnp.int32, (rows, 1), 0) + first < count


def project(weights_ref, normed_ref, out_ref, shard):
    parts, features, depth = weights_ref.shape[1:]
    rows = normed_ref.shape[0]
    block = 512

    def step(i, _):
        at = pl.ds(aligned(i * block, block), block)
        weights = weights_ref[shard].reshape(parts * features, depth)
        out_ref[shard, :, at] = dot(weights, normed_ref[at, :], 1, 1).astype(bf16)
        return 0

    lax.fori_loop(0, rows // block, step, 0)


def attend(qkv_ref, shard, head, count, probs_ref, context_ref, scale_ref, scores, keys, local_heads, pause):
    rows = qkv_ref.shape[2]
    width = local_heads * HEAD
    block, chunk, group = 256, 128, 64
    at = pl.ds(aligned(head * HEAD, HEAD), HEAD)
    number = shard * local_heads + head
    context_at = pl.ds(aligned(number * HEAD, HEAD), HEAD)
    masked = jnp.where(row_keep(count, 0, rows), 0.0, MASKED)
    first_lane = lax.broadcasted_iota(jnp.int32, (rows, HEAD), 1) == 0
    keys[:, :HEAD] = qkv_ref[shard, pl.ds(aligned(width + head * HEAD, HEAD), HEAD), :].T
    keys[:, HEAD:] = jnp.where(first_lane, masked, 0.0).astype(bf16)
    queries = jnp.concatenate([qkv_ref[shard, at, :], jnp.ones((HEAD, rows), bf16)], axis=0)
    values = qkv_ref[shard, pl.ds(aligned(2 * width + head * HEAD, HEAD), HEAD), :]
    values = jnp.concatenate([values, jnp.ones((16, rows), bf16)], axis=0)
    blocks = rows // block
    highest = None
    for i in range(blocks + 1):
        ahead = None
        for first in range(0, rows, chunk):
            part = slice(first, first + chunk)
            if i < blocks:
                product = dot(keys[part, :], queries[:, i * block : (i + 1) * block], 1, 0)
                scores[i % 2, part, :] = product
                top = jnp.max(product.reshape(chunk // group, group, block), axis=0)
                ahead = top if ahead is None else jnp.maximum(ahead, top)
            if i > 0:
                weights = jnp.exp(scores[(i - 1) % 2, part, :] - highest)
                probs_ref[part, (i - 1) * block : i * block] = weights.astype(bf16)
        if i > 0:
            columns = slice((i - 1) * block, i * block)
            context = dot(values, probs_ref[:, columns], 1, 0)
            scale = 1.0 / context[HEAD : HEAD + 1]
            context_ref[context_at, columns] = (context[:HEAD] * scale).astype(bf16)
            scale_ref[number, :, columns] = scale
        if i < blocks:
            highest = jnp.max(ahead, axis=0, keepdims=True)
            pause(0.4)


def gelu_parts(gate):
    root = 0.7978845608028654
    square = gate * gate
    bend = jnp.tanh(gate * (root + (root * 0.044715) * square))
    half = 0.5 + 0.5 * bend
    slope = half + (0.5 * gate) * (1.0 - bend * bend) * (root + (3 * root * 0.044715) * square)
    return gate * half, slope


def attend_back(qkv_ref, grad_ref, shard, head, probs, context_back, delta, score_back, local_heads):
    rows = qkv_ref.shape[2]
    width = local_heads * HEAD
    block = 256
    head_at = pl.ds(aligned(head * HEAD, HEAD), HEAD)
    key_at = pl.ds(aligned(width + head * HEAD, HEAD), HEAD)
    value_at = pl.ds(aligned(2 * width + head * HEAD, HEAD), HEAD)
    number = shard * local_heads + head
    upstream = context_back[pl.ds(aligned(number * HEAD, HEAD), HEAD), :]
    queries, keys = qkv_ref[shard, head_at, :], qkv_ref[shard, key_at, :]
    high = delta[number].astype(bf16)
    low = (delta[number] - high.astype(f32)).astype(bf16)
    right = jnp.concatenate([upstream, high, low, jnp.zeros((14, rows), bf16)], axis=0)
    lane = lax.broadcasted_iota(jnp.int32, (rows, 16), 1)
    minus = jnp.where(lane < 2, -1.0, 0.0).astype(bf16)
    left = jnp.concatenate([qkv_ref[shard, value_at, :].T, minus], axis=1)
    for first in range(0, rows, block):
        part = slice(first, first + block)
        for i in range(0, rows, block):
            columns = slice(i, i + block)
            change = dot(left[part], right[:, columns], 1, 0)
            score_back[part, columns] = (probs[part, columns].astype(f32) * change).astype(bf16)
        grad_ref[shard, value_at, part] = dot(upstream, probs[part, :], 1, 1).astype(bf16)
        grad_ref[shard, key_at, part] = dot(queries, score_back[part, :], 1, 1).astype(bf16)
    grad_ref[shard, head_at, :] = dot(keys, score_back[...], 1, 0).astype(bf16)


class Reduce:
    def __init__(self, local, from_core, from_chips, total, sems):
        self.local, self.from_core = local, from_core
        self.from_chips, self.total, self.sems = from_chips, total, sems
        self.dp, self.mp = lax.axis_index("dp"), lax.axis_index("mp")
        self.core, self.chip = self.dp % 2, (self.dp // 2) % 4

    def copy(self, j):
        if j == 0:
            source, target, peer = self.local.at[:, 1 - self.core], self.from_core, flip(self.dp, 1)
        else:
            source, target = self.local.at[flip(self.chip, j), self.core], self.from_chips.at[j - 1]
            peer = flip(self.dp, 2 * j)
        return pltpu.make_async_remote_copy(
            src_ref=source,
            dst_ref=target,
            send_sem=self.sems.at[0, j],
            recv_sem=self.sems.at[1, j],
            device_id=(peer, self.mp),
            device_id_type=MESH,
        )

    def begin(self):
        self.copy(0).start()

    def middle(self):
        self.copy(0).wait()
        for j in (1, 2, 3, 0):
            chip = flip(self.chip, j)
            part = self.local[chip, self.core].astype(f32) + self.from_core[chip].astype(f32)
            if j == 0:
                self.total[...] = part
            else:
                self.local[chip, self.core] = part.astype(bf16)
                self.copy(j).start()

    def end(self):
        for j in (1, 2, 3):
            self.copy(j).wait()
        first, second, third = (self.from_chips[i].astype(f32) for i in range(3))
        self.total[...] += first + second + third


def main_kernel(
    extent,
    inputs,
    first_gain,
    second_gain,
    upstream,
    query_source,
    key_source,
    value_source,
    output_source,
    gate_source,
    up_source,
    down_source,
    layer_output,
    probs_out,
    grads_out,
    weights_out,
    hidden_out,
    wide_total,
    narrow_total,
    gains_total,
    attention_weights,
    output_weights,
    gate_weights,
    up_weights,
    down_weights,
    qkv,
    context,
    normed_one,
    normed_two,
    out_low,
    hidden,
    scale,
    delta,
    context_back,
    wide_grad,
    narrow_grad,
    wide_core,
    wide_chips,
    narrow_core,
    narrow_chips,
    gains_own,
    gains_in,
    own_weights,
    local_sem,
    probs_sem,
    out_sem,
    grads_sem,
    wide_sem,
    narrow_sem,
    gains_sem,
    send_z,
    recv_z,
    send_x,
    recv_x,
    send_c,
    recv_c,
):
    dp, mp = lax.axis_index("dp"), lax.axis_index("mp")
    shards = attention_weights.shape[0]
    rows, depth = inputs.shape
    features = output_weights.shape[1]
    units = gate_weights.shape[2]
    local_heads = features // HEAD
    heads = shards * local_heads
    count = extent[0, 0] * extent[0, 1]
    block = 256
    blocks = rows // block

    def each_block(step):
        def run(i, _):
            step(i * block, pl.ds(aligned(i * block, block), block))
            return 0

        lax.fori_loop(0, blocks, run, 0)

    sources = (None, output_source, gate_source, up_source, down_source)
    places = (attention_weights, output_weights, gate_weights, up_weights, down_weights)
    owned = [
        pltpu.make_async_copy(source, place.at[mp], local_sem.at[i])
        for i, (source, place) in enumerate(zip(sources[1:], places[1:]))
    ]
    owned.append(pltpu.make_async_copy(upstream, out_low, local_sem.at[4]))
    turned = [
        pltpu.make_async_copy(source, attention_weights.at[mp, i], local_sem.at[5 + i])
        for i, source in enumerate((query_source, key_source, value_source))
    ]
    peers = [(flip(dp, j), mp) for j in range(1, GROUP)]
    peers += [(dp, flip(mp, k)) for k in range(1, shards)]
    semaphore = announce(peers)
    for copy in turned + owned:
        copy.start()
    for copy in turned:
        copy.wait()
    own_weights[...] = attention_weights[mp].reshape(3 * features, depth).T
    pl.semaphore_wait(semaphore, len(peers))
    gather = Gather(sources, places, send_z, recv_z, send_x, recv_x, send_c, recv_c)
    jobs = [(kind, k) for kind in (0, 1) for k in range(1, shards)]
    jobs += [(kind, k) for k in range(1, shards) for kind in (2, 3, 4)]
    steps = gather.schedule(jobs)
    position = [0]
    clock = [0.0]

    def advance(stop):
        for step in steps[position[0] : stop]:
            step[1]()
        position[0] = max(position[0], stop)

    def pause(spent):
        clock[0] += spent
        advance(sum(step[0] <= clock[0] for step in steps))

    def until(job):
        where = [i for i, step in enumerate(steps) if step[3] and step[2] == job][0]
        clock[0] = max(clock[0], steps[where][0])
        advance(where + 1)

    def gain_of(ref):
        return ref[...].astype(f32).reshape(1, depth)

    def normalise(first, at):
        values = inputs[at, :].astype(f32)
        root = lax.rsqrt(jnp.mean(values * values, axis=-1, keepdims=True) + EPSILON)
        normed_one[at, :] = (values * root * gain_of(first_gain)).astype(bf16)

    each_block(normalise)
    pause(1.5)

    def join(first, at):
        every_output = output_weights[...].reshape(depth, depth)
        values = inputs[at, :].astype(f32) + dot(context[:, at], every_output, 0, 0)
        hidden[at, :] = values
        root = lax.rsqrt(jnp.mean(values * values, axis=-1, keepdims=True) + EPSILON)
        normed_two[at, :] = (values * root * gain_of(second_gain)).astype(bf16)
        out_low[at, :] = jnp.where(row_keep(count, first, block), out_low[at, :], jnp.zeros((), bf16))

    def attention(probs, scores, keys):
        def probs_copy(slot, number):
            return pltpu.make_async_copy(probs.at[slot], probs_out.at[number], probs_sem.at[slot])

        done = 0
        for k in range(shards):
            shard = flip(mp, k)
            if k > 0:
                until((0, k))
            project(attention_weights, normed_one, qkv, shard)
            pause(1.8)
            for head in range(local_heads):
                slot = done % 2
                number = shard * local_heads + head
                if done >= 2:
                    probs_copy(slot, number).wait()
                attend(
                    qkv,
                    shard,
                    head,
                    count,
                    probs.at[slot],
                    context,
                    scale,
                    scores,
                    keys,
                    local_heads,
                    pause,
                )
                probs_copy(slot, number).start()
                done += 1
        pltpu.make_async_copy(attention_weights, weights_out, out_sem.at[0]).start()
        owned[0].wait()
        owned[4].wait()
        for k in range(1, shards):
            until((1, k))
        each_block(join)
        pause(2.4)
        for slot in (done % 2, (done + 1) % 2):
            probs_copy(slot, 0).wait()

    pl.run_scoped(
        attention,
        pltpu.VMEM((2, rows, rows), bf16),
        pltpu.VMEM((2, rows, block), f32),
        pltpu.VMEM((rows, 2 * HEAD), bf16),
    )

    slices = wide_grad.shape[:3]
    wide = Reduce(wide_grad, wide_core, wide_chips, wide_total, wide_sem)
    narrow = Reduce(narrow_grad, narrow_core, narrow_chips, narrow_total, narrow_sem)

    def feed_forward(forward_sum, back_sum, mixed_own, gate_own, up_own):
        def feed(shard, k):
            def step(first, at):
                normed, low = normed_two[at, :], out_low[at, :]
                gate = dot(normed, gate_weights[shard], 1, 0)
                up = dot(normed, up_weights[shard], 1, 0)
                mixed_back = dot(low, down_weights[shard], 1, 1)
                bent, slope = gelu_parts(gate)
                mixed = (bent * up).astype(bf16)
                gate_back = (mixed_back * up * slope).astype(bf16)
                up_back = (mixed_back * bent).astype(bf16)
                ahead = dot(mixed, down_weights[shard], 1, 0)
                back = dot(gate_back, gate_weights[shard], 1, 1)
                back = back + dot(up_back, up_weights[shard], 1, 1)
                if k == 0:
                    mixed_own[at, :] = mixed
                    gate_own[at, :] = gate_back
                    up_own[at, :] = up_back
                    forward_sum[at, :] = ahead
                    back_sum[at, :] = back
                else:
                    forward_sum[at, :] += ahead
                    back_sum[at, :] += back

            for first in range(0, rows, block):
                step(first, slice(first, first + block))
                pause(1.5)

        for k in range(shards):
            if k == 0:
                for copy in owned[1:4]:
                    copy.wait()
            else:
                for kind in (2, 3, 4):
                    until((kind, k))
            if k == shards - 1:
                advance(len(steps))
                wide.middle()
            feed(flip(mp, k), k)
            if k == 0:
                pairs = ((normed_two, gate_own), (normed_two, up_own), (out_low, mixed_own))
                for i, (left, right) in enumerate(pairs):
                    part = dot(left[...], right[...], 0, 0).astype(bf16)
                    wide_grad[:, :, :, i * units : (i + 1) * units] = part.reshape(*slices, units)
                    pause(0.9)
                wide.begin()

        def close(first, at):
            keep = row_keep(count, first, block)
            values, back = hidden[at, :], back_sum[at, :]
            out_back = out_low[at, :].astype(f32)
            out_low[at, :] = jnp.where(keep, values + forward_sum[at, :], 0.0).astype(bf16)
            root = lax.rsqrt(jnp.mean(values * values, axis=-1, keepdims=True) + EPSILON)
            scaled = gain_of(second_gain) * back
            mean = jnp.mean(scaled * values, axis=-1, keepdims=True)
            result = out_back + root * scaled - values * (root * root * root * mean)
            hidden[at, :] = result
            normed_two[at, :] = result.astype(bf16)

        each_block(close)

    pl.run_scoped(
        feed_forward,
        pltpu.VMEM((rows, depth), f32),
        pltpu.VMEM((rows, depth), f32),
        pltpu.VMEM((rows, units), bf16),
        pltpu.VMEM((rows, units), bf16),
        pltpu.VMEM((rows, units), bf16),
    )
    pltpu.make_async_copy(out_low, layer_output, out_sem.at[1]).start()
    pltpu.make_async_copy(hidden, hidden_out, out_sem.at[2]).start()
    hidden_low = normed_two

    def context_step(first, at):
        every_output = output_weights[...].reshape(depth, depth)
        back = dot(every_output, hidden_low[at, :], 1, 1).reshape(heads, HEAD, block)
        low = (back * scale[:, :, at]).astype(bf16)
        context_back[:, at] = low.reshape(depth, block)
        ahead = context[:, at].reshape(heads, HEAD, block).astype(f32)
        delta[:, :, at] = jnp.sum(low.astype(f32) * ahead, axis=1, keepdims=True)

    each_block(context_step)

    def gains_copy(k):
        return pltpu.make_async_remote_copy(
            src_ref=gains_own,
            dst_ref=gains_in.at[k - 1],
            send_sem=gains_sem.at[0, k],
            recv_sem=gains_sem.at[1, k],
            device_id=(dp, flip(mp, k)),
            device_id_type=MESH,
        )

    def gains():
        piece = gains_own.shape[0]
        at = pl.ds(aligned((dp % GROUP) * piece, 32), piece)
        second = gate_weights[mp, at, :].astype(f32) * wide_total[:, :units]
        second = second + up_weights[mp, at, :].astype(f32) * wide_total[:, units : 2 * units]
        first = own_weights[at, :].astype(f32) * narrow_total[:, : 3 * features]
        lane = lax.broadcasted_iota(jnp.int32, gains_own.shape, 1)
        first = jnp.sum(first, axis=1, keepdims=True)
        second = jnp.sum(second, axis=1, keepdims=True)
        gains_own[...] = jnp.where(lane == 0, first, jnp.where(lane == 1, second, 0.0))
        for k in range(1, shards):
            gains_copy(k).start()

    def attention_back(probs, score_back, grads):
        def fetch(i):
            number = cross(mp, i // local_heads) * local_heads + i % local_heads
            return pltpu.make_async_copy(probs_out.at[number], probs.at[i % 2], probs_sem.at[i % 2])

        def keep_grads(shard, k):
            return pltpu.make_async_copy(grads.at[shard], grads_out.at[shard], grads_sem.at[k])

        def step(i, _):
            k, head = i // local_heads, i % local_heads
            shard = cross(mp, k)
            fetch(i).wait()

            @pl.when(i + 1 < heads)
            def _():
                fetch(i + 1).start()

            attend_back(
                qkv,
                grads,
                shard,
                head,
                probs.at[i % 2],
                context_back,
                delta,
                score_back,
                local_heads,
            )

            @pl.when(head == local_heads - 1)
            def _():
                keep_grads(shard, k).start()

            @pl.when(i == local_heads - 1)
            def _():
                own = context[pl.ds(aligned(mp * features, HEAD), features), :]
                part = jnp.concatenate(
                    [dot(grads[mp], normed_one[...], 1, 0), dot(own, hidden_low[...], 1, 0)], axis=0
                )
                narrow_grad[...] = part.T.astype(bf16).reshape(narrow_grad.shape)
                narrow.begin()

            @pl.when(i == local_heads)
            def _():
                narrow.middle()

            @pl.when(i == heads - 5)
            def _():
                wide.end()

            @pl.when(i == heads - 3)
            def _():
                narrow.end()
                gains()

            return 0

        fetch(0).start()
        lax.fori_loop(0, heads, step, 0)
        for k in range(shards):
            keep_grads(flip(mp, k), k).wait()

    pl.run_scoped(
        attention_back,
        pltpu.VMEM((2, rows, rows), bf16),
        pltpu.VMEM((rows, rows), bf16),
        pltpu.VMEM((shards, 3 * features, rows), bf16),
    )
    for k in range(1, shards):
        gains_copy(k).wait()
    gains_total[...] = (gains_own[...] + gains_in[0]) + (gains_in[1] + gains_in[2])
    pltpu.make_async_copy(attention_weights, weights_out, out_sem.at[0]).wait()
    pltpu.make_async_copy(out_low, layer_output, out_sem.at[1]).wait()
    pltpu.make_async_copy(hidden, hidden_out, out_sem.at[2]).wait()
    gather.finish()


def close_kernel(
    grads,
    weights,
    hidden_back,
    inputs,
    first_gain,
    layer_in,
    wide_total,
    narrow_total,
    input_grad,
    layer_output,
    query_grad,
    key_grad,
    value_grad,
    output_grad,
    gate_grad,
    up_grad,
    down_grad,
):
    shards, narrow, block = grads.shape
    depth = inputs.shape[1]
    values = inputs[...].astype(f32)
    every_weight = weights[...].reshape(shards * narrow, depth)
    back = dot(grads[...].reshape(shards * narrow, block), every_weight, 0, 0)
    root = lax.rsqrt(jnp.mean(values * values, axis=-1, keepdims=True) + EPSILON)
    scaled = first_gain[...].astype(f32).reshape(1, depth) * back
    mean = jnp.mean(scaled * values, axis=-1, keepdims=True)
    result = hidden_back[...] + root * scaled
    input_grad[...] = result - values * (root * root * root * mean)
    layer_output[...] = layer_in[...]

    @pl.when(pl.program_id(0) == 0)
    def _():
        features, units = query_grad.shape[1], gate_grad.shape[1]
        query_grad[...] = narrow_total[:, :features]
        key_grad[...] = narrow_total[:, features : 2 * features]
        value_grad[...] = narrow_total[:, 2 * features : 3 * features]
        gate_grad[...] = wide_total[:, :units]
        up_grad[...] = wide_total[:, units : 2 * units]
        down_grad[...] = wide_total[:, 2 * units :]
        output_grad[...] = narrow_total[:, 3 * features :].T


def vmem():
    return pl.BlockSpec(memory_space=pltpu.VMEM)


def anywhere():
    return pl.BlockSpec(memory_space=pl.ANY)


def body(groups, shards, *arguments):
    (
        patches,
        attention_gain,
        query_weight,
        key_weight,
        value_weight,
        output_weight,
        feedforward_gain,
        gate_weight,
        up_weight,
        down_weight,
        cotangent,
        grid_extent,
    ) = arguments
    rows, depth = patches.shape
    features, units = query_weight.shape[1], gate_weight.shape[1]
    heads = shards * features // HEAD
    piece = depth // GROUP
    wide, narrow = 3 * units, 3 * features
    mixed = narrow + features

    shape = jax.ShapeDtypeStruct
    kinds = Gather.KINDS
    dma = pltpu.SemaphoreType.DMA
    (
        layer_output,
        _,
        grads,
        weights,
        hidden_back,
        wide_total,
        narrow_total,
        gains_total,
    ) = pl.pallas_call(
        main_kernel,
        name="layer",
        out_shape=(
            shape((rows, depth), bf16),
            shape((heads, rows, rows), bf16),
            shape((shards, narrow, rows), bf16),
            shape((shards, 3, features, depth), bf16),
            shape((rows, depth), f32),
            shape((piece, wide), f32),
            shape((piece, mixed), f32),
            shape((piece, 128), f32),
        ),
        in_specs=[pl.BlockSpec(memory_space=pltpu.SMEM)] + [vmem()] * 3 + [anywhere()] * 8,
        out_specs=(anywhere(),) * 5 + (vmem(),) * 3,
        scratch_shapes=[
            pltpu.VMEM((shards, 3, features, depth), bf16),
            pltpu.VMEM((shards, features, depth), bf16),
            pltpu.VMEM((shards, depth, units), bf16),
            pltpu.VMEM((shards, depth, units), bf16),
            pltpu.VMEM((shards, units, depth), bf16),
            pltpu.VMEM((shards, narrow, rows), bf16),
            pltpu.VMEM((depth, rows), bf16),
            pltpu.VMEM((rows, depth), bf16),
            pltpu.VMEM((rows, depth), bf16),
            pltpu.VMEM((rows, depth), bf16),
            pltpu.VMEM((rows, depth), f32),
            pltpu.VMEM((heads, 1, rows), f32),
            pltpu.VMEM((heads, 1, rows), f32),
            pltpu.VMEM((depth, rows), bf16),
            pltpu.VMEM((4, 2, piece, wide), bf16),
            pltpu.VMEM((4, 2, piece, mixed), bf16),
            pltpu.VMEM((4, piece, wide), bf16),
            pltpu.VMEM((3, piece, wide), bf16),
            pltpu.VMEM((4, piece, mixed), bf16),
            pltpu.VMEM((3, piece, mixed), bf16),
            pltpu.VMEM((piece, 128), f32),
            pltpu.VMEM((3, piece, 128), f32),
            pltpu.VMEM((depth, narrow), bf16),
            dma((8,)),
            dma((2,)),
            dma((3,)),
            dma((shards,)),
            dma((2, 4)),
            dma((2, 4)),
            dma((2, shards)),
            dma((kinds, shards)),
            dma((kinds, shards)),
            dma((kinds, shards, 4)),
            dma((kinds, shards, 4)),
            dma((kinds, shards, 4)),
            dma((kinds, shards, 4)),
        ],
        compiler_params=pltpu.CompilerParams(
            collective_id=0, has_side_effects=True, vmem_limit_bytes=VMEM_LIMIT
        ),
    )(
        grid_extent,
        patches,
        attention_gain,
        feedforward_gain,
        cotangent,
        query_weight.T,
        key_weight.T,
        value_weight.T,
        output_weight,
        gate_weight,
        up_weight,
        down_weight,
    )

    block = 256

    def whole(*dims):
        return pl.BlockSpec(dims, lambda i: (0,) * len(dims))

    by_rows = pl.BlockSpec((block, depth), lambda i: (i, 0))
    small = [(piece, features)] * 3 + [(features, piece)] + [(piece, units)] * 3
    input_grad, layer_output, *small_grads = pl.pallas_call(
        close_kernel,
        name="close",
        grid=(rows // block,),
        out_shape=[shape((rows, depth), f32), shape((rows, depth), bf16)]
        + [shape(dims, f32) for dims in small],
        in_specs=[
            pl.BlockSpec((shards, narrow, block), lambda i: (0, 0, i)),
            whole(shards, 3, features, depth),
            by_rows,
            by_rows,
            whole(depth),
            by_rows,
            whole(piece, wide),
            whole(piece, mixed),
        ],
        out_specs=[by_rows, by_rows] + [whole(*dims) for dims in small],
        compiler_params=pltpu.CompilerParams(vmem_limit_bytes=VMEM_LIMIT),
    )(grads, weights, hidden_back, patches, attention_gain, layer_output, wide_total, narrow_total)

    index = lax.axis_index("dp")
    gains_total = gains_total[:, :2]
    if groups > 1:

        def spread(block, turned=False):
            block = block.T if turned else block
            whole = jnp.zeros((depth, block.shape[1]), f32)
            whole = lax.dynamic_update_slice(whole, block, ((index % GROUP) * piece, 0))
            own = lax.psum_scatter(whole, "dp", scatter_dimension=0, tiled=True)
            return own.T if turned else own

        small_grads = [spread(grad, i == 3) for i, grad in enumerate(small_grads)]
        gains_total = spread(gains_total)
    kept = depth // (groups * GROUP)

    def gain_grad(column, gain):
        own = lax.dynamic_slice_in_dim(gain.astype(f32), index * kept, kept)
        return gains_total[:, column] / own

    query_grad, key_grad, value_grad, output_grad, gate_grad, up_grad, down_grad = small_grads
    return (
        layer_output,
        input_grad,
        gain_grad(0, attention_gain),
        query_grad,
        key_grad,
        value_grad,
        output_grad,
        gain_grad(1, feedforward_gain),
        gate_grad,
        up_grad,
        down_grad.T,
    )


def solution(mesh):
    placed = (
        P("dp", None),
        P(),
        P(None, "mp"),
        P(None, "mp"),
        P(None, "mp"),
        P("mp", None),
        P(),
        P(None, "mp"),
        P(None, "mp"),
        P("mp", None),
        P("dp", None),
        P("dp", None),
    )
    return jax.shard_map(
        functools.partial(body, mesh.shape["dp"] // GROUP, mesh.shape["mp"]),
        mesh=mesh,
        in_specs=placed,
        out_specs=(
            P("dp", None),
            P("dp", None),
            P("dp"),
            P("dp", "mp"),
            P("dp", "mp"),
            P("dp", "mp"),
            P("mp", "dp"),
            P("dp"),
            P("dp", "mp"),
            P("dp", "mp"),
            P("mp", "dp"),
        ),
        check_vma=False,
    )
```

```python
import functools

import jax
import jax.numpy as jnp
from jax import lax
from jax.experimental import pallas as pl
from jax.experimental.pallas import tpu as pltpu
from jax.sharding import PartitionSpec as P

HEAD = 64
EPSILON = 1e-06
MASKED = -1000000000.0
MESH = pl.DeviceIdType.MESH
f32 = jnp.float32
bf16 = jnp.bfloat16
GROUP = 8
VMEM_LIMIT = 61 << 20


def dot(left, right, left_dim, right_dim):
    return lax.dot_general(
        left, right, (((left_dim,), (right_dim,)), ((), ())), preferred_element_type=f32
    )


def flip(value, bits):
    result = value
    for bit in (1, 2, 4):
        if bits & bit:
            result = result + bit - 2 * bit * ((value // bit) % 2)
    return result


def cross(value, mask):
    low = (value + mask) % 2
    return low + 2 * ((value // 2 + mask // 2) % 2)


def aligned(value, multiple):
    return pl.multiple_of(value, multiple)


class Gather:
    KINDS = 5

    def __init__(self, sources, places, send_z, recv_z, send_x, recv_x, send_c, recv_c):
        self.dp, self.mp = lax.axis_index("dp"), lax.axis_index("mp")
        self.core = self.dp % 2
        self.chip = (self.dp // 2) % 4
        self.sources, self.places = sources, places
        self.sems = (send_z, recv_z, send_x, recv_x, send_c, recv_c)
        self.sends = []

    def part(self, ref, lead, quarter, half):
        rows, columns = ref.shape[-2] // 4, ref.shape[-1] // 2
        window = (
            pl.ds(aligned(quarter * rows, 16), rows),
            pl.ds(aligned(half * columns, 128), columns),
        )
        middle = (slice(None),) * (len(ref.shape) - 2 - len(lead))
        return ref.at[(*lead, *middle, *window)]

    def place(self, kind, shard, quarter, half):
        return self.part(self.places[kind], (shard,), quarter, half)

    def copy(self, source, target, send, recv, dp, mp):
        return pltpu.make_async_remote_copy(
            src_ref=source,
            dst_ref=target,
            send_sem=send,
            recv_sem=recv,
            device_id=(dp, mp),
            device_id_type=MESH,
        )

    def start(self, make, *which):
        make(*which).start()
        self.sends.append((make, which))

    def arrived(self, target, send, recv):
        self.copy(target, target, send, recv, self.dp, self.mp).wait_recv()

    def along_mp(self, kind, k):
        send_z, recv_z = self.sems[:2]
        target = self.place(kind, self.mp, self.chip, self.core)
        source = target
        if self.sources[kind] is not None:
            source = self.part(self.sources[kind], (), self.chip, self.core)
        peer = flip(self.mp, k)
        return self.copy(source, target, send_z.at[kind, k], recv_z.at[kind, k], self.dp, peer)

    def to_core(self, kind, k, j):
        piece = self.place(kind, flip(self.mp, k), flip(self.chip, j), self.core)
        send_c, recv_c = self.sems[4:]
        peer = flip(self.dp, 1)
        return self.copy(piece, piece, send_c.at[kind, k, j], recv_c.at[kind, k, j], peer, self.mp)

    def to_chip(self, kind, k, j):
        send_x, recv_x = self.sems[2:4]
        quarter, peer = self.chip, flip(self.dp, 2 * j)
        if j == 3:
            from_y, from_x = flip(self.chip, 2), flip(self.chip, 1)
            to_x, to_y = flip(self.dp, 2), flip(self.dp, 4)
            quarter = from_y + self.core * (from_x - from_y)
            peer = to_x + self.core * (to_y - to_x)
        piece = self.place(kind, flip(self.mp, k), quarter, self.core)
        return self.copy(piece, piece, send_x.at[kind, k, j], recv_x.at[kind, k, j], peer, self.mp)

    def to_chips(self, kind, k):
        send_z, recv_z = self.sems[:2]
        piece = self.place(kind, flip(self.mp, k), self.chip, self.core)
        self.arrived(piece, send_z.at[kind, k], recv_z.at[kind, k])
        self.start(self.to_chip, kind, k, 1)
        self.start(self.to_chip, kind, k, 2)
        self.start(self.to_core, kind, k, 0)

    def to_corner(self, kind, k):
        send_x, recv_x = self.sems[2:4]
        for j in (1, 2):
            piece = self.place(kind, flip(self.mp, k), flip(self.chip, j), self.core)
            self.arrived(piece, send_x.at[kind, k, j], recv_x.at[kind, k, j])
        self.start(self.to_chip, kind, k, 3)
        self.start(self.to_core, kind, k, 1)
        self.start(self.to_core, kind, k, 2)

    def last_core(self, kind, k):
        send_x, recv_x = self.sems[2:4]
        piece = self.place(kind, flip(self.mp, k), flip(self.chip, 3), self.core)
        self.arrived(piece, send_x.at[kind, k, 3], recv_x.at[kind, k, 3])
        self.start(self.to_core, kind, k, 3)

    def settled(self, kind, k):
        send_c, recv_c = self.sems[4:]
        for j in range(4):
            piece = self.place(kind, flip(self.mp, k), flip(self.chip, j), 1 - self.core)
            self.arrived(piece, send_c.at[kind, k, j], recv_c.at[kind, k, j])

    def schedule(self, jobs, window=8, start=3.0, pace=3.2, lags=(6.0, 12.0, 14.0)):
        for job in jobs[:window]:
            self.start(self.along_mp, *job)

        def first(i):
            self.to_chips(*jobs[i])
            if i + window < len(jobs):
                self.start(self.along_mp, *jobs[i + window])

        steps = []
        clock = start
        for i, job in enumerate(jobs):
            clock += 0.37 * pace if job[0] == 1 else pace
            steps.append((clock, functools.partial(first, i), job, False))
            later = (self.to_corner, self.last_core, self.settled)
            for lag, step in zip(lags, later):
                steps.append((clock + lag, functools.partial(step, *job), job, step == later[-1]))
        return sorted(steps, key=lambda step: step[0])

    def finish(self):
        for make, which in self.sends:
            make(*which).wait_send()


def announce(devices):
    semaphore = pltpu.get_barrier_semaphore()
    for device in devices:
        pl.semaphore_signal(semaphore, inc=1, device_id=device, device_id_type=MESH)
    return semaphore


def row_keep(count, first, rows):
    return lax.broadcasted_iota(jnp.int32, (rows, 1), 0) + first < count


def project(weights_ref, normed_ref, out_ref, shard):
    parts, features, depth = weights_ref.shape[1:]
    rows = normed_ref.shape[0]
    block = 512

    def step(i, _):
        at = pl.ds(aligned(i * block, block), block)
        weights = weights_ref[shard].reshape(parts * features, depth)
        out_ref[shard, :, at] = dot(weights, normed_ref[at, :], 1, 1).astype(bf16)
        return 0

    lax.fori_loop(0, rows // block, step, 0)


def attend(qkv_ref, shard, head, count, probs_ref, context_ref, scale_ref, scores, keys, local_heads, pause):
    rows = qkv_ref.shape[2]
    width = local_heads * HEAD
    block, chunk, group = 256, 128, 64
    at = pl.ds(aligned(head * HEAD, HEAD), HEAD)
    number = shard * local_heads + head
    context_at = pl.ds(aligned(number * HEAD, HEAD), HEAD)
    masked = jnp.where(row_keep(count, 0, rows), 0.0, MASKED)
    first_lane = lax.broadcasted_iota(jnp.int32, (rows, HEAD), 1) == 0
    keys[:, :HEAD] = qkv_ref[shard, pl.ds(aligned(width + head * HEAD, HEAD), HEAD), :].T
    keys[:, HEAD:] = jnp.where(first_lane, masked, 0.0).astype(bf16)
    queries = jnp.concatenate([qkv_ref[shard, at, :], jnp.ones((HEAD, rows), bf16)], axis=0)
    values = qkv_ref[shard, pl.ds(aligned(2 * width + head * HEAD, HEAD), HEAD), :]
    values = jnp.concatenate([values, jnp.ones((16, rows), bf16)], axis=0)
    blocks = rows // block
    highest = None
    for i in range(blocks + 1):
        ahead = None
        for first in range(0, rows, chunk):
            part = slice(first, first + chunk)
            if i < blocks:
                product = dot(keys[part, :], queries[:, i * block : (i + 1) * block], 1, 0)
                scores[i % 2, part, :] = product
                top = jnp.max(product.reshape(chunk // group, group, block), axis=0)
                ahead = top if ahead is None else jnp.maximum(ahead, top)
            if i > 0:
                weights = jnp.exp(scores[(i - 1) % 2, part, :] - highest)
                probs_ref[part, (i - 1) * block : i * block] = weights.astype(bf16)
        if i > 0:
            columns = slice((i - 1) * block, i * block)
            context = dot(values, probs_ref[:, columns], 1, 0)
            scale = 1.0 / context[HEAD : HEAD + 1]
            context_ref[context_at, columns] = (context[:HEAD] * scale).astype(bf16)
            scale_ref[number, :, columns] = scale
        if i < blocks:
            highest = jnp.max(ahead, axis=0, keepdims=True)
            pause(i)


def gelu_parts(gate):
    root = 0.7978845608028654
    square = gate * gate
    bend = jnp.tanh(gate * (root + (root * 0.044715) * square))
    half = 0.5 + 0.5 * bend
    slope = half + (0.5 * gate) * (1.0 - bend * bend) * (root + (3 * root * 0.044715) * square)
    return gate * half, slope


def attend_back(qkv_ref, grad_ref, shard, head, probs, context_back, delta, score_back, local_heads):
    rows = qkv_ref.shape[2]
    width = local_heads * HEAD
    block = 256
    head_at = pl.ds(aligned(head * HEAD, HEAD), HEAD)
    key_at = pl.ds(aligned(width + head * HEAD, HEAD), HEAD)
    value_at = pl.ds(aligned(2 * width + head * HEAD, HEAD), HEAD)
    number = shard * local_heads + head
    upstream = context_back[pl.ds(aligned(number * HEAD, HEAD), HEAD), :]
    queries, keys = qkv_ref[shard, head_at, :], qkv_ref[shard, key_at, :]
    high = delta[number].astype(bf16)
    low = (delta[number] - high.astype(f32)).astype(bf16)
    right = jnp.concatenate([upstream, high, low, jnp.zeros((14, rows), bf16)], axis=0)
    lane = lax.broadcasted_iota(jnp.int32, (rows, 16), 1)
    minus = jnp.where(lane < 2, -1.0, 0.0).astype(bf16)
    left = jnp.concatenate([qkv_ref[shard, value_at, :].T, minus], axis=1)
    for first in range(0, rows, block):
        part = slice(first, first + block)
        for i in range(0, rows, block):
            columns = slice(i, i + block)
            change = dot(left[part], right[:, columns], 1, 0)
            score_back[part, columns] = (probs[part, columns].astype(f32) * change).astype(bf16)
        grad_ref[shard, value_at, part] = dot(upstream, probs[part, :], 1, 1).astype(bf16)
        grad_ref[shard, key_at, part] = dot(queries, score_back[part, :], 1, 1).astype(bf16)
    grad_ref[shard, head_at, :] = dot(keys, score_back[...], 1, 0).astype(bf16)


class Reduce:
    def __init__(self, local, from_core, from_chips, total, sems):
        self.local, self.from_core = local, from_core
        self.from_chips, self.total, self.sems = from_chips, total, sems
        self.dp, self.mp = lax.axis_index("dp"), lax.axis_index("mp")
        self.core, self.chip = self.dp % 2, (self.dp // 2) % 4

    def copy(self, j):
        if j == 0:
            source, target, peer = self.local.at[:, 1 - self.core], self.from_core, flip(self.dp, 1)
        else:
            source, target = self.local.at[flip(self.chip, j), self.core], self.from_chips.at[j - 1]
            peer = flip(self.dp, 2 * j)
        return pltpu.make_async_remote_copy(
            src_ref=source,
            dst_ref=target,
            send_sem=self.sems.at[0, j],
            recv_sem=self.sems.at[1, j],
            device_id=(peer, self.mp),
            device_id_type=MESH,
        )

    def begin(self):
        self.copy(0).start()

    def middle(self):
        self.copy(0).wait()
        for j in (1, 2, 3, 0):
            chip = flip(self.chip, j)
            part = self.local[chip, self.core].astype(f32) + self.from_core[chip].astype(f32)
            if j == 0:
                self.total[...] = part
            else:
                self.local[chip, self.core] = part.astype(bf16)
                self.copy(j).start()

    def end(self):
        for j in (1, 2, 3):
            self.copy(j).wait()
        first, second, third = (self.from_chips[i].astype(f32) for i in range(3))
        self.total[...] += first + second + third


def main_kernel(
    extent,
    inputs,
    first_gain,
    second_gain,
    upstream,
    query_source,
    key_source,
    value_source,
    output_source,
    gate_source,
    up_source,
    down_source,
    layer_output,
    probs_out,
    grads_out,
    weights_out,
    hidden_out,
    wide_total,
    narrow_total,
    gains_total,
    attention_weights,
    output_weights,
    gate_weights,
    up_weights,
    down_weights,
    qkv,
    context,
    normed_one,
    normed_two,
    out_low,
    hidden,
    scale,
    delta,
    context_back,
    wide_grad,
    narrow_grad,
    wide_core,
    wide_chips,
    narrow_core,
    narrow_chips,
    gains_own,
    gains_in,
    own_weights,
    local_sem,
    probs_sem,
    out_sem,
    grads_sem,
    wide_sem,
    narrow_sem,
    gains_sem,
    send_z,
    recv_z,
    send_x,
    recv_x,
    send_c,
    recv_c,
):
    dp, mp = lax.axis_index("dp"), lax.axis_index("mp")
    shards = attention_weights.shape[0]
    rows, depth = inputs.shape
    features = output_weights.shape[1]
    units = gate_weights.shape[2]
    local_heads = features // HEAD
    heads = shards * local_heads
    count = extent[0, 0] * extent[0, 1]
    block = 256
    blocks = rows // block

    def each_block(step):
        def run(i, _):
            step(i * block, pl.ds(aligned(i * block, block), block))
            return 0

        lax.fori_loop(0, blocks, run, 0)

    sources = (None, output_source, gate_source, up_source, down_source)
    places = (attention_weights, output_weights, gate_weights, up_weights, down_weights)
    owned = [
        pltpu.make_async_copy(source, place.at[mp], local_sem.at[i])
        for i, (source, place) in enumerate(zip(sources[1:], places[1:]))
    ]
    owned.append(pltpu.make_async_copy(upstream, out_low, local_sem.at[4]))
    turned = [
        pltpu.make_async_copy(source, attention_weights.at[mp, i], local_sem.at[5 + i])
        for i, source in enumerate((query_source, key_source, value_source))
    ]
    peers = [(flip(dp, j), mp) for j in range(1, GROUP)]
    peers += [(dp, flip(mp, k)) for k in range(1, shards)]
    semaphore = announce(peers)
    for copy in turned + owned:
        copy.start()
    for copy in turned:
        copy.wait()
    own_weights[...] = attention_weights[mp].reshape(3 * features, depth).T
    pl.semaphore_wait(semaphore, len(peers))
    gather = Gather(sources, places, send_z, recv_z, send_x, recv_x, send_c, recv_c)
    jobs = [(kind, k) for kind in (0, 1) for k in range(1, shards)]
    jobs += [(kind, k) for k in range(1, shards) for kind in (2, 3, 4)]
    steps = gather.schedule(jobs)
    position = [0]
    clock = [0.0]

    def take(stop):
        chosen = steps[position[0] : stop]
        position[0] = max(position[0], stop)
        return chosen

    def due(spent):
        clock[0] += spent
        return take(sum(step[0] <= clock[0] for step in steps))

    def needed(job):
        where = [i for i, step in enumerate(steps) if step[3] and step[2] == job][0]
        clock[0] = max(clock[0], steps[where][0])
        return take(where + 1)

    def carry_out(chosen):
        for step in chosen:
            step[1]()

    def carry_out_at(index, plan):
        for number, chosen in plan.items():
            if chosen:
                pl.when(index == number)(functools.partial(carry_out, chosen))

    def gain_of(ref):
        return ref[...].astype(f32).reshape(1, depth)

    def normalise(first, at):
        values = inputs[at, :].astype(f32)
        root = lax.rsqrt(jnp.mean(values * values, axis=-1, keepdims=True) + EPSILON)
        normed_one[at, :] = (values * root * gain_of(first_gain)).astype(bf16)

    each_block(normalise)
    carry_out(due(1.5))

    def join(first, at):
        every_output = output_weights[...].reshape(depth, depth)
        values = inputs[at, :].astype(f32) + dot(context[:, at], every_output, 0, 0)
        hidden[at, :] = values
        root = lax.rsqrt(jnp.mean(values * values, axis=-1, keepdims=True) + EPSILON)
        normed_two[at, :] = (values * root * gain_of(second_gain)).astype(bf16)
        out_low[at, :] = jnp.where(row_keep(count, first, block), out_low[at, :], jnp.zeros((), bf16))

    def attention(probs, scores, keys):
        def probs_copy(slot, number):
            return pltpu.make_async_copy(probs.at[slot], probs_out.at[number], probs_sem.at[slot])

        shard_plan, project_plan, block_plans = {}, {}, [{} for _ in range(blocks)]
        for i in range(heads):
            if i % local_heads == 0:
                shard_plan[i] = needed((0, i // local_heads)) if i > 0 else []
                project_plan[i] = due(1.8)
            for plan in block_plans:
                plan[i] = due(0.4)

        def step(i, _):
            shard, head = cross(mp, i // local_heads), i % local_heads
            number = shard * local_heads + head

            @pl.when(head == 0)
            def _():
                carry_out_at(i, shard_plan)
                project(attention_weights, normed_one, qkv, shard)
                carry_out_at(i, project_plan)

            @pl.when(i >= 2)
            def _():
                probs_copy(i % 2, number).wait()

            attend(
                qkv,
                shard,
                head,
                count,
                probs.at[i % 2],
                context,
                scale,
                scores,
                keys,
                local_heads,
                lambda at: carry_out_at(i, block_plans[at]),
            )
            probs_copy(i % 2, number).start()
            return 0

        lax.fori_loop(0, heads, step, 0)
        pltpu.make_async_copy(attention_weights, weights_out, out_sem.at[0]).start()
        owned[0].wait()
        owned[4].wait()
        for k in range(1, shards):
            carry_out(needed((1, k)))
        each_block(join)
        carry_out(due(2.4))
        for slot in range(2):
            probs_copy(slot, 0).wait()

    pl.run_scoped(
        attention,
        pltpu.VMEM((2, rows, rows), bf16),
        pltpu.VMEM((2, rows, block), f32),
        pltpu.VMEM((rows, 2 * HEAD), bf16),
    )

    slices = wide_grad.shape[:3]
    wide = Reduce(wide_grad, wide_core, wide_chips, wide_total, wide_sem)
    narrow = Reduce(narrow_grad, narrow_core, narrow_chips, narrow_total, narrow_sem)

    def feed_forward(forward_sum, back_sum, mixed_own, gate_own, up_own):
        def feed(shard, k):
            def step(first, at):
                normed, low = normed_two[at, :], out_low[at, :]
                gate = dot(normed, gate_weights[shard], 1, 0)
                up = dot(normed, up_weights[shard], 1, 0)
                mixed_back = dot(low, down_weights[shard], 1, 1)
                bent, slope = gelu_parts(gate)
                mixed = (bent * up).astype(bf16)
                gate_back = (mixed_back * up * slope).astype(bf16)
                up_back = (mixed_back * bent).astype(bf16)
                ahead = dot(mixed, down_weights[shard], 1, 0)
                back = dot(gate_back, gate_weights[shard], 1, 1)
                back = back + dot(up_back, up_weights[shard], 1, 1)
                if k == 0:
                    mixed_own[at, :] = mixed
                    gate_own[at, :] = gate_back
                    up_own[at, :] = up_back
                    forward_sum[at, :] = ahead
                    back_sum[at, :] = back
                else:
                    forward_sum[at, :] += ahead
                    back_sum[at, :] += back

            plan = {i: due(1.5) for i in range(blocks)}

            def run(i, _):
                step(i * block, pl.ds(aligned(i * block, block), block))
                carry_out_at(i, plan)
                return 0

            lax.fori_loop(0, blocks, run, 0)

        for k in range(shards):
            if k == 0:
                for copy in owned[1:4]:
                    copy.wait()
            else:
                for kind in (2, 3, 4):
                    carry_out(needed((kind, k)))
            if k == shards - 1:
                carry_out(take(len(steps)))
                wide.middle()
            feed(flip(mp, k), k)
            if k == 0:
                pairs = ((normed_two, gate_own), (normed_two, up_own), (out_low, mixed_own))
                for i, (left, right) in enumerate(pairs):
                    part = dot(left[...], right[...], 0, 0).astype(bf16)
                    wide_grad[:, :, :, i * units : (i + 1) * units] = part.reshape(*slices, units)
                    carry_out(due(0.9))
                wide.begin()

        def close(first, at):
            keep = row_keep(count, first, block)
            values, back = hidden[at, :], back_sum[at, :]
            out_back = out_low[at, :].astype(f32)
            out_low[at, :] = jnp.where(keep, values + forward_sum[at, :], 0.0).astype(bf16)
            root = lax.rsqrt(jnp.mean(values * values, axis=-1, keepdims=True) + EPSILON)
            scaled = gain_of(second_gain) * back
            mean = jnp.mean(scaled * values, axis=-1, keepdims=True)
            result = out_back + root * scaled - values * (root * root * root * mean)
            hidden[at, :] = result
            normed_two[at, :] = result.astype(bf16)

        each_block(close)

    pl.run_scoped(
        feed_forward,
        pltpu.VMEM((rows, depth), f32),
        pltpu.VMEM((rows, depth), f32),
        pltpu.VMEM((rows, units), bf16),
        pltpu.VMEM((rows, units), bf16),
        pltpu.VMEM((rows, units), bf16),
    )
    pltpu.make_async_copy(out_low, layer_output, out_sem.at[1]).start()
    pltpu.make_async_copy(hidden, hidden_out, out_sem.at[2]).start()
    hidden_low = normed_two

    def context_step(first, at):
        every_output = output_weights[...].reshape(depth, depth)
        back = dot(every_output, hidden_low[at, :], 1, 1).reshape(heads, HEAD, block)
        low = (back * scale[:, :, at]).astype(bf16)
        context_back[:, at] = low.reshape(depth, block)
        ahead = context[:, at].reshape(heads, HEAD, block).astype(f32)
        delta[:, :, at] = jnp.sum(low.astype(f32) * ahead, axis=1, keepdims=True)

    each_block(context_step)

    def gains_copy(k):
        return pltpu.make_async_remote_copy(
            src_ref=gains_own,
            dst_ref=gains_in.at[k - 1],
            send_sem=gains_sem.at[0, k],
            recv_sem=gains_sem.at[1, k],
            device_id=(dp, flip(mp, k)),
            device_id_type=MESH,
        )

    def gains():
        piece = gains_own.shape[0]
        at = pl.ds(aligned((dp % GROUP) * piece, 32), piece)
        second = gate_weights[mp, at, :].astype(f32) * wide_total[:, :units]
        second = second + up_weights[mp, at, :].astype(f32) * wide_total[:, units : 2 * units]
        first = own_weights[at, :].astype(f32) * narrow_total[:, : 3 * features]
        lane = lax.broadcasted_iota(jnp.int32, gains_own.shape, 1)
        first = jnp.sum(first, axis=1, keepdims=True)
        second = jnp.sum(second, axis=1, keepdims=True)
        gains_own[...] = jnp.where(lane == 0, first, jnp.where(lane == 1, second, 0.0))
        for k in range(1, shards):
            gains_copy(k).start()

    def attention_back(probs, score_back, grads):
        def fetch(i):
            number = cross(mp, i // local_heads) * local_heads + i % local_heads
            return pltpu.make_async_copy(probs_out.at[number], probs.at[i % 2], probs_sem.at[i % 2])

        def keep_grads(shard, k):
            return pltpu.make_async_copy(grads.at[shard], grads_out.at[shard], grads_sem.at[k])

        def step(i, _):
            k, head = i // local_heads, i % local_heads
            shard = cross(mp, k)
            fetch(i).wait()

            @pl.when(i + 1 < heads)
            def _():
                fetch(i + 1).start()

            attend_back(
                qkv,
                grads,
                shard,
                head,
                probs.at[i % 2],
                context_back,
                delta,
                score_back,
                local_heads,
            )

            @pl.when(head == local_heads - 1)
            def _():
                keep_grads(shard, k).start()

            @pl.when(i == local_heads - 1)
            def _():
                own = context[pl.ds(aligned(mp * features, HEAD), features), :]
                part = jnp.concatenate(
                    [dot(grads[mp], normed_one[...], 1, 0), dot(own, hidden_low[...], 1, 0)], axis=0
                )
                narrow_grad[...] = part.T.astype(bf16).reshape(narrow_grad.shape)
                narrow.begin()

            @pl.when(i == local_heads)
            def _():
                narrow.middle()

            @pl.when(i == heads - 5)
            def _():
                wide.end()

            @pl.when(i == heads - 3)
            def _():
                narrow.end()
                gains()

            return 0

        fetch(0).start()
        lax.fori_loop(0, heads, step, 0)
        for k in range(shards):
            keep_grads(flip(mp, k), k).wait()

    pl.run_scoped(
        attention_back,
        pltpu.VMEM((2, rows, rows), bf16),
        pltpu.VMEM((rows, rows), bf16),
        pltpu.VMEM((shards, 3 * features, rows), bf16),
    )
    for k in range(1, shards):
        gains_copy(k).wait()
    gains_total[...] = (gains_own[...] + gains_in[0]) + (gains_in[1] + gains_in[2])
    pltpu.make_async_copy(attention_weights, weights_out, out_sem.at[0]).wait()
    pltpu.make_async_copy(out_low, layer_output, out_sem.at[1]).wait()
    pltpu.make_async_copy(hidden, hidden_out, out_sem.at[2]).wait()
    gather.finish()


def close_kernel(
    grads,
    weights,
    hidden_back,
    inputs,
    first_gain,
    layer_in,
    wide_total,
    narrow_total,
    input_grad,
    layer_output,
    query_grad,
    key_grad,
    value_grad,
    output_grad,
    gate_grad,
    up_grad,
    down_grad,
):
    shards, narrow, block = grads.shape
    depth = inputs.shape[1]
    values = inputs[...].astype(f32)
    every_weight = weights[...].reshape(shards * narrow, depth)
    back = dot(grads[...].reshape(shards * narrow, block), every_weight, 0, 0)
    root = lax.rsqrt(jnp.mean(values * values, axis=-1, keepdims=True) + EPSILON)
    scaled = first_gain[...].astype(f32).reshape(1, depth) * back
    mean = jnp.mean(scaled * values, axis=-1, keepdims=True)
    result = hidden_back[...] + root * scaled
    input_grad[...] = result - values * (root * root * root * mean)
    layer_output[...] = layer_in[...]

    @pl.when(pl.program_id(0) == 0)
    def _():
        features, units = query_grad.shape[1], gate_grad.shape[1]
        query_grad[...] = narrow_total[:, :features]
        key_grad[...] = narrow_total[:, features : 2 * features]
        value_grad[...] = narrow_total[:, 2 * features : 3 * features]
        gate_grad[...] = wide_total[:, :units]
        up_grad[...] = wide_total[:, units : 2 * units]
        down_grad[...] = wide_total[:, 2 * units :]
        output_grad[...] = narrow_total[:, 3 * features :].T


def vmem():
    return pl.BlockSpec(memory_space=pltpu.VMEM)


def anywhere():
    return pl.BlockSpec(memory_space=pl.ANY)


def body(groups, shards, *arguments):
    (
        patches,
        attention_gain,
        query_weight,
        key_weight,
        value_weight,
        output_weight,
        feedforward_gain,
        gate_weight,
        up_weight,
        down_weight,
        cotangent,
        grid_extent,
    ) = arguments
    rows, depth = patches.shape
    features, units = query_weight.shape[1], gate_weight.shape[1]
    heads = shards * features // HEAD
    piece = depth // GROUP
    wide, narrow = 3 * units, 3 * features
    mixed = narrow + features

    shape = jax.ShapeDtypeStruct
    kinds = Gather.KINDS
    dma = pltpu.SemaphoreType.DMA
    (
        layer_output,
        _,
        grads,
        weights,
        hidden_back,
        wide_total,
        narrow_total,
        gains_total,
    ) = pl.pallas_call(
        main_kernel,
        name="layer",
        out_shape=(
            shape((rows, depth), bf16),
            shape((heads, rows, rows), bf16),
            shape((shards, narrow, rows), bf16),
            shape((shards, 3, features, depth), bf16),
            shape((rows, depth), f32),
            shape((piece, wide), f32),
            shape((piece, mixed), f32),
            shape((piece, 128), f32),
        ),
        in_specs=[pl.BlockSpec(memory_space=pltpu.SMEM)] + [vmem()] * 3 + [anywhere()] * 8,
        out_specs=(anywhere(),) * 5 + (vmem(),) * 3,
        scratch_shapes=[
            pltpu.VMEM((shards, 3, features, depth), bf16),
            pltpu.VMEM((shards, features, depth), bf16),
            pltpu.VMEM((shards, depth, units), bf16),
            pltpu.VMEM((shards, depth, units), bf16),
            pltpu.VMEM((shards, units, depth), bf16),
            pltpu.VMEM((shards, narrow, rows), bf16),
            pltpu.VMEM((depth, rows), bf16),
            pltpu.VMEM((rows, depth), bf16),
            pltpu.VMEM((rows, depth), bf16),
            pltpu.VMEM((rows, depth), bf16),
            pltpu.VMEM((rows, depth), f32),
            pltpu.VMEM((heads, 1, rows), f32),
            pltpu.VMEM((heads, 1, rows), f32),
            pltpu.VMEM((depth, rows), bf16),
            pltpu.VMEM((4, 2, piece, wide), bf16),
            pltpu.VMEM((4, 2, piece, mixed), bf16),
            pltpu.VMEM((4, piece, wide), bf16),
            pltpu.VMEM((3, piece, wide), bf16),
            pltpu.VMEM((4, piece, mixed), bf16),
            pltpu.VMEM((3, piece, mixed), bf16),
            pltpu.VMEM((piece, 128), f32),
            pltpu.VMEM((3, piece, 128), f32),
            pltpu.VMEM((depth, narrow), bf16),
            dma((8,)),
            dma((2,)),
            dma((3,)),
            dma((shards,)),
            dma((2, 4)),
            dma((2, 4)),
            dma((2, shards)),
            dma((kinds, shards)),
            dma((kinds, shards)),
            dma((kinds, shards, 4)),
            dma((kinds, shards, 4)),
            dma((kinds, shards, 4)),
            dma((kinds, shards, 4)),
        ],
        compiler_params=pltpu.CompilerParams(
            collective_id=0, has_side_effects=True, vmem_limit_bytes=VMEM_LIMIT
        ),
    )(
        grid_extent,
        patches,
        attention_gain,
        feedforward_gain,
        cotangent,
        query_weight.T,
        key_weight.T,
        value_weight.T,
        output_weight,
        gate_weight,
        up_weight,
        down_weight,
    )

    block = 256

    def whole(*dims):
        return pl.BlockSpec(dims, lambda i: (0,) * len(dims))

    by_rows = pl.BlockSpec((block, depth), lambda i: (i, 0))
    small = [(piece, features)] * 3 + [(features, piece)] + [(piece, units)] * 3
    input_grad, layer_output, *small_grads = pl.pallas_call(
        close_kernel,
        name="close",
        grid=(rows // block,),
        out_shape=[shape((rows, depth), f32), shape((rows, depth), bf16)]
        + [shape(dims, f32) for dims in small],
        in_specs=[
            pl.BlockSpec((shards, narrow, block), lambda i: (0, 0, i)),
            whole(shards, 3, features, depth),
            by_rows,
            by_rows,
            whole(depth),
            by_rows,
            whole(piece, wide),
            whole(piece, mixed),
        ],
        out_specs=[by_rows, by_rows] + [whole(*dims) for dims in small],
        compiler_params=pltpu.CompilerParams(vmem_limit_bytes=VMEM_LIMIT),
    )(grads, weights, hidden_back, patches, attention_gain, layer_output, wide_total, narrow_total)

    index = lax.axis_index("dp")
    gains_total = gains_total[:, :2]
    if groups > 1:

        def spread(block, turned=False):
            block = block.T if turned else block
            whole = jnp.zeros((depth, block.shape[1]), f32)
            whole = lax.dynamic_update_slice(whole, block, ((index % GROUP) * piece, 0))
            own = lax.psum_scatter(whole, "dp", scatter_dimension=0, tiled=True)
            return own.T if turned else own

        small_grads = [spread(grad, i == 3) for i, grad in enumerate(small_grads)]
        gains_total = spread(gains_total)
    kept = depth // (groups * GROUP)

    def gain_grad(column, gain):
        own = lax.dynamic_slice_in_dim(gain.astype(f32), index * kept, kept)
        return gains_total[:, column] / own

    query_grad, key_grad, value_grad, output_grad, gate_grad, up_grad, down_grad = small_grads
    return (
        layer_output,
        input_grad,
        gain_grad(0, attention_gain),
        query_grad,
        key_grad,
        value_grad,
        output_grad,
        gain_grad(1, feedforward_gain),
        gate_grad,
        up_grad,
        down_grad.T,
    )


def solution(mesh):
    placed = (
        P("dp", None),
        P(),
        P(None, "mp"),
        P(None, "mp"),
        P(None, "mp"),
        P("mp", None),
        P(),
        P(None, "mp"),
        P(None, "mp"),
        P("mp", None),
        P("dp", None),
        P("dp", None),
    )
    return jax.shard_map(
        functools.partial(body, mesh.shape["dp"] // GROUP, mesh.shape["mp"]),
        mesh=mesh,
        in_specs=placed,
        out_specs=(
            P("dp", None),
            P("dp", None),
            P("dp"),
            P("dp", "mp"),
            P("dp", "mp"),
            P("dp", "mp"),
            P("mp", "dp"),
            P("dp"),
            P("dp", "mp"),
            P("dp", "mp"),
            P("mp", "dp"),
        ),
        check_vma=False,
    )
```

```python
import functools

import jax
import jax.numpy as jnp
from jax import lax
from jax.experimental import pallas as pl
from jax.experimental.pallas import tpu as pltpu
from jax.sharding import PartitionSpec as P

HEAD = 64
EPSILON = 1e-06
MASKED = -1000000000.0
MESH = pl.DeviceIdType.MESH
f32 = jnp.float32
bf16 = jnp.bfloat16
GROUP = 8
VMEM_LIMIT = 61 << 20


def dot(left, right, left_dim, right_dim):
    return lax.dot_general(
        left, right, (((left_dim,), (right_dim,)), ((), ())), preferred_element_type=f32
    )


def flip(value, bits):
    result = value
    for bit in (1, 2, 4):
        if bits & bit:
            result = result + bit - 2 * bit * ((value // bit) % 2)
    return result


def cross(value, mask):
    low = (value + mask) % 2
    return low + 2 * ((value // 2 + mask // 2) % 2)


def aligned(value, multiple):
    return pl.multiple_of(value, multiple)


class Gather:
    KINDS = 5

    def __init__(self, sources, places, send_z, recv_z, send_x, recv_x, send_c, recv_c):
        self.dp, self.mp = lax.axis_index("dp"), lax.axis_index("mp")
        self.core = self.dp % 2
        self.chip = (self.dp // 2) % 4
        self.sources, self.places = sources, places
        self.sems = (send_z, recv_z, send_x, recv_x, send_c, recv_c)
        self.sends = []

    def part(self, ref, lead, quarter, half):
        rows, columns = ref.shape[-2] // 4, ref.shape[-1] // 2
        window = (
            pl.ds(aligned(quarter * rows, 16), rows),
            pl.ds(aligned(half * columns, 128), columns),
        )
        middle = (slice(None),) * (len(ref.shape) - 2 - len(lead))
        return ref.at[(*lead, *middle, *window)]

    def place(self, kind, shard, quarter, half):
        return self.part(self.places[kind], (shard,), quarter, half)

    def copy(self, source, target, send, recv, dp, mp):
        return pltpu.make_async_remote_copy(
            src_ref=source,
            dst_ref=target,
            send_sem=send,
            recv_sem=recv,
            device_id=(dp, mp),
            device_id_type=MESH,
        )

    def start(self, make, *which):
        make(*which).start()
        self.sends.append((make, which))

    def arrived(self, target, send, recv):
        self.copy(target, target, send, recv, self.dp, self.mp).wait_recv()

    def along_mp(self, kind, k):
        send_z, recv_z = self.sems[:2]
        target = self.place(kind, self.mp, self.chip, self.core)
        source = target
        if self.sources[kind] is not None:
            source = self.part(self.sources[kind], (), self.chip, self.core)
        peer = flip(self.mp, k)
        return self.copy(source, target, send_z.at[kind, k], recv_z.at[kind, k], self.dp, peer)

    def to_core(self, kind, k, j):
        piece = self.place(kind, flip(self.mp, k), flip(self.chip, j), self.core)
        send_c, recv_c = self.sems[4:]
        peer = flip(self.dp, 1)
        return self.copy(piece, piece, send_c.at[kind, k, j], recv_c.at[kind, k, j], peer, self.mp)

    def to_chip(self, kind, k, j):
        send_x, recv_x = self.sems[2:4]
        quarter, peer = self.chip, flip(self.dp, 2 * j)
        if j == 3:
            from_y, from_x = flip(self.chip, 2), flip(self.chip, 1)
            to_x, to_y = flip(self.dp, 2), flip(self.dp, 4)
            quarter = from_y + self.core * (from_x - from_y)
            peer = to_x + self.core * (to_y - to_x)
        piece = self.place(kind, flip(self.mp, k), quarter, self.core)
        return self.copy(piece, piece, send_x.at[kind, k, j], recv_x.at[kind, k, j], peer, self.mp)

    def to_chips(self, kind, k):
        send_z, recv_z = self.sems[:2]
        piece = self.place(kind, flip(self.mp, k), self.chip, self.core)
        self.arrived(piece, send_z.at[kind, k], recv_z.at[kind, k])
        self.start(self.to_chip, kind, k, 1)
        self.start(self.to_chip, kind, k, 2)
        self.start(self.to_core, kind, k, 0)

    def to_corner(self, kind, k):
        send_x, recv_x = self.sems[2:4]
        for j in (1, 2):
            piece = self.place(kind, flip(self.mp, k), flip(self.chip, j), self.core)
            self.arrived(piece, send_x.at[kind, k, j], recv_x.at[kind, k, j])
        self.start(self.to_chip, kind, k, 3)
        self.start(self.to_core, kind, k, 1)
        self.start(self.to_core, kind, k, 2)

    def last_core(self, kind, k):
        send_x, recv_x = self.sems[2:4]
        piece = self.place(kind, flip(self.mp, k), flip(self.chip, 3), self.core)
        self.arrived(piece, send_x.at[kind, k, 3], recv_x.at[kind, k, 3])
        self.start(self.to_core, kind, k, 3)

    def settled(self, kind, k):
        send_c, recv_c = self.sems[4:]
        for j in range(4):
            piece = self.place(kind, flip(self.mp, k), flip(self.chip, j), 1 - self.core)
            self.arrived(piece, send_c.at[kind, k, j], recv_c.at[kind, k, j])

    def schedule(self, jobs, window=8, start=3.0, pace=3.0, lags=(6.0, 12.0, 14.0)):
        for job in jobs[:window]:
            self.start(self.along_mp, *job)

        def first(i):
            self.to_chips(*jobs[i])
            if i + window < len(jobs):
                self.start(self.along_mp, *jobs[i + window])

        steps = []
        clock = start
        for i, job in enumerate(jobs):
            clock += 0.37 * pace if job[0] == 1 else pace
            steps.append((clock, functools.partial(first, i), job, False))
            later = (self.to_corner, self.last_core, self.settled)
            for lag, step in zip(lags, later):
                steps.append((clock + lag, functools.partial(step, *job), job, step == later[-1]))
        return sorted(steps, key=lambda step: step[0])

    def finish(self):
        for make, which in self.sends:
            make(*which).wait_send()


def announce(devices):
    semaphore = pltpu.get_barrier_semaphore()
    for device in devices:
        pl.semaphore_signal(semaphore, inc=1, device_id=device, device_id_type=MESH)
    return semaphore


def row_keep(count, first, rows):
    return lax.broadcasted_iota(jnp.int32, (rows, 1), 0) + first < count


def project(weights_ref, normed_ref, out_ref, shard):
    parts, features, depth = weights_ref.shape[1:]
    rows = normed_ref.shape[0]
    block = 512

    def step(i, _):
        at = pl.ds(aligned(i * block, block), block)
        weights = weights_ref[shard].reshape(parts * features, depth)
        out_ref[shard, :, at] = dot(weights, normed_ref[at, :], 1, 1).astype(bf16)
        return 0

    lax.fori_loop(0, rows // block, step, 0)


def attend(qkv_ref, shard, head, count, probs_ref, context_ref, scale_ref, scores, keys, local_heads, pause):
    rows = qkv_ref.shape[2]
    width = local_heads * HEAD
    block, chunk, group = 256, 128, 64
    at = pl.ds(aligned(head * HEAD, HEAD), HEAD)
    number = shard * local_heads + head
    context_at = pl.ds(aligned(number * HEAD, HEAD), HEAD)
    masked = jnp.where(row_keep(count, 0, rows), 0.0, MASKED)
    first_lane = lax.broadcasted_iota(jnp.int32, (rows, HEAD), 1) == 0
    keys[:, :HEAD] = qkv_ref[shard, pl.ds(aligned(width + head * HEAD, HEAD), HEAD), :].T
    keys[:, HEAD:] = jnp.where(first_lane, masked, 0.0).astype(bf16)
    queries = jnp.concatenate([qkv_ref[shard, at, :], jnp.ones((HEAD, rows), bf16)], axis=0)
    values = qkv_ref[shard, pl.ds(aligned(2 * width + head * HEAD, HEAD), HEAD), :]
    values = jnp.concatenate([values, jnp.ones((16, rows), bf16)], axis=0)
    blocks = rows // block
    highest = None
    for i in range(blocks + 1):
        ahead = None
        for first in range(0, rows, chunk):
            part = slice(first, first + chunk)
            if i < blocks:
                product = dot(keys[part, :], queries[:, i * block : (i + 1) * block], 1, 0)
                scores[i % 2, part, :] = product
                top = jnp.max(product.reshape(chunk // group, group, block), axis=0)
                ahead = top if ahead is None else jnp.maximum(ahead, top)
            if i > 0:
                weights = jnp.exp(scores[(i - 1) % 2, part, :] - highest)
                probs_ref[part, (i - 1) * block : i * block] = weights.astype(bf16)
        if i > 0:
            columns = slice((i - 1) * block, i * block)
            context = dot(values, probs_ref[:, columns], 1, 0)
            scale = 1.0 / context[HEAD : HEAD + 1]
            context_ref[context_at, columns] = (context[:HEAD] * scale).astype(bf16)
            scale_ref[number, :, columns] = scale
        if i < blocks:
            highest = jnp.max(ahead, axis=0, keepdims=True)
            pause(i)


def gelu_parts(gate):
    root = 0.7978845608028654
    square = gate * gate
    bend = jnp.tanh(gate * (root + (root * 0.044715) * square))
    half = 0.5 + 0.5 * bend
    slope = half + (0.5 * gate) * (1.0 - bend * bend) * (root + (3 * root * 0.044715) * square)
    return gate * half, slope


def attend_back(qkv_ref, grad_ref, shard, head, probs, context_back, delta, score_back, local_heads):
    rows = qkv_ref.shape[2]
    width = local_heads * HEAD
    block = 256
    head_at = pl.ds(aligned(head * HEAD, HEAD), HEAD)
    key_at = pl.ds(aligned(width + head * HEAD, HEAD), HEAD)
    value_at = pl.ds(aligned(2 * width + head * HEAD, HEAD), HEAD)
    number = shard * local_heads + head
    upstream = context_back[pl.ds(aligned(number * HEAD, HEAD), HEAD), :]
    queries, keys = qkv_ref[shard, head_at, :], qkv_ref[shard, key_at, :]
    high = delta[number].astype(bf16)
    low = (delta[number] - high.astype(f32)).astype(bf16)
    right = jnp.concatenate([upstream, high, low, jnp.zeros((14, rows), bf16)], axis=0)
    lane = lax.broadcasted_iota(jnp.int32, (rows, 16), 1)
    minus = jnp.where(lane < 2, -1.0, 0.0).astype(bf16)
    left = jnp.concatenate([qkv_ref[shard, value_at, :].T, minus], axis=1)
    for first in range(0, rows, block):
        part = slice(first, first + block)
        for i in range(0, rows, block):
            columns = slice(i, i + block)
            change = dot(left[part], right[:, columns], 1, 0)
            score_back[part, columns] = (probs[part, columns].astype(f32) * change).astype(bf16)
        grad_ref[shard, value_at, part] = dot(upstream, probs[part, :], 1, 1).astype(bf16)
        grad_ref[shard, key_at, part] = dot(queries, score_back[part, :], 1, 1).astype(bf16)
    grad_ref[shard, head_at, :] = dot(keys, score_back[...], 1, 0).astype(bf16)


class Reduce:
    def __init__(self, local, from_core, from_chips, total, sems):
        self.local, self.from_core = local, from_core
        self.from_chips, self.total, self.sems = from_chips, total, sems
        self.dp, self.mp = lax.axis_index("dp"), lax.axis_index("mp")
        self.core, self.chip = self.dp % 2, (self.dp // 2) % 4

    def copy(self, j):
        if j == 0:
            source, target, peer = self.local.at[:, 1 - self.core], self.from_core, flip(self.dp, 1)
        else:
            source, target = self.local.at[flip(self.chip, j), self.core], self.from_chips.at[j - 1]
            peer = flip(self.dp, 2 * j)
        return pltpu.make_async_remote_copy(
            src_ref=source,
            dst_ref=target,
            send_sem=self.sems.at[0, j],
            recv_sem=self.sems.at[1, j],
            device_id=(peer, self.mp),
            device_id_type=MESH,
        )

    def begin(self):
        self.copy(0).start()

    def middle(self):
        self.copy(0).wait()
        for j in (1, 2, 3, 0):
            chip = flip(self.chip, j)
            part = self.local[chip, self.core].astype(f32) + self.from_core[chip].astype(f32)
            if j == 0:
                self.total[...] = part
            else:
                self.local[chip, self.core] = part.astype(bf16)
                self.copy(j).start()

    def end(self):
        for j in (1, 2, 3):
            self.copy(j).wait()
        first, second, third = (self.from_chips[i].astype(f32) for i in range(3))
        self.total[...] += first + second + third


def main_kernel(
    extent,
    inputs,
    first_gain,
    second_gain,
    upstream,
    query_source,
    key_source,
    value_source,
    output_source,
    gate_source,
    up_source,
    down_source,
    layer_output,
    probs_out,
    grads_out,
    weights_out,
    hidden_out,
    wide_total,
    narrow_total,
    gains_total,
    attention_weights,
    output_weights,
    gate_weights,
    up_weights,
    down_weights,
    qkv,
    context,
    normed_one,
    normed_two,
    out_low,
    hidden,
    scale,
    delta,
    context_back,
    wide_grad,
    narrow_grad,
    wide_core,
    wide_chips,
    narrow_core,
    narrow_chips,
    gains_own,
    gains_in,
    own_weights,
    local_sem,
    probs_sem,
    out_sem,
    grads_sem,
    wide_sem,
    narrow_sem,
    gains_sem,
    send_z,
    recv_z,
    send_x,
    recv_x,
    send_c,
    recv_c,
):
    dp, mp = lax.axis_index("dp"), lax.axis_index("mp")
    shards = attention_weights.shape[0]
    rows, depth = inputs.shape
    features = output_weights.shape[1]
    units = gate_weights.shape[2]
    local_heads = features // HEAD
    heads = shards * local_heads
    count = extent[0, 0] * extent[0, 1]
    block = 256
    blocks = rows // block

    def each_block(step):
        def run(i, _):
            step(i * block, pl.ds(aligned(i * block, block), block))
            return 0

        lax.fori_loop(0, blocks, run, 0)

    sources = (None, output_source, gate_source, up_source, down_source)
    places = (attention_weights, output_weights, gate_weights, up_weights, down_weights)
    owned = [
        pltpu.make_async_copy(source, place.at[mp], local_sem.at[i])
        for i, (source, place) in enumerate(zip(sources[1:], places[1:]))
    ]
    owned.append(pltpu.make_async_copy(upstream, out_low, local_sem.at[4]))
    turned = [
        pltpu.make_async_copy(source, attention_weights.at[mp, i], local_sem.at[5 + i])
        for i, source in enumerate((query_source, key_source, value_source))
    ]
    peers = [(flip(dp, j), mp) for j in range(1, GROUP)]
    peers += [(dp, flip(mp, k)) for k in range(1, shards)]
    semaphore = announce(peers)
    for copy in turned + owned:
        copy.start()
    for copy in turned:
        copy.wait()
    own_weights[...] = attention_weights[mp].reshape(3 * features, depth).T
    pl.semaphore_wait(semaphore, len(peers))
    gather = Gather(sources, places, send_z, recv_z, send_x, recv_x, send_c, recv_c)
    jobs = [(kind, k) for kind in (0, 1) for k in range(1, shards)]
    jobs += [(kind, k) for k in range(1, shards) for kind in (2, 3, 4)]
    steps = gather.schedule(jobs)
    position = [0]
    clock = [0.0]

    def take(stop):
        chosen = steps[position[0] : stop]
        position[0] = max(position[0], stop)
        return chosen

    def due(spent):
        clock[0] += spent
        return take(sum(step[0] <= clock[0] for step in steps))

    def needed(job):
        where = [i for i, step in enumerate(steps) if step[3] and step[2] == job][0]
        clock[0] = max(clock[0], steps[where][0])
        return take(where + 1)

    def carry_out(chosen):
        for step in chosen:
            step[1]()

    def carry_out_at(index, plan):
        for number, chosen in plan.items():
            if chosen:
                pl.when(index == number)(functools.partial(carry_out, chosen))

    def gain_of(ref):
        return ref[...].astype(f32).reshape(1, depth)

    def normalise(first, at):
        values = inputs[at, :].astype(f32)
        root = lax.rsqrt(jnp.mean(values * values, axis=-1, keepdims=True) + EPSILON)
        normed_one[at, :] = (values * root * gain_of(first_gain)).astype(bf16)

    each_block(normalise)
    carry_out(due(1.5))

    def join(first, at):
        every_output = output_weights[...].reshape(depth, depth)
        values = inputs[at, :].astype(f32) + dot(context[:, at], every_output, 0, 0)
        hidden[at, :] = values
        root = lax.rsqrt(jnp.mean(values * values, axis=-1, keepdims=True) + EPSILON)
        normed_two[at, :] = (values * root * gain_of(second_gain)).astype(bf16)
        out_low[at, :] = jnp.where(row_keep(count, first, block), out_low[at, :], jnp.zeros((), bf16))

    def attention(probs, scores, keys):
        def probs_copy(slot, number):
            return pltpu.make_async_copy(probs.at[slot], probs_out.at[number], probs_sem.at[slot])

        shard_plan, project_plan, block_plans = {}, {}, [{} for _ in range(blocks)]
        for i in range(heads):
            if i % local_heads == 0:
                shard_plan[i] = needed((0, i // local_heads)) if i > 0 else []
                project_plan[i] = due(1.8)
            for plan in block_plans:
                plan[i] = due(0.4)

        def step(i, _):
            shard, head = cross(mp, i // local_heads), i % local_heads
            number = shard * local_heads + head

            @pl.when(head == 0)
            def _():
                carry_out_at(i, shard_plan)
                project(attention_weights, normed_one, qkv, shard)
                carry_out_at(i, project_plan)

            @pl.when(i >= 2)
            def _():
                probs_copy(i % 2, number).wait()

            attend(
                qkv,
                shard,
                head,
                count,
                probs.at[i % 2],
                context,
                scale,
                scores,
                keys,
                local_heads,
                lambda at: carry_out_at(i, block_plans[at]),
            )
            probs_copy(i % 2, number).start()
            return 0

        lax.fori_loop(0, heads, step, 0)
        pltpu.make_async_copy(attention_weights, weights_out, out_sem.at[0]).start()
        owned[0].wait()
        owned[4].wait()
        for k in range(1, shards):
            carry_out(needed((1, k)))
        each_block(join)
        carry_out(due(2.4))
        for slot in range(2):
            probs_copy(slot, 0).wait()

    pl.run_scoped(
        attention,
        pltpu.VMEM((2, rows, rows), bf16),
        pltpu.VMEM((2, rows, block), f32),
        pltpu.VMEM((rows, 2 * HEAD), bf16),
    )

    slices = wide_grad.shape[:3]
    wide = Reduce(wide_grad, wide_core, wide_chips, wide_total, wide_sem)
    narrow = Reduce(narrow_grad, narrow_core, narrow_chips, narrow_total, narrow_sem)

    def feed_forward(forward_sum, back_sum, mixed_own, gate_own, up_own):
        def feed(shard, k):
            def step(first, at):
                normed, low = normed_two[at, :], out_low[at, :]
                gate = dot(normed, gate_weights[shard], 1, 0)
                up = dot(normed, up_weights[shard], 1, 0)
                mixed_back = dot(low, down_weights[shard], 1, 1)
                bent, slope = gelu_parts(gate)
                mixed = (bent * up).astype(bf16)
                gate_back = (mixed_back * up * slope).astype(bf16)
                up_back = (mixed_back * bent).astype(bf16)
                ahead = dot(mixed, down_weights[shard], 1, 0)
                back = dot(gate_back, gate_weights[shard], 1, 1)
                back = back + dot(up_back, up_weights[shard], 1, 1)
                if k == 0:
                    mixed_own[at, :] = mixed
                    gate_own[at, :] = gate_back
                    up_own[at, :] = up_back
                    forward_sum[at, :] = ahead
                    back_sum[at, :] = back
                else:
                    forward_sum[at, :] += ahead
                    back_sum[at, :] += back

            plan = {i: due(1.5) for i in range(blocks)}

            def run(i, _):
                step(i * block, pl.ds(aligned(i * block, block), block))
                carry_out_at(i, plan)
                return 0

            lax.fori_loop(0, blocks, run, 0)

        for k in range(shards):
            if k == 0:
                for copy in owned[1:4]:
                    copy.wait()
            else:
                for kind in (2, 3, 4):
                    carry_out(needed((kind, k)))
            if k == shards - 1:
                carry_out(take(len(steps)))
                wide.middle()
            feed(flip(mp, k), k)
            if k == 0:
                pairs = ((normed_two, gate_own), (normed_two, up_own), (out_low, mixed_own))
                for i, (left, right) in enumerate(pairs):
                    part = dot(left[...], right[...], 0, 0).astype(bf16)
                    wide_grad[:, :, :, i * units : (i + 1) * units] = part.reshape(*slices, units)
                    carry_out(due(0.9))
                wide.begin()

        def close(first, at):
            keep = row_keep(count, first, block)
            values, back = hidden[at, :], back_sum[at, :]
            out_back = out_low[at, :].astype(f32)
            out_low[at, :] = jnp.where(keep, values + forward_sum[at, :], 0.0).astype(bf16)
            root = lax.rsqrt(jnp.mean(values * values, axis=-1, keepdims=True) + EPSILON)
            scaled = gain_of(second_gain) * back
            mean = jnp.mean(scaled * values, axis=-1, keepdims=True)
            result = out_back + root * scaled - values * (root * root * root * mean)
            hidden[at, :] = result
            normed_two[at, :] = result.astype(bf16)

        each_block(close)

    pl.run_scoped(
        feed_forward,
        pltpu.VMEM((rows, depth), f32),
        pltpu.VMEM((rows, depth), f32),
        pltpu.VMEM((rows, units), bf16),
        pltpu.VMEM((rows, units), bf16),
        pltpu.VMEM((rows, units), bf16),
    )
    pltpu.make_async_copy(out_low, layer_output, out_sem.at[1]).start()
    pltpu.make_async_copy(hidden, hidden_out, out_sem.at[2]).start()
    hidden_low = normed_two

    def context_step(first, at):
        every_output = output_weights[...].reshape(depth, depth)
        back = dot(every_output, hidden_low[at, :], 1, 1).reshape(heads, HEAD, block)
        low = (back * scale[:, :, at]).astype(bf16)
        context_back[:, at] = low.reshape(depth, block)
        ahead = context[:, at].reshape(heads, HEAD, block).astype(f32)
        delta[:, :, at] = jnp.sum(low.astype(f32) * ahead, axis=1, keepdims=True)

    each_block(context_step)

    def gains_copy(k):
        return pltpu.make_async_remote_copy(
            src_ref=gains_own,
            dst_ref=gains_in.at[k - 1],
            send_sem=gains_sem.at[0, k],
            recv_sem=gains_sem.at[1, k],
            device_id=(dp, flip(mp, k)),
            device_id_type=MESH,
        )

    def gains():
        piece = gains_own.shape[0]
        at = pl.ds(aligned((dp % GROUP) * piece, 32), piece)
        second = gate_weights[mp, at, :].astype(f32) * wide_total[:, :units]
        second = second + up_weights[mp, at, :].astype(f32) * wide_total[:, units : 2 * units]
        first = own_weights[at, :].astype(f32) * narrow_total[:, : 3 * features]
        lane = lax.broadcasted_iota(jnp.int32, gains_own.shape, 1)
        first = jnp.sum(first, axis=1, keepdims=True)
        second = jnp.sum(second, axis=1, keepdims=True)
        gains_own[...] = jnp.where(lane == 0, first, jnp.where(lane == 1, second, 0.0))
        for k in range(1, shards):
            gains_copy(k).start()

    def attention_back(probs, score_back, grads):
        def fetch(i):
            number = cross(mp, i // local_heads) * local_heads + i % local_heads
            return pltpu.make_async_copy(probs_out.at[number], probs.at[i % 2], probs_sem.at[i % 2])

        def keep_grads(shard, k):
            return pltpu.make_async_copy(grads.at[shard], grads_out.at[shard], grads_sem.at[k])

        def step(i, _):
            k, head = i // local_heads, i % local_heads
            shard = cross(mp, k)
            fetch(i).wait()

            @pl.when(i + 1 < heads)
            def _():
                fetch(i + 1).start()

            attend_back(
                qkv,
                grads,
                shard,
                head,
                probs.at[i % 2],
                context_back,
                delta,
                score_back,
                local_heads,
            )

            @pl.when(head == local_heads - 1)
            def _():
                keep_grads(shard, k).start()

            @pl.when(i == local_heads - 1)
            def _():
                own = context[pl.ds(aligned(mp * features, HEAD), features), :]
                part = jnp.concatenate(
                    [dot(grads[mp], normed_one[...], 1, 0), dot(own, hidden_low[...], 1, 0)], axis=0
                )
                narrow_grad[...] = part.T.astype(bf16).reshape(narrow_grad.shape)
                narrow.begin()

            @pl.when(i == local_heads)
            def _():
                narrow.middle()

            @pl.when(i == heads - 5)
            def _():
                wide.end()

            @pl.when(i == heads - 3)
            def _():
                narrow.end()
                gains()

            return 0

        fetch(0).start()
        lax.fori_loop(0, heads, step, 0)
        for k in range(shards):
            keep_grads(flip(mp, k), k).wait()

    pl.run_scoped(
        attention_back,
        pltpu.VMEM((2, rows, rows), bf16),
        pltpu.VMEM((rows, rows), bf16),
        pltpu.VMEM((shards, 3 * features, rows), bf16),
    )
    for k in range(1, shards):
        gains_copy(k).wait()
    gains_total[...] = (gains_own[...] + gains_in[0]) + (gains_in[1] + gains_in[2])
    pltpu.make_async_copy(attention_weights, weights_out, out_sem.at[0]).wait()
    pltpu.make_async_copy(out_low, layer_output, out_sem.at[1]).wait()
    pltpu.make_async_copy(hidden, hidden_out, out_sem.at[2]).wait()
    gather.finish()


def close_kernel(
    grads,
    weights,
    hidden_back,
    inputs,
    first_gain,
    layer_in,
    wide_total,
    narrow_total,
    input_grad,
    layer_output,
    query_grad,
    key_grad,
    value_grad,
    output_grad,
    gate_grad,
    up_grad,
    down_grad,
):
    shards, narrow, block = grads.shape
    depth = inputs.shape[1]
    values = inputs[...].astype(f32)
    every_weight = weights[...].reshape(shards * narrow, depth)
    back = dot(grads[...].reshape(shards * narrow, block), every_weight, 0, 0)
    root = lax.rsqrt(jnp.mean(values * values, axis=-1, keepdims=True) + EPSILON)
    scaled = first_gain[...].astype(f32).reshape(1, depth) * back
    mean = jnp.mean(scaled * values, axis=-1, keepdims=True)
    result = hidden_back[...] + root * scaled
    input_grad[...] = result - values * (root * root * root * mean)
    layer_output[...] = layer_in[...]

    @pl.when(pl.program_id(0) == 0)
    def _():
        features, units = query_grad.shape[1], gate_grad.shape[1]
        query_grad[...] = narrow_total[:, :features]
        key_grad[...] = narrow_total[:, features : 2 * features]
        value_grad[...] = narrow_total[:, 2 * features : 3 * features]
        gate_grad[...] = wide_total[:, :units]
        up_grad[...] = wide_total[:, units : 2 * units]
        down_grad[...] = wide_total[:, 2 * units :]
        output_grad[...] = narrow_total[:, 3 * features :].T


def vmem():
    return pl.BlockSpec(memory_space=pltpu.VMEM)


def anywhere():
    return pl.BlockSpec(memory_space=pl.ANY)


def body(groups, shards, *arguments):
    (
        patches,
        attention_gain,
        query_weight,
        key_weight,
        value_weight,
        output_weight,
        feedforward_gain,
        gate_weight,
        up_weight,
        down_weight,
        cotangent,
        grid_extent,
    ) = arguments
    rows, depth = patches.shape
    features, units = query_weight.shape[1], gate_weight.shape[1]
    heads = shards * features // HEAD
    piece = depth // GROUP
    wide, narrow = 3 * units, 3 * features
    mixed = narrow + features

    shape = jax.ShapeDtypeStruct
    kinds = Gather.KINDS
    dma = pltpu.SemaphoreType.DMA
    (
        layer_output,
        _,
        grads,
        weights,
        hidden_back,
        wide_total,
        narrow_total,
        gains_total,
    ) = pl.pallas_call(
        main_kernel,
        name="layer",
        out_shape=(
            shape((rows, depth), bf16),
            shape((heads, rows, rows), bf16),
            shape((shards, narrow, rows), bf16),
            shape((shards, 3, features, depth), bf16),
            shape((rows, depth), f32),
            shape((piece, wide), f32),
            shape((piece, mixed), f32),
            shape((piece, 128), f32),
        ),
        in_specs=[pl.BlockSpec(memory_space=pltpu.SMEM)] + [vmem()] * 3 + [anywhere()] * 8,
        out_specs=(anywhere(),) * 5 + (vmem(),) * 3,
        scratch_shapes=[
            pltpu.VMEM((shards, 3, features, depth), bf16),
            pltpu.VMEM((shards, features, depth), bf16),
            pltpu.VMEM((shards, depth, units), bf16),
            pltpu.VMEM((shards, depth, units), bf16),
            pltpu.VMEM((shards, units, depth), bf16),
            pltpu.VMEM((shards, narrow, rows), bf16),
            pltpu.VMEM((depth, rows), bf16),
            pltpu.VMEM((rows, depth), bf16),
            pltpu.VMEM((rows, depth), bf16),
            pltpu.VMEM((rows, depth), bf16),
            pltpu.VMEM((rows, depth), f32),
            pltpu.VMEM((heads, 1, rows), f32),
            pltpu.VMEM((heads, 1, rows), f32),
            pltpu.VMEM((depth, rows), bf16),
            pltpu.VMEM((4, 2, piece, wide), bf16),
            pltpu.VMEM((4, 2, piece, mixed), bf16),
            pltpu.VMEM((4, piece, wide), bf16),
            pltpu.VMEM((3, piece, wide), bf16),
            pltpu.VMEM((4, piece, mixed), bf16),
            pltpu.VMEM((3, piece, mixed), bf16),
            pltpu.VMEM((piece, 128), f32),
            pltpu.VMEM((3, piece, 128), f32),
            pltpu.VMEM((depth, narrow), bf16),
            dma((8,)),
            dma((2,)),
            dma((3,)),
            dma((shards,)),
            dma((2, 4)),
            dma((2, 4)),
            dma((2, shards)),
            dma((kinds, shards)),
            dma((kinds, shards)),
            dma((kinds, shards, 4)),
            dma((kinds, shards, 4)),
            dma((kinds, shards, 4)),
            dma((kinds, shards, 4)),
        ],
        compiler_params=pltpu.CompilerParams(
            collective_id=0, has_side_effects=True, vmem_limit_bytes=VMEM_LIMIT
        ),
    )(
        grid_extent,
        patches,
        attention_gain,
        feedforward_gain,
        cotangent,
        query_weight.T,
        key_weight.T,
        value_weight.T,
        output_weight,
        gate_weight,
        up_weight,
        down_weight,
    )

    block = 256

    def whole(*dims):
        return pl.BlockSpec(dims, lambda i: (0,) * len(dims))

    by_rows = pl.BlockSpec((block, depth), lambda i: (i, 0))
    small = [(piece, features)] * 3 + [(features, piece)] + [(piece, units)] * 3
    input_grad, layer_output, *small_grads = pl.pallas_call(
        close_kernel,
        name="close",
        grid=(rows // block,),
        out_shape=[shape((rows, depth), f32), shape((rows, depth), bf16)]
        + [shape(dims, f32) for dims in small],
        in_specs=[
            pl.BlockSpec((shards, narrow, block), lambda i: (0, 0, i)),
            whole(shards, 3, features, depth),
            by_rows,
            by_rows,
            whole(depth),
            by_rows,
            whole(piece, wide),
            whole(piece, mixed),
        ],
        out_specs=[by_rows, by_rows] + [whole(*dims) for dims in small],
        compiler_params=pltpu.CompilerParams(vmem_limit_bytes=VMEM_LIMIT),
    )(grads, weights, hidden_back, patches, attention_gain, layer_output, wide_total, narrow_total)

    index = lax.axis_index("dp")
    gains_total = gains_total[:, :2]
    if groups > 1:

        def spread(block, turned=False):
            block = block.T if turned else block
            whole = jnp.zeros((depth, block.shape[1]), f32)
            whole = lax.dynamic_update_slice(whole, block, ((index % GROUP) * piece, 0))
            own = lax.psum_scatter(whole, "dp", scatter_dimension=0, tiled=True)
            return own.T if turned else own

        small_grads = [spread(grad, i == 3) for i, grad in enumerate(small_grads)]
        gains_total = spread(gains_total)
    kept = depth // (groups * GROUP)

    def gain_grad(column, gain):
        own = lax.dynamic_slice_in_dim(gain.astype(f32), index * kept, kept)
        return gains_total[:, column] / own

    query_grad, key_grad, value_grad, output_grad, gate_grad, up_grad, down_grad = small_grads
    return (
        layer_output,
        input_grad,
        gain_grad(0, attention_gain),
        query_grad,
        key_grad,
        value_grad,
        output_grad,
        gain_grad(1, feedforward_gain),
        gate_grad,
        up_grad,
        down_grad.T,
    )


def solution(mesh):
    placed = (
        P("dp", None),
        P(),
        P(None, "mp"),
        P(None, "mp"),
        P(None, "mp"),
        P("mp", None),
        P(),
        P(None, "mp"),
        P(None, "mp"),
        P("mp", None),
        P("dp", None),
        P("dp", None),
    )
    return jax.shard_map(
        functools.partial(body, mesh.shape["dp"] // GROUP, mesh.shape["mp"]),
        mesh=mesh,
        in_specs=placed,
        out_specs=(
            P("dp", None),
            P("dp", None),
            P("dp"),
            P("dp", "mp"),
            P("dp", "mp"),
            P("dp", "mp"),
            P("mp", "dp"),
            P("dp"),
            P("dp", "mp"),
            P("dp", "mp"),
            P("mp", "dp"),
        ),
        check_vma=False,
    )
```

```python
import functools

import jax
import jax.numpy as jnp
from jax import lax
from jax.experimental import pallas as pl
from jax.experimental.pallas import tpu as pltpu
from jax.sharding import PartitionSpec as P

HEAD = 64
EPSILON = 1e-06
MASKED = -1000000000.0
MESH = pl.DeviceIdType.MESH
f32 = jnp.float32
bf16 = jnp.bfloat16
GROUP = 8
VMEM_LIMIT = 61 << 20


def dot(left, right, left_dim, right_dim):
    return lax.dot_general(
        left, right, (((left_dim,), (right_dim,)), ((), ())), preferred_element_type=f32
    )


def flip(value, bits):
    result = value
    for bit in (1, 2, 4):
        if bits & bit:
            result = result + bit - 2 * bit * ((value // bit) % 2)
    return result


def cross(value, mask):
    low = (value + mask) % 2
    return low + 2 * ((value // 2 + mask // 2) % 2)


def aligned(value, multiple):
    return pl.multiple_of(value, multiple)


class Gather:
    KINDS = 5

    def __init__(self, sources, places, send_z, recv_z, send_x, recv_x, send_c, recv_c):
        self.dp, self.mp = lax.axis_index("dp"), lax.axis_index("mp")
        self.core = self.dp % 2
        self.chip = (self.dp // 2) % 4
        self.sources, self.places = sources, places
        self.sems = (send_z, recv_z, send_x, recv_x, send_c, recv_c)
        self.sends = []

    def part(self, ref, lead, quarter, half):
        rows, columns = ref.shape[-2] // 4, ref.shape[-1] // 2
        window = (
            pl.ds(aligned(quarter * rows, 16), rows),
            pl.ds(aligned(half * columns, 128), columns),
        )
        middle = (slice(None),) * (len(ref.shape) - 2 - len(lead))
        return ref.at[(*lead, *middle, *window)]

    def place(self, kind, shard, quarter, half):
        return self.part(self.places[kind], (shard,), quarter, half)

    def copy(self, source, target, send, recv, dp, mp):
        return pltpu.make_async_remote_copy(
            src_ref=source,
            dst_ref=target,
            send_sem=send,
            recv_sem=recv,
            device_id=(dp, mp),
            device_id_type=MESH,
        )

    def start(self, make, *which):
        make(*which).start()
        self.sends.append((make, which))

    def arrived(self, target, send, recv):
        self.copy(target, target, send, recv, self.dp, self.mp).wait_recv()

    def along_mp(self, kind, k):
        send_z, recv_z = self.sems[:2]
        target = self.place(kind, self.mp, self.chip, self.core)
        source = target
        if self.sources[kind] is not None:
            source = self.part(self.sources[kind], (), self.chip, self.core)
        peer = flip(self.mp, k)
        return self.copy(source, target, send_z.at[kind, k], recv_z.at[kind, k], self.dp, peer)

    def to_core(self, kind, k, j):
        piece = self.place(kind, flip(self.mp, k), flip(self.chip, j), self.core)
        send_c, recv_c = self.sems[4:]
        peer = flip(self.dp, 1)
        return self.copy(piece, piece, send_c.at[kind, k, j], recv_c.at[kind, k, j], peer, self.mp)

    def to_chip(self, kind, k, j):
        send_x, recv_x = self.sems[2:4]
        quarter, peer = self.chip, flip(self.dp, 2 * j)
        if j == 3:
            from_y, from_x = flip(self.chip, 2), flip(self.chip, 1)
            to_x, to_y = flip(self.dp, 2), flip(self.dp, 4)
            quarter = from_y + self.core * (from_x - from_y)
            peer = to_x + self.core * (to_y - to_x)
        piece = self.place(kind, flip(self.mp, k), quarter, self.core)
        return self.copy(piece, piece, send_x.at[kind, k, j], recv_x.at[kind, k, j], peer, self.mp)

    def to_chips(self, kind, k):
        send_z, recv_z = self.sems[:2]
        piece = self.place(kind, flip(self.mp, k), self.chip, self.core)
        self.arrived(piece, send_z.at[kind, k], recv_z.at[kind, k])
        self.start(self.to_chip, kind, k, 1)
        self.start(self.to_chip, kind, k, 2)
        self.start(self.to_core, kind, k, 0)

    def to_corner(self, kind, k):
        send_x, recv_x = self.sems[2:4]
        for j in (1, 2):
            piece = self.place(kind, flip(self.mp, k), flip(self.chip, j), self.core)
            self.arrived(piece, send_x.at[kind, k, j], recv_x.at[kind, k, j])
        self.start(self.to_chip, kind, k, 3)
        self.start(self.to_core, kind, k, 1)
        self.start(self.to_core, kind, k, 2)

    def last_core(self, kind, k):
        send_x, recv_x = self.sems[2:4]
        piece = self.place(kind, flip(self.mp, k), flip(self.chip, 3), self.core)
        self.arrived(piece, send_x.at[kind, k, 3], recv_x.at[kind, k, 3])
        self.start(self.to_core, kind, k, 3)

    def settled(self, kind, k):
        send_c, recv_c = self.sems[4:]
        for j in range(4):
            piece = self.place(kind, flip(self.mp, k), flip(self.chip, j), 1 - self.core)
            self.arrived(piece, send_c.at[kind, k, j], recv_c.at[kind, k, j])

    def schedule(self, jobs, window=8, start=3.0, pace=3.0, lags=(6.0, 12.0, 14.0)):
        for job in jobs[:window]:
            self.start(self.along_mp, *job)

        def first(i):
            self.to_chips(*jobs[i])
            if i + window < len(jobs):
                self.start(self.along_mp, *jobs[i + window])

        steps = []
        clock = start
        for i, job in enumerate(jobs):
            clock += 0.37 * pace if job[0] == 1 else pace
            steps.append((clock, functools.partial(first, i), job, False))
            later = (self.to_corner, self.last_core, self.settled)
            for lag, step in zip(lags, later):
                steps.append((clock + lag, functools.partial(step, *job), job, step == later[-1]))
        return sorted(steps, key=lambda step: step[0])

    def finish(self):
        for make, which in self.sends:
            make(*which).wait_send()


def announce(devices):
    semaphore = pltpu.get_barrier_semaphore()
    for device in devices:
        pl.semaphore_signal(semaphore, inc=1, device_id=device, device_id_type=MESH)
    return semaphore


def row_keep(count, first, rows):
    return lax.broadcasted_iota(jnp.int32, (rows, 1), 0) + first < count


def project(weights_ref, normed_ref, out_ref, shard):
    parts, features, depth = weights_ref.shape[1:]
    rows = normed_ref.shape[0]
    block = 1024

    def step(i, _):
        at = pl.ds(aligned(i * block, block), block)
        weights = weights_ref[shard].reshape(parts * features, depth)
        out_ref[shard, :, at] = dot(weights, normed_ref[at, :], 1, 1).astype(bf16)
        return 0

    lax.fori_loop(0, rows // block, step, 0)


def attend(qkv_ref, shard, head, count, probs_ref, context_ref, scale_ref, scores, keys, local_heads, pause):
    rows = qkv_ref.shape[2]
    width = local_heads * HEAD
    block, chunk, group = 256, 128, 64
    at = pl.ds(aligned(head * HEAD, HEAD), HEAD)
    number = shard * local_heads + head
    context_at = pl.ds(aligned(number * HEAD, HEAD), HEAD)
    masked = jnp.where(row_keep(count, 0, rows), 0.0, MASKED)
    first_lane = lax.broadcasted_iota(jnp.int32, (rows, HEAD), 1) == 0
    keys[:, :HEAD] = qkv_ref[shard, pl.ds(aligned(width + head * HEAD, HEAD), HEAD), :].T
    keys[:, HEAD:] = jnp.where(first_lane, masked, 0.0).astype(bf16)
    queries = jnp.concatenate([qkv_ref[shard, at, :], jnp.ones((HEAD, rows), bf16)], axis=0)
    values = qkv_ref[shard, pl.ds(aligned(2 * width + head * HEAD, HEAD), HEAD), :]
    values = jnp.concatenate([values, jnp.ones((16, rows), bf16)], axis=0)
    blocks = rows // block
    highest = None
    for i in range(blocks + 1):
        ahead = None
        for first in range(0, rows, chunk):
            part = slice(first, first + chunk)
            if i < blocks:
                product = dot(keys[part, :], queries[:, i * block : (i + 1) * block], 1, 0)
                scores[i % 2, part, :] = product
                top = jnp.max(product.reshape(chunk // group, group, block), axis=0)
                ahead = top if ahead is None else jnp.maximum(ahead, top)
            if i > 0:
                weights = jnp.exp(scores[(i - 1) % 2, part, :] - highest)
                probs_ref[part, (i - 1) * block : i * block] = weights.astype(bf16)
        if i > 0:
            columns = slice((i - 1) * block, i * block)
            context = dot(values, probs_ref[:, columns], 1, 0)
            scale = 1.0 / context[HEAD : HEAD + 1]
            context_ref[context_at, columns] = (context[:HEAD] * scale).astype(bf16)
            scale_ref[number, :, columns] = scale
        if i < blocks:
            highest = jnp.max(ahead, axis=0, keepdims=True)
            pause(i)


def gelu_parts(gate):
    root = 0.7978845608028654
    square = gate * gate
    bend = jnp.tanh(gate * (root + (root * 0.044715) * square))
    half = 0.5 + 0.5 * bend
    slope = half + (0.5 * gate) * (1.0 - bend * bend) * (root + (3 * root * 0.044715) * square)
    return gate * half, slope


def attend_back(qkv_ref, grad_ref, shard, head, probs, context_back, delta, score_back, local_heads):
    rows = qkv_ref.shape[2]
    width = local_heads * HEAD
    block = 256
    head_at = pl.ds(aligned(head * HEAD, HEAD), HEAD)
    key_at = pl.ds(aligned(width + head * HEAD, HEAD), HEAD)
    value_at = pl.ds(aligned(2 * width + head * HEAD, HEAD), HEAD)
    number = shard * local_heads + head
    upstream = context_back[pl.ds(aligned(number * HEAD, HEAD), HEAD), :]
    queries, keys = qkv_ref[shard, head_at, :], qkv_ref[shard, key_at, :]
    high = delta[number].astype(bf16)
    low = (delta[number] - high.astype(f32)).astype(bf16)
    right = jnp.concatenate([upstream, high, low, jnp.zeros((14, rows), bf16)], axis=0)
    lane = lax.broadcasted_iota(jnp.int32, (rows, 16), 1)
    minus = jnp.where(lane < 2, -1.0, 0.0).astype(bf16)
    left = jnp.concatenate([qkv_ref[shard, value_at, :].T, minus], axis=1)
    for first in range(0, rows, block):
        part = slice(first, first + block)
        for i in range(0, rows, block):
            columns = slice(i, i + block)
            change = dot(left[part], right[:, columns], 1, 0)
            score_back[part, columns] = (probs[part, columns].astype(f32) * change).astype(bf16)
        grad_ref[shard, value_at, part] = dot(upstream, probs[part, :], 1, 1).astype(bf16)
        grad_ref[shard, key_at, part] = dot(queries, score_back[part, :], 1, 1).astype(bf16)
    grad_ref[shard, head_at, :] = dot(keys, score_back[...], 1, 0).astype(bf16)


class Reduce:
    def __init__(self, local, from_core, from_chips, total, sems):
        self.local, self.from_core = local, from_core
        self.from_chips, self.total, self.sems = from_chips, total, sems
        self.dp, self.mp = lax.axis_index("dp"), lax.axis_index("mp")
        self.core, self.chip = self.dp % 2, (self.dp // 2) % 4

    def copy(self, j):
        if j == 0:
            source, target, peer = self.local.at[:, 1 - self.core], self.from_core, flip(self.dp, 1)
        else:
            source, target = self.local.at[flip(self.chip, j), self.core], self.from_chips.at[j - 1]
            peer = flip(self.dp, 2 * j)
        return pltpu.make_async_remote_copy(
            src_ref=source,
            dst_ref=target,
            send_sem=self.sems.at[0, j],
            recv_sem=self.sems.at[1, j],
            device_id=(peer, self.mp),
            device_id_type=MESH,
        )

    def begin(self):
        self.copy(0).start()

    def middle(self):
        self.copy(0).wait()
        for j in (1, 2, 3, 0):
            chip = flip(self.chip, j)
            part = self.local[chip, self.core].astype(f32) + self.from_core[chip].astype(f32)
            if j == 0:
                self.total[...] = part
            else:
                self.local[chip, self.core] = part.astype(bf16)
                self.copy(j).start()

    def end(self):
        for j in (1, 2, 3):
            self.copy(j).wait()
        first, second, third = (self.from_chips[i].astype(f32) for i in range(3))
        self.total[...] += first + second + third


def main_kernel(
    extent,
    inputs,
    first_gain,
    second_gain,
    upstream,
    query_source,
    key_source,
    value_source,
    output_source,
    gate_source,
    up_source,
    down_source,
    layer_output,
    probs_out,
    grads_out,
    weights_out,
    hidden_out,
    wide_total,
    narrow_total,
    gains_total,
    attention_weights,
    output_weights,
    gate_weights,
    up_weights,
    down_weights,
    qkv,
    context,
    normed_one,
    normed_two,
    out_low,
    hidden,
    scale,
    delta,
    context_back,
    wide_grad,
    narrow_grad,
    wide_core,
    wide_chips,
    narrow_core,
    narrow_chips,
    gains_own,
    gains_in,
    own_weights,
    local_sem,
    probs_sem,
    out_sem,
    grads_sem,
    wide_sem,
    narrow_sem,
    gains_sem,
    send_z,
    recv_z,
    send_x,
    recv_x,
    send_c,
    recv_c,
):
    dp, mp = lax.axis_index("dp"), lax.axis_index("mp")
    shards = attention_weights.shape[0]
    rows, depth = inputs.shape
    features = output_weights.shape[1]
    units = gate_weights.shape[2]
    local_heads = features // HEAD
    heads = shards * local_heads
    count = extent[0, 0] * extent[0, 1]
    block = 256
    blocks = rows // block

    def each_block(step):
        def run(i, _):
            step(i * block, pl.ds(aligned(i * block, block), block))
            return 0

        lax.fori_loop(0, blocks, run, 0)

    sources = (None, output_source, gate_source, up_source, down_source)
    places = (attention_weights, output_weights, gate_weights, up_weights, down_weights)
    owned = [
        pltpu.make_async_copy(source, place.at[mp], local_sem.at[i])
        for i, (source, place) in enumerate(zip(sources[1:], places[1:]))
    ]
    owned.append(pltpu.make_async_copy(upstream, out_low, local_sem.at[4]))
    turned = [
        pltpu.make_async_copy(source, attention_weights.at[mp, i], local_sem.at[5 + i])
        for i, source in enumerate((query_source, key_source, value_source))
    ]
    peers = [(flip(dp, j), mp) for j in range(1, GROUP)]
    peers += [(dp, flip(mp, k)) for k in range(1, shards)]
    semaphore = announce(peers)
    for copy in turned + owned:
        copy.start()
    for copy in turned:
        copy.wait()
    own_weights[...] = attention_weights[mp].reshape(3 * features, depth).T
    pl.semaphore_wait(semaphore, len(peers))
    gather = Gather(sources, places, send_z, recv_z, send_x, recv_x, send_c, recv_c)
    jobs = [(kind, k) for kind in (0, 1) for k in range(1, shards)]
    jobs += [(kind, k) for k in range(1, shards) for kind in (2, 3, 4)]
    steps = gather.schedule(jobs)
    position = [0]
    clock = [0.0]

    def take(stop):
        chosen = steps[position[0] : stop]
        position[0] = max(position[0], stop)
        return chosen

    def due(spent):
        clock[0] += spent
        return take(sum(step[0] <= clock[0] for step in steps))

    def needed(job):
        where = [i for i, step in enumerate(steps) if step[3] and step[2] == job][0]
        clock[0] = max(clock[0], steps[where][0])
        return take(where + 1)

    def carry_out(chosen):
        for step in chosen:
            step[1]()

    def carry_out_at(index, plan):
        for number, chosen in plan.items():
            if chosen:
                pl.when(index == number)(functools.partial(carry_out, chosen))

    def gain_of(ref):
        return ref[...].astype(f32).reshape(1, depth)

    def normalise(first, at):
        values = inputs[at, :].astype(f32)
        root = lax.rsqrt(jnp.mean(values * values, axis=-1, keepdims=True) + EPSILON)
        normed_one[at, :] = (values * root * gain_of(first_gain)).astype(bf16)

    each_block(normalise)
    carry_out(due(1.5))

    def join(first, at):
        every_output = output_weights[...].reshape(depth, depth)
        values = inputs[at, :].astype(f32) + dot(context[:, at], every_output, 0, 0)
        hidden[at, :] = values
        root = lax.rsqrt(jnp.mean(values * values, axis=-1, keepdims=True) + EPSILON)
        normed_two[at, :] = (values * root * gain_of(second_gain)).astype(bf16)
        out_low[at, :] = jnp.where(row_keep(count, first, block), out_low[at, :], jnp.zeros((), bf16))

    def attention(probs, scores, keys):
        def probs_copy(slot, number):
            return pltpu.make_async_copy(probs.at[slot], probs_out.at[number], probs_sem.at[slot])

        shard_plan, project_plan, block_plans = {}, {}, [{} for _ in range(blocks)]
        for i in range(heads):
            if i % local_heads == 0:
                shard_plan[i] = needed((0, i // local_heads)) if i > 0 else []
                project_plan[i] = due(1.8)
            for plan in block_plans:
                plan[i] = due(0.4)

        def step(i, _):
            shard, head = cross(mp, i // local_heads), i % local_heads
            number = shard * local_heads + head

            @pl.when(head == 0)
            def _():
                carry_out_at(i, shard_plan)
                project(attention_weights, normed_one, qkv, shard)
                carry_out_at(i, project_plan)

            @pl.when(i >= 2)
            def _():
                probs_copy(i % 2, number).wait()

            attend(
                qkv,
                shard,
                head,
                count,
                probs.at[i % 2],
                context,
                scale,
                scores,
                keys,
                local_heads,
                lambda at: carry_out_at(i, block_plans[at]),
            )
            probs_copy(i % 2, number).start()
            return 0

        lax.fori_loop(0, heads, step, 0)
        pltpu.make_async_copy(attention_weights, weights_out, out_sem.at[0]).start()
        owned[0].wait()
        owned[4].wait()
        for k in range(1, shards):
            carry_out(needed((1, k)))
        each_block(join)
        carry_out(due(2.4))
        for slot in range(2):
            probs_copy(slot, 0).wait()

    pl.run_scoped(
        attention,
        pltpu.VMEM((2, rows, rows), bf16),
        pltpu.VMEM((2, rows, block), f32),
        pltpu.VMEM((rows, 2 * HEAD), bf16),
    )

    slices = wide_grad.shape[:3]
    wide = Reduce(wide_grad, wide_core, wide_chips, wide_total, wide_sem)
    narrow = Reduce(narrow_grad, narrow_core, narrow_chips, narrow_total, narrow_sem)

    def feed_forward(forward_sum, back_sum, mixed_own, gate_own, up_own):
        def feed(shard, k):
            def step(first, at):
                normed, low = normed_two[at, :], out_low[at, :]
                gate = dot(normed, gate_weights[shard], 1, 0)
                up = dot(normed, up_weights[shard], 1, 0)
                mixed_back = dot(low, down_weights[shard], 1, 1)
                bent, slope = gelu_parts(gate)
                mixed = (bent * up).astype(bf16)
                gate_back = (mixed_back * up * slope).astype(bf16)
                up_back = (mixed_back * bent).astype(bf16)
                ahead = dot(mixed, down_weights[shard], 1, 0)
                back = dot(gate_back, gate_weights[shard], 1, 1)
                back = back + dot(up_back, up_weights[shard], 1, 1)
                if k == 0:
                    mixed_own[at, :] = mixed
                    gate_own[at, :] = gate_back
                    up_own[at, :] = up_back
                    forward_sum[at, :] = ahead
                    back_sum[at, :] = back
                else:
                    forward_sum[at, :] += ahead
                    back_sum[at, :] += back

            plan = {i: due(1.5) for i in range(blocks)}

            def run(i, _):
                step(i * block, pl.ds(aligned(i * block, block), block))
                carry_out_at(i, plan)
                return 0

            lax.fori_loop(0, blocks, run, 0)

        for k in range(shards):
            if k == 0:
                for copy in owned[1:4]:
                    copy.wait()
            else:
                for kind in (2, 3, 4):
                    carry_out(needed((kind, k)))
            if k == shards - 1:
                carry_out(take(len(steps)))
                wide.middle()
            feed(flip(mp, k), k)
            if k == 0:
                pairs = ((normed_two, gate_own), (normed_two, up_own), (out_low, mixed_own))
                for i, (left, right) in enumerate(pairs):
                    part = dot(left[...], right[...], 0, 0).astype(bf16)
                    wide_grad[:, :, :, i * units : (i + 1) * units] = part.reshape(*slices, units)
                    carry_out(due(0.9))
                wide.begin()

        def close(first, at):
            keep = row_keep(count, first, block)
            values, back = hidden[at, :], back_sum[at, :]
            out_back = out_low[at, :].astype(f32)
            out_low[at, :] = jnp.where(keep, values + forward_sum[at, :], 0.0).astype(bf16)
            root = lax.rsqrt(jnp.mean(values * values, axis=-1, keepdims=True) + EPSILON)
            scaled = gain_of(second_gain) * back
            mean = jnp.mean(scaled * values, axis=-1, keepdims=True)
            result = out_back + root * scaled - values * (root * root * root * mean)
            hidden[at, :] = result
            normed_two[at, :] = result.astype(bf16)

        each_block(close)

    pl.run_scoped(
        feed_forward,
        pltpu.VMEM((rows, depth), f32),
        pltpu.VMEM((rows, depth), f32),
        pltpu.VMEM((rows, units), bf16),
        pltpu.VMEM((rows, units), bf16),
        pltpu.VMEM((rows, units), bf16),
    )
    pltpu.make_async_copy(out_low, layer_output, out_sem.at[1]).start()
    pltpu.make_async_copy(hidden, hidden_out, out_sem.at[2]).start()
    hidden_low = normed_two

    def context_step(first, at):
        every_output = output_weights[...].reshape(depth, depth)
        back = dot(every_output, hidden_low[at, :], 1, 1).reshape(heads, HEAD, block)
        low = (back * scale[:, :, at]).astype(bf16)
        context_back[:, at] = low.reshape(depth, block)
        ahead = context[:, at].reshape(heads, HEAD, block).astype(f32)
        delta[:, :, at] = jnp.sum(low.astype(f32) * ahead, axis=1, keepdims=True)

    each_block(context_step)

    def gains_copy(k):
        return pltpu.make_async_remote_copy(
            src_ref=gains_own,
            dst_ref=gains_in.at[k - 1],
            send_sem=gains_sem.at[0, k],
            recv_sem=gains_sem.at[1, k],
            device_id=(dp, flip(mp, k)),
            device_id_type=MESH,
        )

    def gains():
        piece = gains_own.shape[0]
        at = pl.ds(aligned((dp % GROUP) * piece, 32), piece)
        second = gate_weights[mp, at, :].astype(f32) * wide_total[:, :units]
        second = second + up_weights[mp, at, :].astype(f32) * wide_total[:, units : 2 * units]
        first = own_weights[at, :].astype(f32) * narrow_total[:, : 3 * features]
        lane = lax.broadcasted_iota(jnp.int32, gains_own.shape, 1)
        first = jnp.sum(first, axis=1, keepdims=True)
        second = jnp.sum(second, axis=1, keepdims=True)
        gains_own[...] = jnp.where(lane == 0, first, jnp.where(lane == 1, second, 0.0))
        for k in range(1, shards):
            gains_copy(k).start()

    def attention_back(probs, score_back, grads):
        def fetch(i):
            number = cross(mp, i // local_heads) * local_heads + i % local_heads
            return pltpu.make_async_copy(probs_out.at[number], probs.at[i % 2], probs_sem.at[i % 2])

        def keep_grads(shard, k):
            return pltpu.make_async_copy(grads.at[shard], grads_out.at[shard], grads_sem.at[k])

        def step(i, _):
            k, head = i // local_heads, i % local_heads
            shard = cross(mp, k)
            fetch(i).wait()

            @pl.when(i + 1 < heads)
            def _():
                fetch(i + 1).start()

            attend_back(
                qkv,
                grads,
                shard,
                head,
                probs.at[i % 2],
                context_back,
                delta,
                score_back,
                local_heads,
            )

            @pl.when(head == local_heads - 1)
            def _():
                keep_grads(shard, k).start()

            @pl.when(i == local_heads - 1)
            def _():
                own = context[pl.ds(aligned(mp * features, HEAD), features), :]
                part = jnp.concatenate(
                    [dot(grads[mp], normed_one[...], 1, 0), dot(own, hidden_low[...], 1, 0)], axis=0
                )
                narrow_grad[...] = part.T.astype(bf16).reshape(narrow_grad.shape)
                narrow.begin()

            @pl.when(i == local_heads)
            def _():
                narrow.middle()

            @pl.when(i == heads - 5)
            def _():
                wide.end()

            @pl.when(i == heads - 3)
            def _():
                narrow.end()
                gains()

            return 0

        fetch(0).start()
        lax.fori_loop(0, heads, step, 0)
        for k in range(shards):
            keep_grads(flip(mp, k), k).wait()

    pl.run_scoped(
        attention_back,
        pltpu.VMEM((2, rows, rows), bf16),
        pltpu.VMEM((rows, rows), bf16),
        pltpu.VMEM((shards, 3 * features, rows), bf16),
    )
    for k in range(1, shards):
        gains_copy(k).wait()
    gains_total[...] = (gains_own[...] + gains_in[0]) + (gains_in[1] + gains_in[2])
    pltpu.make_async_copy(attention_weights, weights_out, out_sem.at[0]).wait()
    pltpu.make_async_copy(out_low, layer_output, out_sem.at[1]).wait()
    pltpu.make_async_copy(hidden, hidden_out, out_sem.at[2]).wait()
    gather.finish()


def close_kernel(
    grads,
    weights,
    hidden_back,
    inputs,
    first_gain,
    layer_in,
    wide_total,
    narrow_total,
    input_grad,
    layer_output,
    query_grad,
    key_grad,
    value_grad,
    output_grad,
    gate_grad,
    up_grad,
    down_grad,
):
    shards, narrow, block = grads.shape
    depth = inputs.shape[1]
    values = inputs[...].astype(f32)
    every_weight = weights[...].reshape(shards * narrow, depth)
    back = dot(grads[...].reshape(shards * narrow, block), every_weight, 0, 0)
    root = lax.rsqrt(jnp.mean(values * values, axis=-1, keepdims=True) + EPSILON)
    scaled = first_gain[...].astype(f32).reshape(1, depth) * back
    mean = jnp.mean(scaled * values, axis=-1, keepdims=True)
    result = hidden_back[...] + root * scaled
    input_grad[...] = result - values * (root * root * root * mean)
    layer_output[...] = layer_in[...]

    @pl.when(pl.program_id(0) == 0)
    def _():
        features, units = query_grad.shape[1], gate_grad.shape[1]
        query_grad[...] = narrow_total[:, :features]
        key_grad[...] = narrow_total[:, features : 2 * features]
        value_grad[...] = narrow_total[:, 2 * features : 3 * features]
        gate_grad[...] = wide_total[:, :units]
        up_grad[...] = wide_total[:, units : 2 * units]
        down_grad[...] = wide_total[:, 2 * units :]
        output_grad[...] = narrow_total[:, 3 * features :].T


def vmem():
    return pl.BlockSpec(memory_space=pltpu.VMEM)


def anywhere():
    return pl.BlockSpec(memory_space=pl.ANY)


def body(groups, shards, *arguments):
    (
        patches,
        attention_gain,
        query_weight,
        key_weight,
        value_weight,
        output_weight,
        feedforward_gain,
        gate_weight,
        up_weight,
        down_weight,
        cotangent,
        grid_extent,
    ) = arguments
    rows, depth = patches.shape
    features, units = query_weight.shape[1], gate_weight.shape[1]
    heads = shards * features // HEAD
    piece = depth // GROUP
    wide, narrow = 3 * units, 3 * features
    mixed = narrow + features

    shape = jax.ShapeDtypeStruct
    kinds = Gather.KINDS
    dma = pltpu.SemaphoreType.DMA
    (
        layer_output,
        _,
        grads,
        weights,
        hidden_back,
        wide_total,
        narrow_total,
        gains_total,
    ) = pl.pallas_call(
        main_kernel,
        name="layer",
        out_shape=(
            shape((rows, depth), bf16),
            shape((heads, rows, rows), bf16),
            shape((shards, narrow, rows), bf16),
            shape((shards, 3, features, depth), bf16),
            shape((rows, depth), f32),
            shape((piece, wide), f32),
            shape((piece, mixed), f32),
            shape((piece, 128), f32),
        ),
        in_specs=[pl.BlockSpec(memory_space=pltpu.SMEM)] + [vmem()] * 3 + [anywhere()] * 8,
        out_specs=(anywhere(),) * 5 + (vmem(),) * 3,
        scratch_shapes=[
            pltpu.VMEM((shards, 3, features, depth), bf16),
            pltpu.VMEM((shards, features, depth), bf16),
            pltpu.VMEM((shards, depth, units), bf16),
            pltpu.VMEM((shards, depth, units), bf16),
            pltpu.VMEM((shards, units, depth), bf16),
            pltpu.VMEM((shards, narrow, rows), bf16),
            pltpu.VMEM((depth, rows), bf16),
            pltpu.VMEM((rows, depth), bf16),
            pltpu.VMEM((rows, depth), bf16),
            pltpu.VMEM((rows, depth), bf16),
            pltpu.VMEM((rows, depth), f32),
            pltpu.VMEM((heads, 1, rows), f32),
            pltpu.VMEM((heads, 1, rows), f32),
            pltpu.VMEM((depth, rows), bf16),
            pltpu.VMEM((4, 2, piece, wide), bf16),
            pltpu.VMEM((4, 2, piece, mixed), bf16),
            pltpu.VMEM((4, piece, wide), bf16),
            pltpu.VMEM((3, piece, wide), bf16),
            pltpu.VMEM((4, piece, mixed), bf16),
            pltpu.VMEM((3, piece, mixed), bf16),
            pltpu.VMEM((piece, 128), f32),
            pltpu.VMEM((3, piece, 128), f32),
            pltpu.VMEM((depth, narrow), bf16),
            dma((8,)),
            dma((2,)),
            dma((3,)),
            dma((shards,)),
            dma((2, 4)),
            dma((2, 4)),
            dma((2, shards)),
            dma((kinds, shards)),
            dma((kinds, shards)),
            dma((kinds, shards, 4)),
            dma((kinds, shards, 4)),
            dma((kinds, shards, 4)),
            dma((kinds, shards, 4)),
        ],
        compiler_params=pltpu.CompilerParams(
            collective_id=0, has_side_effects=True, vmem_limit_bytes=VMEM_LIMIT
        ),
    )(
        grid_extent,
        patches,
        attention_gain,
        feedforward_gain,
        cotangent,
        query_weight.T,
        key_weight.T,
        value_weight.T,
        output_weight,
        gate_weight,
        up_weight,
        down_weight,
    )

    block = 256

    def whole(*dims):
        return pl.BlockSpec(dims, lambda i: (0,) * len(dims))

    by_rows = pl.BlockSpec((block, depth), lambda i: (i, 0))
    small = [(piece, features)] * 3 + [(features, piece)] + [(piece, units)] * 3
    input_grad, layer_output, *small_grads = pl.pallas_call(
        close_kernel,
        name="close",
        grid=(rows // block,),
        out_shape=[shape((rows, depth), f32), shape((rows, depth), bf16)]
        + [shape(dims, f32) for dims in small],
        in_specs=[
            pl.BlockSpec((shards, narrow, block), lambda i: (0, 0, i)),
            whole(shards, 3, features, depth),
            by_rows,
            by_rows,
            whole(depth),
            by_rows,
            whole(piece, wide),
            whole(piece, mixed),
        ],
        out_specs=[by_rows, by_rows] + [whole(*dims) for dims in small],
        compiler_params=pltpu.CompilerParams(vmem_limit_bytes=VMEM_LIMIT),
    )(grads, weights, hidden_back, patches, attention_gain, layer_output, wide_total, narrow_total)

    index = lax.axis_index("dp")
    gains_total = gains_total[:, :2]
    if groups > 1:

        def spread(block, turned=False):
            block = block.T if turned else block
            whole = jnp.zeros((depth, block.shape[1]), f32)
            whole = lax.dynamic_update_slice(whole, block, ((index % GROUP) * piece, 0))
            own = lax.psum_scatter(whole, "dp", scatter_dimension=0, tiled=True)
            return own.T if turned else own

        small_grads = [spread(grad, i == 3) for i, grad in enumerate(small_grads)]
        gains_total = spread(gains_total)
    kept = depth // (groups * GROUP)

    def gain_grad(column, gain):
        own = lax.dynamic_slice_in_dim(gain.astype(f32), index * kept, kept)
        return gains_total[:, column] / own

    query_grad, key_grad, value_grad, output_grad, gate_grad, up_grad, down_grad = small_grads
    return (
        layer_output,
        input_grad,
        gain_grad(0, attention_gain),
        query_grad,
        key_grad,
        value_grad,
        output_grad,
        gain_grad(1, feedforward_gain),
        gate_grad,
        up_grad,
        down_grad.T,
    )


def solution(mesh):
    placed = (
        P("dp", None),
        P(),
        P(None, "mp"),
        P(None, "mp"),
        P(None, "mp"),
        P("mp", None),
        P(),
        P(None, "mp"),
        P(None, "mp"),
        P("mp", None),
        P("dp", None),
        P("dp", None),
    )
    return jax.shard_map(
        functools.partial(body, mesh.shape["dp"] // GROUP, mesh.shape["mp"]),
        mesh=mesh,
        in_specs=placed,
        out_specs=(
            P("dp", None),
            P("dp", None),
            P("dp"),
            P("dp", "mp"),
            P("dp", "mp"),
            P("dp", "mp"),
            P("mp", "dp"),
            P("dp"),
            P("dp", "mp"),
            P("dp", "mp"),
            P("mp", "dp"),
        ),
        check_vma=False,
    )
```

```python
import functools

import jax
import jax.numpy as jnp
from jax import lax
from jax.experimental import pallas as pl
from jax.experimental.pallas import tpu as pltpu
from jax.sharding import PartitionSpec as P

HEAD = 64
EPSILON = 1e-06
MASKED = -1000000000.0
MESH = pl.DeviceIdType.MESH
f32 = jnp.float32
bf16 = jnp.bfloat16
GROUP = 8
VMEM_LIMIT = 61 << 20


def dot(left, right, left_dim, right_dim):
    return lax.dot_general(
        left, right, (((left_dim,), (right_dim,)), ((), ())), preferred_element_type=f32
    )


def flip(value, bits):
    result = value
    for bit in (1, 2, 4):
        if bits & bit:
            result = result + bit - 2 * bit * ((value // bit) % 2)
    return result


def cross(value, mask):
    low = (value + mask) % 2
    return low + 2 * ((value // 2 + mask // 2) % 2)


def aligned(value, multiple):
    return pl.multiple_of(value, multiple)


class Gather:
    KINDS = 5

    def __init__(self, sources, places, send_z, recv_z, send_x, recv_x, send_c, recv_c):
        self.dp, self.mp = lax.axis_index("dp"), lax.axis_index("mp")
        self.core = self.dp % 2
        self.chip = (self.dp // 2) % 4
        self.sources, self.places = sources, places
        self.sems = (send_z, recv_z, send_x, recv_x, send_c, recv_c)
        self.sends = []

    def part(self, ref, lead, quarter, half):
        rows, columns = ref.shape[-2] // 4, ref.shape[-1] // 2
        window = (
            pl.ds(aligned(quarter * rows, 16), rows),
            pl.ds(aligned(half * columns, 128), columns),
        )
        middle = (slice(None),) * (len(ref.shape) - 2 - len(lead))
        return ref.at[(*lead, *middle, *window)]

    def place(self, kind, shard, quarter, half):
        return self.part(self.places[kind], (shard,), quarter, half)

    def copy(self, source, target, send, recv, dp, mp):
        return pltpu.make_async_remote_copy(
            src_ref=source,
            dst_ref=target,
            send_sem=send,
            recv_sem=recv,
            device_id=(dp, mp),
            device_id_type=MESH,
        )

    def start(self, make, *which):
        make(*which).start()
        self.sends.append((make, which))

    def arrived(self, target, send, recv):
        self.copy(target, target, send, recv, self.dp, self.mp).wait_recv()

    def along_mp(self, kind, k):
        send_z, recv_z = self.sems[:2]
        target = self.place(kind, self.mp, self.chip, self.core)
        source = target
        if self.sources[kind] is not None:
            source = self.part(self.sources[kind], (), self.chip, self.core)
        peer = flip(self.mp, k)
        return self.copy(source, target, send_z.at[kind, k], recv_z.at[kind, k], self.dp, peer)

    def to_core(self, kind, k, j):
        piece = self.place(kind, flip(self.mp, k), flip(self.chip, j), self.core)
        send_c, recv_c = self.sems[4:]
        peer = flip(self.dp, 1)
        return self.copy(piece, piece, send_c.at[kind, k, j], recv_c.at[kind, k, j], peer, self.mp)

    def to_chip(self, kind, k, j):
        send_x, recv_x = self.sems[2:4]
        quarter, peer = self.chip, flip(self.dp, 2 * j)
        if j == 3:
            from_y, from_x = flip(self.chip, 2), flip(self.chip, 1)
            to_x, to_y = flip(self.dp, 2), flip(self.dp, 4)
            quarter = from_y + self.core * (from_x - from_y)
            peer = to_x + self.core * (to_y - to_x)
        piece = self.place(kind, flip(self.mp, k), quarter, self.core)
        return self.copy(piece, piece, send_x.at[kind, k, j], recv_x.at[kind, k, j], peer, self.mp)

    def to_chips(self, kind, k):
        send_z, recv_z = self.sems[:2]
        piece = self.place(kind, flip(self.mp, k), self.chip, self.core)
        self.arrived(piece, send_z.at[kind, k], recv_z.at[kind, k])
        self.start(self.to_chip, kind, k, 1)
        self.start(self.to_chip, kind, k, 2)
        self.start(self.to_core, kind, k, 0)

    def to_corner(self, kind, k):
        send_x, recv_x = self.sems[2:4]
        for j in (1, 2):
            piece = self.place(kind, flip(self.mp, k), flip(self.chip, j), self.core)
            self.arrived(piece, send_x.at[kind, k, j], recv_x.at[kind, k, j])
        self.start(self.to_chip, kind, k, 3)
        self.start(self.to_core, kind, k, 1)
        self.start(self.to_core, kind, k, 2)

    def last_core(self, kind, k):
        send_x, recv_x = self.sems[2:4]
        piece = self.place(kind, flip(self.mp, k), flip(self.chip, 3), self.core)
        self.arrived(piece, send_x.at[kind, k, 3], recv_x.at[kind, k, 3])
        self.start(self.to_core, kind, k, 3)

    def settled(self, kind, k):
        send_c, recv_c = self.sems[4:]
        for j in range(4):
            piece = self.place(kind, flip(self.mp, k), flip(self.chip, j), 1 - self.core)
            self.arrived(piece, send_c.at[kind, k, j], recv_c.at[kind, k, j])

    def schedule(self, jobs, window=8, start=3.0, pace=3.0, lags=(6.0, 12.0, 14.0)):
        for job in jobs[:window]:
            self.start(self.along_mp, *job)

        def first(i):
            self.to_chips(*jobs[i])
            if i + window < len(jobs):
                self.start(self.along_mp, *jobs[i + window])

        steps = []
        clock = start
        for i, job in enumerate(jobs):
            clock += 0.37 * pace if job[0] == 1 else pace
            steps.append((clock, functools.partial(first, i), job, False))
            later = (self.to_corner, self.last_core, self.settled)
            for lag, step in zip(lags, later):
                steps.append((clock + lag, functools.partial(step, *job), job, step == later[-1]))
        return sorted(steps, key=lambda step: step[0])

    def finish(self):
        for make, which in self.sends:
            make(*which).wait_send()


def announce(devices):
    semaphore = pltpu.get_barrier_semaphore()
    for device in devices:
        pl.semaphore_signal(semaphore, inc=1, device_id=device, device_id_type=MESH)
    return semaphore


def row_keep(count, first, rows):
    return lax.broadcasted_iota(jnp.int32, (rows, 1), 0) + first < count


def project(weights_ref, normed_ref, out_ref, shard):
    parts, features, depth = weights_ref.shape[1:]
    rows = normed_ref.shape[0]
    block = 1024

    def step(i, _):
        at = pl.ds(aligned(i * block, block), block)
        weights = weights_ref[shard].reshape(parts * features, depth)
        out_ref[shard, :, at] = dot(weights, normed_ref[at, :], 1, 1).astype(bf16)
        return 0

    lax.fori_loop(0, rows // block, step, 0)


def attend(qkv_ref, shard, head, count, probs_ref, context_ref, scale_ref, scores, keys, local_heads, pause):
    rows = qkv_ref.shape[2]
    width = local_heads * HEAD
    block, chunk, group = 256, 128, 128
    at = pl.ds(aligned(head * HEAD, HEAD), HEAD)
    number = shard * local_heads + head
    context_at = pl.ds(aligned(number * HEAD, HEAD), HEAD)
    masked = jnp.where(row_keep(count, 0, rows), 0.0, MASKED)
    first_lane = lax.broadcasted_iota(jnp.int32, (rows, HEAD), 1) == 0
    keys[:, :HEAD] = qkv_ref[shard, pl.ds(aligned(width + head * HEAD, HEAD), HEAD), :].T
    keys[:, HEAD:] = jnp.where(first_lane, masked, 0.0).astype(bf16)
    queries = jnp.concatenate([qkv_ref[shard, at, :], jnp.ones((HEAD, rows), bf16)], axis=0)
    values = qkv_ref[shard, pl.ds(aligned(2 * width + head * HEAD, HEAD), HEAD), :]
    values = jnp.concatenate([values, jnp.ones((16, rows), bf16)], axis=0)
    blocks = rows // block
    highest = None
    for i in range(blocks + 1):
        ahead = None
        for first in range(0, rows, chunk):
            part = slice(first, first + chunk)
            if i < blocks:
                product = dot(keys[part, :], queries[:, i * block : (i + 1) * block], 1, 0)
                scores[i % 2, part, :] = product
                top = jnp.max(product.reshape(chunk // group, group, block), axis=0)
                ahead = top if ahead is None else jnp.maximum(ahead, top)
            if i > 0:
                weights = jnp.exp(scores[(i - 1) % 2, part, :] - highest)
                probs_ref[part, (i - 1) * block : i * block] = weights.astype(bf16)
        if i > 0:
            columns = slice((i - 1) * block, i * block)
            context = dot(values, probs_ref[:, columns], 1, 0)
            scale = 1.0 / context[HEAD : HEAD + 1]
            context_ref[context_at, columns] = (context[:HEAD] * scale).astype(bf16)
            scale_ref[number, :, columns] = scale
        if i < blocks:
            highest = jnp.max(ahead, axis=0, keepdims=True)
            pause(i)


def gelu_parts(gate):
    root = 0.7978845608028654
    square = gate * gate
    bend = jnp.tanh(gate * (root + (root * 0.044715) * square))
    half = 0.5 + 0.5 * bend
    slope = half + (0.5 * gate) * (1.0 - bend * bend) * (root + (3 * root * 0.044715) * square)
    return gate * half, slope


def attend_back(qkv_ref, grad_ref, shard, head, probs, context_back, delta, score_back, local_heads):
    rows = qkv_ref.shape[2]
    width = local_heads * HEAD
    block = 256
    head_at = pl.ds(aligned(head * HEAD, HEAD), HEAD)
    key_at = pl.ds(aligned(width + head * HEAD, HEAD), HEAD)
    value_at = pl.ds(aligned(2 * width + head * HEAD, HEAD), HEAD)
    number = shard * local_heads + head
    upstream = context_back[pl.ds(aligned(number * HEAD, HEAD), HEAD), :]
    queries, keys = qkv_ref[shard, head_at, :], qkv_ref[shard, key_at, :]
    high = delta[number].astype(bf16)
    low = (delta[number] - high.astype(f32)).astype(bf16)
    right = jnp.concatenate([upstream, high, low, jnp.zeros((14, rows), bf16)], axis=0)
    lane = lax.broadcasted_iota(jnp.int32, (rows, 16), 1)
    minus = jnp.where(lane < 2, -1.0, 0.0).astype(bf16)
    left = jnp.concatenate([qkv_ref[shard, value_at, :].T, minus], axis=1)
    for first in range(0, rows, block):
        part = slice(first, first + block)
        for i in range(0, rows, block):
            columns = slice(i, i + block)
            change = dot(left[part], right[:, columns], 1, 0)
            score_back[part, columns] = (probs[part, columns].astype(f32) * change).astype(bf16)
        grad_ref[shard, value_at, part] = dot(upstream, probs[part, :], 1, 1).astype(bf16)
        grad_ref[shard, key_at, part] = dot(queries, score_back[part, :], 1, 1).astype(bf16)
    grad_ref[shard, head_at, :] = dot(keys, score_back[...], 1, 0).astype(bf16)


class Reduce:
    def __init__(self, local, from_core, from_chips, total, sems):
        self.local, self.from_core = local, from_core
        self.from_chips, self.total, self.sems = from_chips, total, sems
        self.dp, self.mp = lax.axis_index("dp"), lax.axis_index("mp")
        self.core, self.chip = self.dp % 2, (self.dp // 2) % 4

    def copy(self, j):
        if j == 0:
            source, target, peer = self.local.at[:, 1 - self.core], self.from_core, flip(self.dp, 1)
        else:
            source, target = self.local.at[flip(self.chip, j), self.core], self.from_chips.at[j - 1]
            peer = flip(self.dp, 2 * j)
        return pltpu.make_async_remote_copy(
            src_ref=source,
            dst_ref=target,
            send_sem=self.sems.at[0, j],
            recv_sem=self.sems.at[1, j],
            device_id=(peer, self.mp),
            device_id_type=MESH,
        )

    def begin(self):
        self.copy(0).start()

    def middle(self):
        self.copy(0).wait()
        for j in (1, 2, 3, 0):
            chip = flip(self.chip, j)
            part = self.local[chip, self.core].astype(f32) + self.from_core[chip].astype(f32)
            if j == 0:
                self.total[...] = part
            else:
                self.local[chip, self.core] = part.astype(bf16)
                self.copy(j).start()

    def end(self):
        for j in (1, 2, 3):
            self.copy(j).wait()
        first, second, third = (self.from_chips[i].astype(f32) for i in range(3))
        self.total[...] += first + second + third


def main_kernel(
    extent,
    inputs,
    first_gain,
    second_gain,
    upstream,
    query_source,
    key_source,
    value_source,
    output_source,
    gate_source,
    up_source,
    down_source,
    layer_output,
    probs_out,
    grads_out,
    weights_out,
    hidden_out,
    wide_total,
    narrow_total,
    gains_total,
    attention_weights,
    output_weights,
    gate_weights,
    up_weights,
    down_weights,
    qkv,
    context,
    normed_one,
    normed_two,
    out_low,
    hidden,
    scale,
    delta,
    context_back,
    wide_grad,
    narrow_grad,
    wide_core,
    wide_chips,
    narrow_core,
    narrow_chips,
    gains_own,
    gains_in,
    own_weights,
    local_sem,
    probs_sem,
    out_sem,
    grads_sem,
    wide_sem,
    narrow_sem,
    gains_sem,
    send_z,
    recv_z,
    send_x,
    recv_x,
    send_c,
    recv_c,
):
    dp, mp = lax.axis_index("dp"), lax.axis_index("mp")
    shards = attention_weights.shape[0]
    rows, depth = inputs.shape
    features = output_weights.shape[1]
    units = gate_weights.shape[2]
    local_heads = features // HEAD
    heads = shards * local_heads
    count = extent[0, 0] * extent[0, 1]
    block = 256
    blocks = rows // block

    def each_block(step):
        def run(i, _):
            step(i * block, pl.ds(aligned(i * block, block), block))
            return 0

        lax.fori_loop(0, blocks, run, 0)

    sources = (None, output_source, gate_source, up_source, down_source)
    places = (attention_weights, output_weights, gate_weights, up_weights, down_weights)
    owned = [
        pltpu.make_async_copy(source, place.at[mp], local_sem.at[i])
        for i, (source, place) in enumerate(zip(sources[1:], places[1:]))
    ]
    owned.append(pltpu.make_async_copy(upstream, out_low, local_sem.at[4]))
    turned = [
        pltpu.make_async_copy(source, attention_weights.at[mp, i], local_sem.at[5 + i])
        for i, source in enumerate((query_source, key_source, value_source))
    ]
    peers = [(flip(dp, j), mp) for j in range(1, GROUP)]
    peers += [(dp, flip(mp, k)) for k in range(1, shards)]
    semaphore = announce(peers)
    for copy in turned + owned:
        copy.start()
    for copy in turned:
        copy.wait()
    own_weights[...] = attention_weights[mp].reshape(3 * features, depth).T
    pl.semaphore_wait(semaphore, len(peers))
    gather = Gather(sources, places, send_z, recv_z, send_x, recv_x, send_c, recv_c)
    jobs = [(kind, k) for kind in (0, 1) for k in range(1, shards)]
    jobs += [(kind, k) for k in range(1, shards) for kind in (2, 3, 4)]
    steps = gather.schedule(jobs)
    position = [0]
    clock = [0.0]

    def take(stop):
        chosen = steps[position[0] : stop]
        position[0] = max(position[0], stop)
        return chosen

    def due(spent):
        clock[0] += spent
        return take(sum(step[0] <= clock[0] for step in steps))

    def needed(job):
        where = [i for i, step in enumerate(steps) if step[3] and step[2] == job][0]
        clock[0] = max(clock[0], steps[where][0])
        return take(where + 1)

    def carry_out(chosen):
        for step in chosen:
            step[1]()

    def carry_out_at(index, plan):
        for number, chosen in plan.items():
            if chosen:
                pl.when(index == number)(functools.partial(carry_out, chosen))

    def gain_of(ref):
        return ref[...].astype(f32).reshape(1, depth)

    def normalise(first, at):
        values = inputs[at, :].astype(f32)
        root = lax.rsqrt(jnp.mean(values * values, axis=-1, keepdims=True) + EPSILON)
        normed_one[at, :] = (values * root * gain_of(first_gain)).astype(bf16)

    each_block(normalise)
    carry_out(due(1.5))

    def join(first, at):
        every_output = output_weights[...].reshape(depth, depth)
        values = inputs[at, :].astype(f32) + dot(context[:, at], every_output, 0, 0)
        hidden[at, :] = values
        root = lax.rsqrt(jnp.mean(values * values, axis=-1, keepdims=True) + EPSILON)
        normed_two[at, :] = (values * root * gain_of(second_gain)).astype(bf16)
        out_low[at, :] = jnp.where(row_keep(count, first, block), out_low[at, :], jnp.zeros((), bf16))

    def attention(probs, scores, keys):
        def probs_copy(slot, number):
            return pltpu.make_async_copy(probs.at[slot], probs_out.at[number], probs_sem.at[slot])

        shard_plan, project_plan, block_plans = {}, {}, [{} for _ in range(blocks)]
        for i in range(heads):
            if i % local_heads == 0:
                shard_plan[i] = needed((0, i // local_heads)) if i > 0 else []
                project_plan[i] = due(1.8)
            for plan in block_plans:
                plan[i] = due(0.4)

        def step(i, _):
            shard, head = cross(mp, i // local_heads), i % local_heads
            number = shard * local_heads + head

            @pl.when(head == 0)
            def _():
                carry_out_at(i, shard_plan)
                project(attention_weights, normed_one, qkv, shard)
                carry_out_at(i, project_plan)

            @pl.when(i >= 2)
            def _():
                probs_copy(i % 2, number).wait()

            attend(
                qkv,
                shard,
                head,
                count,
                probs.at[i % 2],
                context,
                scale,
                scores,
                keys,
                local_heads,
                lambda at: carry_out_at(i, block_plans[at]),
            )
            probs_copy(i % 2, number).start()
            return 0

        lax.fori_loop(0, heads, step, 0)
        pltpu.make_async_copy(attention_weights, weights_out, out_sem.at[0]).start()
        owned[0].wait()
        owned[4].wait()
        for k in range(1, shards):
            carry_out(needed((1, k)))
        each_block(join)
        carry_out(due(2.4))
        for slot in range(2):
            probs_copy(slot, 0).wait()

    pl.run_scoped(
        attention,
        pltpu.VMEM((2, rows, rows), bf16),
        pltpu.VMEM((2, rows, block), f32),
        pltpu.VMEM((rows, 2 * HEAD), bf16),
    )

    slices = wide_grad.shape[:3]
    wide = Reduce(wide_grad, wide_core, wide_chips, wide_total, wide_sem)
    narrow = Reduce(narrow_grad, narrow_core, narrow_chips, narrow_total, narrow_sem)

    def feed_forward(forward_sum, back_sum, mixed_own, gate_own, up_own):
        def feed(shard, k):
            def step(first, at):
                normed, low = normed_two[at, :], out_low[at, :]
                gate = dot(normed, gate_weights[shard], 1, 0)
                up = dot(normed, up_weights[shard], 1, 0)
                mixed_back = dot(low, down_weights[shard], 1, 1)
                bent, slope = gelu_parts(gate)
                mixed = (bent * up).astype(bf16)
                gate_back = (mixed_back * up * slope).astype(bf16)
                up_back = (mixed_back * bent).astype(bf16)
                ahead = dot(mixed, down_weights[shard], 1, 0)
                back = dot(gate_back, gate_weights[shard], 1, 1)
                back = back + dot(up_back, up_weights[shard], 1, 1)
                if k == 0:
                    mixed_own[at, :] = mixed
                    gate_own[at, :] = gate_back
                    up_own[at, :] = up_back
                    forward_sum[at, :] = ahead
                    back_sum[at, :] = back
                else:
                    forward_sum[at, :] += ahead
                    back_sum[at, :] += back

            plan = {i: due(1.5) for i in range(blocks)}

            def run(i, _):
                step(i * block, pl.ds(aligned(i * block, block), block))
                carry_out_at(i, plan)
                return 0

            lax.fori_loop(0, blocks, run, 0)

        for k in range(shards):
            if k == 0:
                for copy in owned[1:4]:
                    copy.wait()
            else:
                for kind in (2, 3, 4):
                    carry_out(needed((kind, k)))
            if k == shards - 1:
                carry_out(take(len(steps)))
                wide.middle()
            feed(flip(mp, k), k)
            if k == 0:
                pairs = ((normed_two, gate_own), (normed_two, up_own), (out_low, mixed_own))
                for i, (left, right) in enumerate(pairs):
                    part = dot(left[...], right[...], 0, 0).astype(bf16)
                    wide_grad[:, :, :, i * units : (i + 1) * units] = part.reshape(*slices, units)
                    carry_out(due(0.9))
                wide.begin()

        def close(first, at):
            keep = row_keep(count, first, block)
            values, back = hidden[at, :], back_sum[at, :]
            out_back = out_low[at, :].astype(f32)
            out_low[at, :] = jnp.where(keep, values + forward_sum[at, :], 0.0).astype(bf16)
            root = lax.rsqrt(jnp.mean(values * values, axis=-1, keepdims=True) + EPSILON)
            scaled = gain_of(second_gain) * back
            mean = jnp.mean(scaled * values, axis=-1, keepdims=True)
            result = out_back + root * scaled - values * (root * root * root * mean)
            hidden[at, :] = result
            normed_two[at, :] = result.astype(bf16)

        each_block(close)

    pl.run_scoped(
        feed_forward,
        pltpu.VMEM((rows, depth), f32),
        pltpu.VMEM((rows, depth), f32),
        pltpu.VMEM((rows, units), bf16),
        pltpu.VMEM((rows, units), bf16),
        pltpu.VMEM((rows, units), bf16),
    )
    pltpu.make_async_copy(out_low, layer_output, out_sem.at[1]).start()
    pltpu.make_async_copy(hidden, hidden_out, out_sem.at[2]).start()
    hidden_low = normed_two

    def context_step(first, at):
        every_output = output_weights[...].reshape(depth, depth)
        back = dot(every_output, hidden_low[at, :], 1, 1).reshape(heads, HEAD, block)
        low = (back * scale[:, :, at]).astype(bf16)
        context_back[:, at] = low.reshape(depth, block)
        ahead = context[:, at].reshape(heads, HEAD, block).astype(f32)
        delta[:, :, at] = jnp.sum(low.astype(f32) * ahead, axis=1, keepdims=True)

    each_block(context_step)

    def gains_copy(k):
        return pltpu.make_async_remote_copy(
            src_ref=gains_own,
            dst_ref=gains_in.at[k - 1],
            send_sem=gains_sem.at[0, k],
            recv_sem=gains_sem.at[1, k],
            device_id=(dp, flip(mp, k)),
            device_id_type=MESH,
        )

    def gains():
        piece = gains_own.shape[0]
        at = pl.ds(aligned((dp % GROUP) * piece, 32), piece)
        second = gate_weights[mp, at, :].astype(f32) * wide_total[:, :units]
        second = second + up_weights[mp, at, :].astype(f32) * wide_total[:, units : 2 * units]
        first = own_weights[at, :].astype(f32) * narrow_total[:, : 3 * features]
        lane = lax.broadcasted_iota(jnp.int32, gains_own.shape, 1)
        first = jnp.sum(first, axis=1, keepdims=True)
        second = jnp.sum(second, axis=1, keepdims=True)
        gains_own[...] = jnp.where(lane == 0, first, jnp.where(lane == 1, second, 0.0))
        for k in range(1, shards):
            gains_copy(k).start()

    def attention_back(probs, score_back, grads):
        def fetch(i):
            number = cross(mp, i // local_heads) * local_heads + i % local_heads
            return pltpu.make_async_copy(probs_out.at[number], probs.at[i % 2], probs_sem.at[i % 2])

        def keep_grads(shard, k):
            return pltpu.make_async_copy(grads.at[shard], grads_out.at[shard], grads_sem.at[k])

        def step(i, _):
            k, head = i // local_heads, i % local_heads
            shard = cross(mp, k)
            fetch(i).wait()

            @pl.when(i + 1 < heads)
            def _():
                fetch(i + 1).start()

            attend_back(
                qkv,
                grads,
                shard,
                head,
                probs.at[i % 2],
                context_back,
                delta,
                score_back,
                local_heads,
            )

            @pl.when(head == local_heads - 1)
            def _():
                keep_grads(shard, k).start()

            @pl.when(i == local_heads - 1)
            def _():
                own = context[pl.ds(aligned(mp * features, HEAD), features), :]
                part = jnp.concatenate(
                    [dot(grads[mp], normed_one[...], 1, 0), dot(own, hidden_low[...], 1, 0)], axis=0
                )
                narrow_grad[...] = part.T.astype(bf16).reshape(narrow_grad.shape)
                narrow.begin()

            @pl.when(i == local_heads)
            def _():
                narrow.middle()

            @pl.when(i == heads - 5)
            def _():
                wide.end()

            @pl.when(i == heads - 3)
            def _():
                narrow.end()
                gains()

            return 0

        fetch(0).start()
        lax.fori_loop(0, heads, step, 0)
        for k in range(shards):
            keep_grads(flip(mp, k), k).wait()

    pl.run_scoped(
        attention_back,
        pltpu.VMEM((2, rows, rows), bf16),
        pltpu.VMEM((rows, rows), bf16),
        pltpu.VMEM((shards, 3 * features, rows), bf16),
    )
    for k in range(1, shards):
        gains_copy(k).wait()
    gains_total[...] = (gains_own[...] + gains_in[0]) + (gains_in[1] + gains_in[2])
    pltpu.make_async_copy(attention_weights, weights_out, out_sem.at[0]).wait()
    pltpu.make_async_copy(out_low, layer_output, out_sem.at[1]).wait()
    pltpu.make_async_copy(hidden, hidden_out, out_sem.at[2]).wait()
    gather.finish()


def close_kernel(
    grads,
    weights,
    hidden_back,
    inputs,
    first_gain,
    layer_in,
    wide_total,
    narrow_total,
    input_grad,
    layer_output,
    query_grad,
    key_grad,
    value_grad,
    output_grad,
    gate_grad,
    up_grad,
    down_grad,
):
    shards, narrow, block = grads.shape
    depth = inputs.shape[1]
    values = inputs[...].astype(f32)
    every_weight = weights[...].reshape(shards * narrow, depth)
    back = dot(grads[...].reshape(shards * narrow, block), every_weight, 0, 0)
    root = lax.rsqrt(jnp.mean(values * values, axis=-1, keepdims=True) + EPSILON)
    scaled = first_gain[...].astype(f32).reshape(1, depth) * back
    mean = jnp.mean(scaled * values, axis=-1, keepdims=True)
    result = hidden_back[...] + root * scaled
    input_grad[...] = result - values * (root * root * root * mean)
    layer_output[...] = layer_in[...]

    @pl.when(pl.program_id(0) == 0)
    def _():
        features, units = query_grad.shape[1], gate_grad.shape[1]
        query_grad[...] = narrow_total[:, :features]
        key_grad[...] = narrow_total[:, features : 2 * features]
        value_grad[...] = narrow_total[:, 2 * features : 3 * features]
        gate_grad[...] = wide_total[:, :units]
        up_grad[...] = wide_total[:, units : 2 * units]
        down_grad[...] = wide_total[:, 2 * units :]
        output_grad[...] = narrow_total[:, 3 * features :].T


def vmem():
    return pl.BlockSpec(memory_space=pltpu.VMEM)


def anywhere():
    return pl.BlockSpec(memory_space=pl.ANY)


def body(groups, shards, *arguments):
    (
        patches,
        attention_gain,
        query_weight,
        key_weight,
        value_weight,
        output_weight,
        feedforward_gain,
        gate_weight,
        up_weight,
        down_weight,
        cotangent,
        grid_extent,
    ) = arguments
    rows, depth = patches.shape
    features, units = query_weight.shape[1], gate_weight.shape[1]
    heads = shards * features // HEAD
    piece = depth // GROUP
    wide, narrow = 3 * units, 3 * features
    mixed = narrow + features

    shape = jax.ShapeDtypeStruct
    kinds = Gather.KINDS
    dma = pltpu.SemaphoreType.DMA
    (
        layer_output,
        _,
        grads,
        weights,
        hidden_back,
        wide_total,
        narrow_total,
        gains_total,
    ) = pl.pallas_call(
        main_kernel,
        name="layer",
        out_shape=(
            shape((rows, depth), bf16),
            shape((heads, rows, rows), bf16),
            shape((shards, narrow, rows), bf16),
            shape((shards, 3, features, depth), bf16),
            shape((rows, depth), f32),
            shape((piece, wide), f32),
            shape((piece, mixed), f32),
            shape((piece, 128), f32),
        ),
        in_specs=[pl.BlockSpec(memory_space=pltpu.SMEM)] + [vmem()] * 3 + [anywhere()] * 8,
        out_specs=(anywhere(),) * 5 + (vmem(),) * 3,
        scratch_shapes=[
            pltpu.VMEM((shards, 3, features, depth), bf16),
            pltpu.VMEM((shards, features, depth), bf16),
            pltpu.VMEM((shards, depth, units), bf16),
            pltpu.VMEM((shards, depth, units), bf16),
            pltpu.VMEM((shards, units, depth), bf16),
            pltpu.VMEM((shards, narrow, rows), bf16),
            pltpu.VMEM((depth, rows), bf16),
            pltpu.VMEM((rows, depth), bf16),
            pltpu.VMEM((rows, depth), bf16),
            pltpu.VMEM((rows, depth), bf16),
            pltpu.VMEM((rows, depth), f32),
            pltpu.VMEM((heads, 1, rows), f32),
            pltpu.VMEM((heads, 1, rows), f32),
            pltpu.VMEM((depth, rows), bf16),
            pltpu.VMEM((4, 2, piece, wide), bf16),
            pltpu.VMEM((4, 2, piece, mixed), bf16),
            pltpu.VMEM((4, piece, wide), bf16),
            pltpu.VMEM((3, piece, wide), bf16),
            pltpu.VMEM((4, piece, mixed), bf16),
            pltpu.VMEM((3, piece, mixed), bf16),
            pltpu.VMEM((piece, 128), f32),
            pltpu.VMEM((3, piece, 128), f32),
            pltpu.VMEM((depth, narrow), bf16),
            dma((8,)),
            dma((2,)),
            dma((3,)),
            dma((shards,)),
            dma((2, 4)),
            dma((2, 4)),
            dma((2, shards)),
            dma((kinds, shards)),
            dma((kinds, shards)),
            dma((kinds, shards, 4)),
            dma((kinds, shards, 4)),
            dma((kinds, shards, 4)),
            dma((kinds, shards, 4)),
        ],
        compiler_params=pltpu.CompilerParams(
            collective_id=0, has_side_effects=True, vmem_limit_bytes=VMEM_LIMIT
        ),
    )(
        grid_extent,
        patches,
        attention_gain,
        feedforward_gain,
        cotangent,
        query_weight.T,
        key_weight.T,
        value_weight.T,
        output_weight,
        gate_weight,
        up_weight,
        down_weight,
    )

    block = 256

    def whole(*dims):
        return pl.BlockSpec(dims, lambda i: (0,) * len(dims))

    by_rows = pl.BlockSpec((block, depth), lambda i: (i, 0))
    small = [(piece, features)] * 3 + [(features, piece)] + [(piece, units)] * 3
    input_grad, layer_output, *small_grads = pl.pallas_call(
        close_kernel,
        name="close",
        grid=(rows // block,),
        out_shape=[shape((rows, depth), f32), shape((rows, depth), bf16)]
        + [shape(dims, f32) for dims in small],
        in_specs=[
            pl.BlockSpec((shards, narrow, block), lambda i: (0, 0, i)),
            whole(shards, 3, features, depth),
            by_rows,
            by_rows,
            whole(depth),
            by_rows,
            whole(piece, wide),
            whole(piece, mixed),
        ],
        out_specs=[by_rows, by_rows] + [whole(*dims) for dims in small],
        compiler_params=pltpu.CompilerParams(vmem_limit_bytes=VMEM_LIMIT),
    )(grads, weights, hidden_back, patches, attention_gain, layer_output, wide_total, narrow_total)

    index = lax.axis_index("dp")
    gains_total = gains_total[:, :2]
    if groups > 1:

        def spread(block, turned=False):
            block = block.T if turned else block
            whole = jnp.zeros((depth, block.shape[1]), f32)
            whole = lax.dynamic_update_slice(whole, block, ((index % GROUP) * piece, 0))
            own = lax.psum_scatter(whole, "dp", scatter_dimension=0, tiled=True)
            return own.T if turned else own

        small_grads = [spread(grad, i == 3) for i, grad in enumerate(small_grads)]
        gains_total = spread(gains_total)
    kept = depth // (groups * GROUP)

    def gain_grad(column, gain):
        own = lax.dynamic_slice_in_dim(gain.astype(f32), index * kept, kept)
        return gains_total[:, column] / own

    query_grad, key_grad, value_grad, output_grad, gate_grad, up_grad, down_grad = small_grads
    return (
        layer_output,
        input_grad,
        gain_grad(0, attention_gain),
        query_grad,
        key_grad,
        value_grad,
        output_grad,
        gain_grad(1, feedforward_gain),
        gate_grad,
        up_grad,
        down_grad.T,
    )


def solution(mesh):
    placed = (
        P("dp", None),
        P(),
        P(None, "mp"),
        P(None, "mp"),
        P(None, "mp"),
        P("mp", None),
        P(),
        P(None, "mp"),
        P(None, "mp"),
        P("mp", None),
        P("dp", None),
        P("dp", None),
    )
    return jax.shard_map(
        functools.partial(body, mesh.shape["dp"] // GROUP, mesh.shape["mp"]),
        mesh=mesh,
        in_specs=placed,
        out_specs=(
            P("dp", None),
            P("dp", None),
            P("dp"),
            P("dp", "mp"),
            P("dp", "mp"),
            P("dp", "mp"),
            P("mp", "dp"),
            P("dp"),
            P("dp", "mp"),
            P("dp", "mp"),
            P("mp", "dp"),
        ),
        check_vma=False,
    )
```
